256 devices in a mesh: heads: 4 (over x), pages: 64 (over z, y, core).
Axes of the slice: x: 4, y: 4, z: 8, core: 2. Of those that a mesh axis runs over, the one named last changes fastest.
Arguments:
- queries: bfloat16 [4608, 16, 128], P('pages', 'heads'), may hold values from -60 to 60
- keys: bfloat16 [4608, 16, 128], P('pages', 'heads'), may hold values from -6 to 6
- values: bfloat16 [4608, 16, 128], P('pages', 'heads'), may hold values from -6 to 6
- key_cache: bfloat16 [768, 128, 16, 128], P('pages', None, 'heads'), may hold values from -6 to 6
- value_cache: bfloat16 [768, 128, 16, 128], P('pages', None, 'heads'), may hold values from -6 to 6
- cache_len: int32 [6], replicated, may hold values from 0 to 15616, as said below
- page_table: int32 [6, 122], replicated, may hold values from 0 to 767, as said below
- append_slots: int32 [6, 6], replicated, may hold values from 0 to 767
- out_weight: bfloat16 [2048, 4096], P('heads', 'pages'), may hold values from -0.125 to 0.125
- out_bias: float32 [4096], P('heads'), may hold values from -3 to 3
Outputs:
- hidden: bfloat16 [4608, 4096], P('pages', 'heads')
- key_cache_out: bfloat16 [768, 128, 16, 128], P('pages', None, 'heads')
- value_cache_out: bfloat16 [768, 128, 16, 128], P('pages', None, 'heads')
The draws below stay inside these ranges and needn't reach their ends.
Inputs may be any that keep to these rules, and one draw needn't show every extreme that they name: Every entry of page_table and append_slots together is a different slot. `cache_len`: A multiple of 128; some request has exactly 15616.
All inputs are finite; a program needn't handle non-finite values.
Results may differ from the reference program's by a relative error of at most 0.018.
Values may be sent and summed in bfloat16 or wider, within the bound.
A program may use at most 128 MiB of HBM per device.

```python
import math
import jax
import jax.numpy as jnp
from jax import lax

D = 4096
HEADS = 16
HD = 128
ROT = 32
PAGE = 128
REQS = 6
SPAN = 768
TOKENS = 4608
NEWP = 6
SLOTS = 768
MAXP = 122


def shared_order(key):
    return jax.random.permutation(jax.random.fold_in(key, 7), SLOTS)


def draw_page_table(key, part):
    slot_order = shared_order(key)
    return slot_order[:REQS * MAXP].reshape(REQS, MAXP).astype(jnp.int32)


def draw_append_slots(key, part):
    slot_order = shared_order(key)
    return slot_order[REQS * MAXP:REQS * (MAXP + NEWP)].reshape(REQS, NEWP).astype(jnp.int32)


def draw_cache_len(key, part):
    page_count = jax.random.randint(jax.random.fold_in(key, 1), (REQS,), 0, MAXP + 1)
    longest = jax.random.randint(jax.random.fold_in(key, 2), (), 0, REQS)
    page_count = jnp.where(jnp.arange(REQS) == longest, MAXP, page_count)
    return (page_count * PAGE).astype(jnp.int32)


def draw_queries(key, part):
    scaled = jax.random.normal(jax.random.fold_in(key, 3), (TOKENS, HEADS, HD), jnp.float32) * 2.5
    return jnp.clip(scaled, -60.0, 60.0).astype(jnp.bfloat16)


def level_of(stream_key, shape, split, smallest, top_value):
    def one(axis_at, shards_of):
        draws = jax.random.uniform(jax.random.fold_in(jax.random.fold_in(stream_key, 6), axis_at), (shards_of,), jnp.float32, smallest / len(split), top_value / len(split))
        return jnp.repeat(jnp.exp(draws), shape[axis_at] // shards_of).reshape((-1,) + (1,) * (len(shape) - axis_at - 1))

    factor_of = one(*split[0])
    for cut in split[1:]:
        factor_of = factor_of * one(*cut)
    return factor_of


def bell_draw(own_key, dims, scale, limit, cuts=(), kind=jnp.bfloat16):
    loudness = level_of(own_key, dims, cuts, -0.22, 0.18) if cuts else 1.0
    drawn = jax.random.normal(own_key, dims, jnp.float32) * scale * loudness
    return jnp.minimum(jnp.maximum(drawn, -limit), limit).astype(kind)


def setup_inputs(seed: int = 0) -> dict:
    seeds = jax.random.split(jax.random.key(seed), 11)
    queries = draw_queries(jax.random.fold_in(seeds[10], 71), 0)
    keys = bell_draw(seeds[1], (TOKENS, HEADS, HD), 1.0, 6.0, ((0, 64), (1, 4)))
    values = bell_draw(seeds[2], (TOKENS, HEADS, HD), 1.0, 6.0, ((0, 64), (1, 4)))
    key_cache = bell_draw(seeds[3], (SLOTS, PAGE, HEADS, HD), 1.0, 6.0, ((0, 64), (2, 4)))
    value_cache = bell_draw(seeds[4], (SLOTS, PAGE, HEADS, HD), 1.0, 6.0, ((0, 64), (2, 4)))
    cache_len = draw_cache_len(jax.random.fold_in(seeds[10], 71), 0)
    page_table = draw_page_table(jax.random.fold_in(seeds[10], 71), 0)
    append_slots = draw_append_slots(jax.random.fold_in(seeds[10], 71), 0)
    out_weight = bell_draw(seeds[8], (HEADS * HD, D), (HEADS * HD) ** -0.5, 0.125, ((0, 4), (1, 64)))
    out_bias = bell_draw(seeds[9], (D,), 0.5, 3.0, ((0, 4),), jnp.float32)
    return dict(queries=queries, keys=keys, values=values, key_cache=key_cache, value_cache=value_cache, cache_len=cache_len, page_table=page_table, append_slots=append_slots, out_weight=out_weight, out_bias=out_bias)


low_score = -1e+30

def rotate(vectors, positions):
    half_rot = ROT // 2
    inv_freq = 10000.0 ** (-2.0 * jnp.arange(half_rot, dtype=jnp.float32) / ROT)
    angles = positions[:, None] * inv_freq[None, :]
    cosine = jnp.cos(angles)[:, None, :]
    sine = jnp.sin(angles)[:, None, :]
    first_half = vectors[..., :half_rot]
    second_half = vectors[..., half_rot:ROT]
    return jnp.concatenate([first_half * cosine - second_half * sine, second_half * cosine + first_half * sine, vectors[..., ROT:]], axis=-1)

def reference(queries, keys, values, key_cache, value_cache, cache_len, page_table, append_slots, out_weight, out_bias):
    token_ids = jnp.arange(TOKENS, dtype=jnp.int32)
    request_ids = token_ids // SPAN
    starts = jnp.take(cache_len, request_ids)
    positions = (starts + token_ids % SPAN).astype(jnp.float32)
    rotated_q = rotate(queries.astype(jnp.float32), positions).astype(jnp.bfloat16)
    rotated_k = rotate(keys.astype(jnp.float32), positions).astype(jnp.bfloat16)
    fresh_slots = append_slots.reshape(-1)
    key_out = key_cache.at[fresh_slots].set(rotated_k.reshape(REQS * NEWP, PAGE, HEADS, HD))
    value_out = value_cache.at[fresh_slots].set(values.reshape(REQS * NEWP, PAGE, HEADS, HD))
    score_scale = 1.0 / math.sqrt(HD)
    offsets = jnp.arange(PAGE * (MAXP + NEWP), dtype=jnp.int32)
    query_offsets = jnp.arange(SPAN, dtype=jnp.int32)

    def one_request(request):
        length = cache_len[request]
        slot_list = jnp.concatenate([page_table[request], append_slots[request]]).astype(jnp.int32)
        req_keys = jnp.take(key_out, slot_list, axis=0).reshape(-1, HEADS, HD).astype(jnp.float32)
        req_values = jnp.take(value_out, slot_list, axis=0).reshape(-1, HEADS, HD).astype(jnp.float32)
        query_pos = length + query_offsets
        cached_part = offsets < PAGE * MAXP
        key_pos = jnp.where(cached_part, offsets, length + offsets - PAGE * MAXP)
        allowed = jnp.where(cached_part[None, :], (key_pos < length)[None, :], key_pos[None, :] <= query_pos[:, None])
        block = lax.dynamic_slice_in_dim(rotated_q, (request * SPAN).astype(jnp.int32), SPAN, 0).astype(jnp.float32)

        def one_head(head):
            head_q = lax.dynamic_index_in_dim(block, head, 1, keepdims=False)
            head_k = lax.dynamic_index_in_dim(req_keys, head, 1, keepdims=False)
            head_v = lax.dynamic_index_in_dim(req_values, head, 1, keepdims=False)
            scores = jnp.dot(head_q, head_k.T, precision=lax.Precision.HIGHEST) * score_scale
            scores = jnp.where(allowed, scores, low_score)
            peak = lax.optimization_barrier(jnp.max(scores, axis=1, keepdims=True))
            weights = jnp.where(allowed, jnp.exp(scores - peak), 0.0)
            totals = lax.optimization_barrier(jnp.sum(weights, axis=1, keepdims=True))
            rounded = lax.optimization_barrier(weights.astype(jnp.bfloat16))
            weighted = jnp.dot(rounded.astype(jnp.float32), head_v, precision=lax.Precision.HIGHEST)
            return (weighted / totals).astype(jnp.bfloat16)
        return lax.map(one_head, jnp.arange(HEADS, dtype=jnp.int32))
    attended = lax.map(one_request, jnp.arange(REQS, dtype=jnp.int32))
    attended = jnp.transpose(attended, (0, 2, 1, 3)).reshape(TOKENS, HEADS * HD)
    hidden = (jnp.dot(attended, out_weight, preferred_element_type=jnp.float32) + out_bias[None, :]).astype(jnp.bfloat16)
    return (hidden, key_out, value_out)
```

```python
import functools
import math

import jax
import jax.numpy as jnp
from jax import lax
from jax.experimental import pallas as pl
from jax.experimental.pallas import tpu as pltpu
from jax.sharding import PartitionSpec as P

ROT = 32
PAGE = 128


low_score = -1e30


def rotate(vectors, positions):
    half_rot = ROT // 2
    inv_freq = 10000.0 ** (-2.0 * jnp.arange(half_rot, dtype=jnp.float32) / ROT)
    angles = positions[:, None] * inv_freq[None, :]
    cosine = jnp.cos(angles)[:, None, :]
    sine = jnp.sin(angles)[:, None, :]
    first_half = vectors[..., :half_rot]
    second_half = vectors[..., half_rot:ROT]
    return jnp.concatenate(
        [
            first_half * cosine - second_half * sine,
            second_half * cosine + first_half * sine,
            vectors[..., ROT:],
        ],
        axis=-1,
    )


def attend_kernel(heads, head_dim, sreq_ref, skind_ref, slim_ref, q_ref, k_ref, v_ref, o_ref, ml_ref):
    step = pl.program_id(0)
    span = q_ref.shape[1]
    lanes = ml_ref.shape[2]

    @pl.when(step == 0)
    def _init():
        o_ref[...] = jnp.zeros_like(o_ref)
        lane = lax.broadcasted_iota(jnp.int32, ml_ref.shape, 2)
        ml_ref[...] = jnp.where(lane < heads, low_score, 0.0).astype(jnp.float32)

    request = sreq_ref[step]
    kind = skind_ref[step]
    limit = slim_ref[step]
    scale = 1.0 / math.sqrt(head_dim)

    @pl.when(kind != 0)
    def _work():
        rows = lax.broadcasted_iota(jnp.int32, (span, PAGE), 0)
        cols = lax.broadcasted_iota(jnp.int32, (span, PAGE), 1)
        allowed = rows - cols >= limit
        lane = lax.broadcasted_iota(jnp.int32, (span, lanes), 1)
        ml = ml_ref[request]
        for h in range(heads):
            cut = slice(h * head_dim, (h + 1) * head_dim)
            q_h = q_ref[request, :, cut]
            k_h = k_ref[0, :, cut]
            v_h = v_ref[0, :, cut]
            scores = lax.dot_general(
                q_h, k_h, (((1,), (1,)), ((), ())), preferred_element_type=jnp.float32
            ) * scale
            scores = jnp.where(allowed, scores, low_score)
            m_prev = ml[:, h : h + 1]
            l_prev = ml[:, heads + h : heads + h + 1]
            m_new = jnp.maximum(m_prev, jnp.max(scores, axis=1, keepdims=True))
            alpha = jnp.exp(m_prev - m_new)
            weights = jnp.where(allowed, jnp.exp(scores - m_new), 0.0)
            l_new = alpha * l_prev + jnp.sum(weights, axis=1, keepdims=True)
            contrib = jnp.dot(
                weights.astype(jnp.bfloat16), v_h, preferred_element_type=jnp.float32
            )
            o_ref[request, :, cut] = alpha * o_ref[request, :, cut] + contrib
            ml = jnp.where(lane == h, m_new, jnp.where(lane == heads + h, l_new, ml))
        ml_ref[request] = ml


def local_attention(slot_request, slot_kind, slot_limit, q_all, k_slots, v_slots, heads, head_dim):
    requests, span, width = q_all.shape
    slot_count = k_slots.shape[0]
    kernel = functools.partial(attend_kernel, heads, head_dim)
    flops = 4 * slot_count * span * PAGE * width
    return pl.pallas_call(
        kernel,
        out_shape=(
            jax.ShapeDtypeStruct((requests, span, width), jnp.float32),
            jax.ShapeDtypeStruct((requests, span, 128), jnp.float32),
        ),
        grid_spec=pltpu.PrefetchScalarGridSpec(
            num_scalar_prefetch=3,
            grid=(slot_count,),
            in_specs=[
                pl.BlockSpec((requests, span, width), lambda s, *_: (0, 0, 0)),
                pl.BlockSpec((1, PAGE, width), lambda s, *_: (s, 0, 0)),
                pl.BlockSpec((1, PAGE, width), lambda s, *_: (s, 0, 0)),
            ],
            out_specs=[
                pl.BlockSpec((requests, span, width), lambda s, *_: (0, 0, 0)),
                pl.BlockSpec((requests, span, 128), lambda s, *_: (0, 0, 0)),
            ],
        ),
        compiler_params=pltpu.CompilerParams(
            dimension_semantics=("arbitrary",), vmem_limit_bytes=60 * 1024 * 1024
        ),
        cost_estimate=pl.CostEstimate(
            flops=flops,
            transcendentals=slot_count * span * PAGE * heads,
            bytes_accessed=q_all.size * 2 + 2 * k_slots.size * 2 + requests * span * (width + 128) * 4,
        ),
    )(slot_request, slot_kind, slot_limit, q_all, k_slots, v_slots)


def per_device(
    queries,
    keys,
    values,
    key_cache,
    value_cache,
    cache_len,
    page_table,
    append_slots,
    out_weight,
    out_bias,
):
    tok_dev, head_count, head_dim = queries.shape
    width = head_count * head_dim
    requests = cache_len.shape[0]
    max_pages = page_table.shape[1]
    new_pages = append_slots.shape[1]
    span_len = new_pages * PAGE
    slot_count = key_cache.shape[0]
    page_devices = lax.axis_size("pages")
    device_at = lax.axis_index("pages")
    token_ids = device_at * tok_dev + jnp.arange(tok_dev, dtype=jnp.int32)
    request_ids = token_ids // span_len
    request_grid = jnp.arange(requests, dtype=jnp.int32)
    starts = jnp.sum(
        jnp.where(request_ids[:, None] == request_grid[None, :], cache_len[None, :], 0), axis=1
    )
    positions = (starts + token_ids % span_len).astype(jnp.float32)
    rotated_q = rotate(queries.astype(jnp.float32), positions).astype(jnp.bfloat16)
    rotated_k = rotate(keys.astype(jnp.float32), positions).astype(jnp.bfloat16)
    stacked = jnp.stack(
        [
            rotated_q.reshape(tok_dev, width),
            rotated_k.reshape(tok_dev, width),
            values.reshape(tok_dev, width),
        ]
    )
    gathered = lax.all_gather(stacked, "pages", axis=1, tiled=True)
    all_q = gathered[0].reshape(requests, span_len, width)
    page_shape = (requests * new_pages, PAGE, head_count, head_dim)
    all_k = gathered[1].reshape(page_shape)
    all_v = gathered[2].reshape(page_shape)
    my_slots = device_at * slot_count + jnp.arange(slot_count, dtype=jnp.int32)
    cached_hit = page_table.reshape(-1)[None, :] == my_slots[:, None]
    fresh_hit = append_slots.reshape(-1)[None, :] == my_slots[:, None]
    is_cached = jnp.any(cached_hit, axis=1)
    is_fresh = jnp.any(fresh_hit, axis=1)
    cached_index = jnp.sum(
        jnp.where(cached_hit, jnp.arange(requests * max_pages, dtype=jnp.int32)[None, :], 0), axis=1
    )
    fresh_index = jnp.sum(
        jnp.where(fresh_hit, jnp.arange(requests * new_pages, dtype=jnp.int32)[None, :], 0), axis=1
    )
    slot_request = jnp.where(is_fresh, fresh_index // new_pages, cached_index // max_pages)
    slot_page = jnp.where(is_fresh, fresh_index % new_pages, cached_index % max_pages)
    slot_length = jnp.sum(
        jnp.where(slot_request[:, None] == request_grid[None, :], cache_len[None, :], 0), axis=1
    )
    visible = is_fresh | (is_cached & (slot_page * PAGE < slot_length))
    slot_kind = visible.astype(jnp.int32)
    slot_limit = jnp.where(is_fresh, slot_page * PAGE, -4 * span_len)
    key_out = jnp.where(
        is_fresh[:, None, None, None],
        jnp.take(all_k, fresh_index, axis=0),
        key_cache,
    )
    value_out = jnp.where(
        is_fresh[:, None, None, None],
        jnp.take(all_v, fresh_index, axis=0),
        value_cache,
    )
    o_loc, ml = local_attention(
        slot_request,
        slot_kind,
        slot_limit,
        all_q,
        key_out.reshape(slot_count, PAGE, width),
        value_out.reshape(slot_count, PAGE, width),
        head_count,
        head_dim,
    )
    m_loc = ml[:, :, :head_count]
    l_loc = ml[:, :, head_count : 2 * head_count]
    m_all = lax.all_gather(m_loc.astype(jnp.bfloat16), "pages", axis=0, tiled=False)
    peak = jnp.max(m_all, axis=0).astype(jnp.float32)
    factor = jnp.exp(m_loc - peak)
    o_scaled = o_loc.reshape(requests, span_len, head_count, head_dim) * factor[..., None]
    l_scaled = l_loc * factor
    extra = 8
    l_rows = jnp.pad(
        l_scaled.reshape(page_devices, tok_dev * head_count),
        ((0, 0), (0, extra * width - tok_dev * head_count)),
    ).reshape(page_devices, extra, width)
    packed = jnp.concatenate(
        [o_scaled.reshape(page_devices, tok_dev, width), l_rows], axis=1
    ).reshape(page_devices * (tok_dev + extra), width)
    mine = lax.psum_scatter(packed, "pages", scatter_dimension=0, tiled=True)
    weighted = mine[:tok_dev].reshape(tok_dev, head_count, head_dim)
    totals = mine[tok_dev:].reshape(-1)[: tok_dev * head_count].reshape(tok_dev, head_count)
    attended = (weighted / totals[:, :, None]).reshape(tok_dev, width).astype(jnp.bfloat16)
    projected = jnp.dot(
        attended,
        lax.all_gather(out_weight, "pages", axis=1, tiled=True),
        preferred_element_type=jnp.float32,
    )
    summed = lax.psum_scatter(
        projected.astype(jnp.bfloat16), "heads", scatter_dimension=1, tiled=True
    ).astype(jnp.float32)
    hidden = (summed + out_bias[None, :]).astype(jnp.bfloat16)
    return (hidden, key_out, value_out)


def solution(mesh):
    placed = (
        P("pages", "heads", None),
        P("pages", "heads", None),
        P("pages", "heads", None),
        P("pages", None, "heads", None),
        P("pages", None, "heads", None),
        P(),
        P(),
        P(),
        P("heads", "pages"),
        P("heads"),
    )
    return jax.shard_map(
        per_device,
        mesh=mesh,
        in_specs=placed,
        out_specs=(
            P("pages", "heads"),
            P("pages", None, "heads", None),
            P("pages", None, "heads", None),
        ),
        check_vma=False,
    )
```

```python
import functools
import math

import jax
import jax.numpy as jnp
from jax import lax
from jax.experimental import pallas as pl
from jax.experimental.pallas import tpu as pltpu
from jax.sharding import PartitionSpec as P

ROT = 32
PAGE = 128


low_score = -1e30
mask_score = -(2.0 ** 100)


def rotate(vectors, positions):
    half_rot = ROT // 2
    inv_freq = 10000.0 ** (-2.0 * jnp.arange(half_rot, dtype=jnp.float32) / ROT)
    angles = positions[:, None] * inv_freq[None, :]
    cosine = jnp.cos(angles)[:, None, :]
    sine = jnp.sin(angles)[:, None, :]
    first_half = vectors[..., :half_rot]
    second_half = vectors[..., half_rot:ROT]
    return jnp.concatenate(
        [
            first_half * cosine - second_half * sine,
            second_half * cosine + first_half * sine,
            vectors[..., ROT:],
        ],
        axis=-1,
    )


def attend_kernel(
    heads, head_dim, requests, span,
    sreq_ref, skind_ref, slim_ref, sfresh_ref,
    q_ref, kf_ref, vf_ref, kc_ref, vc_ref,
    out_ref, acc_ref, ml_ref,
):
    step = pl.program_id(0)
    lanes = ml_ref.shape[1]
    width = heads * head_dim

    @pl.when(step == 0)
    def _init():
        acc_ref[...] = jnp.zeros_like(acc_ref)
        lane = lax.broadcasted_iota(jnp.int32, ml_ref.shape, 1)
        ml_ref[...] = jnp.where(lane < heads, mask_score, 0.0).astype(jnp.float32)

    request = sreq_ref[step]
    kind = skind_ref[step]
    limit = slim_ref[step]
    scale = 1.0 / math.sqrt(head_dim)

    def attend(k_ref, v_ref):
        base = pl.multiple_of(request * span, span)
        rows = lax.broadcasted_iota(jnp.int32, (span, PAGE), 0)
        cols = lax.broadcasted_iota(jnp.int32, (span, PAGE), 1)
        allowed = rows - cols >= limit
        lane = lax.broadcasted_iota(jnp.int32, (span, lanes), 1)
        ml = ml_ref[pl.ds(base, span), :]
        for h in range(heads):
            cut = slice(h * head_dim, (h + 1) * head_dim)
            q_h = q_ref[0, pl.ds(base, span), cut]
            k_h = k_ref[0, :, cut]
            v_h = v_ref[0, :, cut]
            scores = lax.dot_general(
                q_h, k_h, (((1,), (1,)), ((), ())), preferred_element_type=jnp.float32
            ) * scale
            scores = jnp.where(allowed, scores, mask_score)
            m_prev = ml[:, h : h + 1]
            l_prev = ml[:, heads + h : heads + h + 1]
            m_new = jnp.maximum(m_prev, jnp.max(scores, axis=1, keepdims=True))
            m_new = m_new.astype(jnp.bfloat16).astype(jnp.float32)
            alpha = jnp.exp(m_prev - m_new)
            weights = jnp.where(allowed, jnp.exp(scores - m_new), 0.0)
            l_new = alpha * l_prev + jnp.sum(weights, axis=1, keepdims=True)
            contrib = jnp.dot(
                weights.astype(jnp.bfloat16), v_h, preferred_element_type=jnp.float32
            )
            acc_ref[pl.ds(base, span), cut] = alpha * acc_ref[pl.ds(base, span), cut] + contrib
            ml = jnp.where(
                lane == h,
                m_new,
                jnp.where((lane == heads + h) | (lane == 2 * heads + h), l_new, ml),
            )
        ml_ref[pl.ds(base, span), :] = ml

    @pl.when(kind == 1)
    def _cached():
        attend(kc_ref, vc_ref)

    @pl.when(kind == 2)
    def _fresh():
        attend(kf_ref, vf_ref)

    @pl.when(step == pl.num_programs(0) - 1)
    def _emit():
        chunks, rows_per, _ = out_ref.shape
        lane = lax.broadcasted_iota(jnp.int32, (rows_per, lanes), 1)
        for d in range(chunks):
            rows = pl.ds(d * rows_per, rows_per)
            out_ref[d, :, :width] = acc_ref[rows, :].astype(jnp.bfloat16)
            ml = ml_ref[rows, :]
            rounded = ml.astype(jnp.bfloat16).astype(jnp.float32)
            packed = jnp.where(
                lane < 2 * heads,
                rounded,
                jnp.where(lane < 3 * heads, ml - rounded, 0.0),
            )
            out_ref[d, :, width:] = packed.astype(jnp.bfloat16)


def local_attention(slot_request, slot_kind, slot_limit, slot_fresh, gathered, kc, vc,
                    heads, head_dim, requests, span, chunks):
    _, tokens, width = gathered.shape
    slot_count = kc.shape[0]
    rows_per = tokens // chunks
    kernel = functools.partial(attend_kernel, heads, head_dim, requests, span)
    flops = 4 * slot_count * span * PAGE * width
    return pl.pallas_call(
        kernel,
        out_shape=jax.ShapeDtypeStruct((chunks, rows_per, width + 128), jnp.bfloat16),
        grid_spec=pltpu.PrefetchScalarGridSpec(
            num_scalar_prefetch=4,
            grid=(slot_count,),
            in_specs=[
                pl.BlockSpec((1, tokens, width), lambda s, *_: (0, 0, 0),
                             pipeline_mode=pl.Buffered(1)),
                pl.BlockSpec((1, PAGE, width), lambda s, rq, kd, lm, fr: (1, fr[s], 0)),
                pl.BlockSpec((1, PAGE, width), lambda s, rq, kd, lm, fr: (2, fr[s], 0)),
                pl.BlockSpec((1, PAGE, width), lambda s, *_: (s, 0, 0)),
                pl.BlockSpec((1, PAGE, width), lambda s, *_: (s, 0, 0)),
            ],
            out_specs=pl.BlockSpec((chunks, rows_per, width + 128), lambda s, *_: (0, 0, 0)),
            scratch_shapes=[
                pltpu.VMEM((tokens, width), jnp.float32),
                pltpu.VMEM((tokens, 128), jnp.float32),
            ],
        ),
        compiler_params=pltpu.CompilerParams(
            dimension_semantics=("arbitrary",), vmem_limit_bytes=60 * 1024 * 1024
        ),
        cost_estimate=pl.CostEstimate(
            flops=flops,
            transcendentals=slot_count * span * PAGE * heads,
            bytes_accessed=tokens * width * 2 + 4 * kc.size * 2 + tokens * (width + 128) * 2,
        ),
    )(slot_request, slot_kind, slot_limit, slot_fresh, gathered, gathered, gathered, kc, vc)


def per_device(
    queries,
    keys,
    values,
    key_cache,
    value_cache,
    cache_len,
    page_table,
    append_slots,
    out_weight,
    out_bias,
):
    tok_dev, head_count, head_dim = queries.shape
    width = head_count * head_dim
    requests = cache_len.shape[0]
    max_pages = page_table.shape[1]
    new_pages = append_slots.shape[1]
    span_len = new_pages * PAGE
    slot_count = key_cache.shape[0]
    page_devices = lax.axis_size("pages")
    device_at = lax.axis_index("pages")
    token_ids = device_at * tok_dev + jnp.arange(tok_dev, dtype=jnp.int32)
    request_ids = token_ids // span_len
    request_grid = jnp.arange(requests, dtype=jnp.int32)
    starts = jnp.sum(
        jnp.where(request_ids[:, None] == request_grid[None, :], cache_len[None, :], 0), axis=1
    )
    positions = (starts + token_ids % span_len).astype(jnp.float32)
    rotated_q = rotate(queries.astype(jnp.float32), positions).astype(jnp.bfloat16)
    rotated_k = rotate(keys.astype(jnp.float32), positions).astype(jnp.bfloat16)
    w_cols = out_weight.shape[1]
    w_plane = jnp.pad(out_weight.T, ((0, tok_dev - w_cols), (0, 0)))
    stacked = jnp.stack(
        [
            rotated_q.reshape(tok_dev, width),
            rotated_k.reshape(tok_dev, width),
            values.reshape(tok_dev, width),
            w_plane,
        ]
    )
    gathered = lax.all_gather(stacked, "pages", axis=1, tiled=True)
    my_slots = device_at * slot_count + jnp.arange(slot_count, dtype=jnp.int32)
    cached_hit = page_table.reshape(-1)[None, :] == my_slots[:, None]
    fresh_hit = append_slots.reshape(-1)[None, :] == my_slots[:, None]
    is_cached = jnp.any(cached_hit, axis=1)
    is_fresh = jnp.any(fresh_hit, axis=1)
    cached_index = jnp.sum(
        jnp.where(cached_hit, jnp.arange(requests * max_pages, dtype=jnp.int32)[None, :], 0), axis=1
    )
    fresh_index = jnp.sum(
        jnp.where(fresh_hit, jnp.arange(requests * new_pages, dtype=jnp.int32)[None, :], 0), axis=1
    )
    slot_request = jnp.where(is_fresh, fresh_index // new_pages, cached_index // max_pages)
    slot_page = jnp.where(is_fresh, fresh_index % new_pages, cached_index % max_pages)
    slot_length = jnp.sum(
        jnp.where(slot_request[:, None] == request_grid[None, :], cache_len[None, :], 0), axis=1
    )
    visible = is_cached & (slot_page * PAGE < slot_length)
    slot_kind = jnp.where(is_fresh, 2, jnp.where(visible, 1, 0)).astype(jnp.int32)
    slot_limit = jnp.where(is_fresh, slot_page * PAGE, -4 * span_len)
    page_pool = (requests * new_pages, PAGE, width)
    fresh_k = jnp.take(gathered[1].reshape(page_pool), fresh_index, axis=0)
    fresh_v = jnp.take(gathered[2].reshape(page_pool), fresh_index, axis=0)
    cache_shape = key_cache.shape
    key_out = jnp.where(is_fresh[:, None, None, None], fresh_k.reshape(cache_shape), key_cache)
    value_out = jnp.where(is_fresh[:, None, None, None], fresh_v.reshape(cache_shape), value_cache)
    packed = local_attention(
        slot_request,
        slot_kind,
        slot_limit,
        fresh_index,
        gathered,
        key_cache.reshape(slot_count, PAGE, width),
        value_cache.reshape(slot_count, PAGE, width),
        head_count,
        head_dim,
        requests,
        span_len,
        page_devices,
    )
    received = lax.all_to_all(packed, "pages", 0, 0, tiled=True).astype(jnp.float32)
    part_o = received[:, :, :width].reshape(page_devices, tok_dev, head_count, head_dim)
    part_m = received[:, :, width : width + head_count]
    part_l = (
        received[:, :, width + head_count : width + 2 * head_count]
        + received[:, :, width + 2 * head_count : width + 3 * head_count]
    )
    peak = jnp.max(part_m, axis=0)
    factor = jnp.exp(part_m - peak[None])
    weighted = jnp.sum(part_o * factor[..., None], axis=0)
    totals = jnp.sum(part_l * factor, axis=0)
    attended = (weighted / totals[:, :, None]).reshape(tok_dev, width).astype(jnp.bfloat16)
    projected = lax.dot_general(
        attended, gathered[3], (((1,), (1,)), ((), ())), preferred_element_type=jnp.float32
    )
    projected = projected.reshape(tok_dev, page_devices, tok_dev)[:, :, :w_cols].reshape(
        tok_dev, page_devices * w_cols
    )
    summed = lax.psum_scatter(
        projected.astype(jnp.bfloat16), "heads", scatter_dimension=1, tiled=True
    ).astype(jnp.float32)
    hidden = (summed + out_bias[None, :]).astype(jnp.bfloat16)
    return (hidden, key_out, value_out)


def solution(mesh):
    placed = (
        P("pages", "heads", None),
        P("pages", "heads", None),
        P("pages", "heads", None),
        P("pages", None, "heads", None),
        P("pages", None, "heads", None),
        P(),
        P(),
        P(),
        P("heads", "pages"),
        P("heads"),
    )
    return jax.shard_map(
        per_device,
        mesh=mesh,
        in_specs=placed,
        out_specs=(
            P("pages", "heads"),
            P("pages", None, "heads", None),
            P("pages", None, "heads", None),
        ),
        check_vma=False,
    )
```

```python
import functools
import math

import jax
import jax.numpy as jnp
from jax import lax
from jax.experimental import pallas as pl
from jax.experimental.pallas import tpu as pltpu
from jax.sharding import PartitionSpec as P

ROT = 32
PAGE = 128


low_score = -1e30
mask_score = -(2.0 ** 100)


def rotate(vectors, positions):
    half_rot = ROT // 2
    inv_freq = 10000.0 ** (-2.0 * jnp.arange(half_rot, dtype=jnp.float32) / ROT)
    angles = positions[:, None] * inv_freq[None, :]
    cosine = jnp.cos(angles)[:, None, :]
    sine = jnp.sin(angles)[:, None, :]
    first_half = vectors[..., :half_rot]
    second_half = vectors[..., half_rot:ROT]
    return jnp.concatenate(
        [
            first_half * cosine - second_half * sine,
            second_half * cosine + first_half * sine,
            vectors[..., ROT:],
        ],
        axis=-1,
    )


def attend_kernel(
    heads, head_dim, requests, span,
    sreq_ref, skind_ref, slim_ref, sfresh_ref,
    q_ref, kf_ref, vf_ref, kc_ref, vc_ref,
    out_ref, ko_ref, vo_ref, acc_ref, ml_ref,
):
    step = pl.program_id(0)
    lanes = ml_ref.shape[1]
    width = heads * head_dim

    @pl.when(step == 0)
    def _init():
        acc_ref[...] = jnp.zeros_like(acc_ref)
        lane = lax.broadcasted_iota(jnp.int32, ml_ref.shape, 1)
        ml_ref[...] = jnp.where(lane < heads, mask_score, 0.0).astype(jnp.float32)

    request = sreq_ref[step]
    kind = skind_ref[step]
    limit = slim_ref[step]
    scale = 1.0 / math.sqrt(head_dim)

    def attend(k_ref, v_ref):
        base = pl.multiple_of(request * span, span)
        rows = lax.broadcasted_iota(jnp.int32, (span, PAGE), 0)
        cols = lax.broadcasted_iota(jnp.int32, (span, PAGE), 1)
        allowed = rows - cols >= limit
        lane = lax.broadcasted_iota(jnp.int32, (span, lanes), 1)
        ml = ml_ref[pl.ds(base, span), :]
        for h in range(heads):
            cut = slice(h * head_dim, (h + 1) * head_dim)
            q_h = q_ref[0, pl.ds(base, span), cut]
            k_h = k_ref[0, :, cut]
            v_h = v_ref[0, :, cut]
            scores = lax.dot_general(
                q_h, k_h, (((1,), (1,)), ((), ())), preferred_element_type=jnp.float32
            ) * scale
            scores = jnp.where(allowed, scores, mask_score)
            m_prev = ml[:, h : h + 1]
            l_prev = ml[:, heads + h : heads + h + 1]
            m_new = jnp.maximum(m_prev, jnp.max(scores, axis=1, keepdims=True))
            m_new = m_new.astype(jnp.bfloat16).astype(jnp.float32)
            alpha = jnp.exp(m_prev - m_new)
            weights = jnp.where(allowed, jnp.exp(scores - m_new), 0.0)
            l_new = alpha * l_prev + jnp.sum(weights, axis=1, keepdims=True)
            contrib = jnp.dot(
                weights.astype(jnp.bfloat16), v_h, preferred_element_type=jnp.float32
            )
            acc_ref[pl.ds(base, span), cut] = alpha * acc_ref[pl.ds(base, span), cut] + contrib
            ml = jnp.where(
                lane == h,
                m_new,
                jnp.where((lane == heads + h) | (lane == 2 * heads + h), l_new, ml),
            )
        ml_ref[pl.ds(base, span), :] = ml

    @pl.when(kind == 1)
    def _cached():
        attend(kc_ref, vc_ref)

    @pl.when(kind == 2)
    def _fresh():
        attend(kf_ref, vf_ref)

    @pl.when(kind == 2)
    def _store_fresh():
        ko_ref[...] = kf_ref[...]
        vo_ref[...] = vf_ref[...]

    @pl.when(kind != 2)
    def _store_cached():
        ko_ref[...] = kc_ref[...]
        vo_ref[...] = vc_ref[...]

    @pl.when(step == pl.num_programs(0) - 1)
    def _emit():
        chunks, rows_per, _ = out_ref.shape
        lane = lax.broadcasted_iota(jnp.int32, (rows_per, lanes), 1)
        for d in range(chunks):
            rows = pl.ds(d * rows_per, rows_per)
            out_ref[d, :, :width] = acc_ref[rows, :].astype(jnp.bfloat16)
            ml = ml_ref[rows, :]
            rounded = ml.astype(jnp.bfloat16).astype(jnp.float32)
            packed = jnp.where(
                lane < 2 * heads,
                rounded,
                jnp.where(lane < 3 * heads, ml - rounded, 0.0),
            )
            out_ref[d, :, width:] = packed.astype(jnp.bfloat16)


def local_attention(slot_request, slot_kind, slot_limit, slot_fresh, gathered, kc, vc,
                    heads, head_dim, requests, span, chunks):
    _, tokens, width = gathered.shape
    slot_count = kc.shape[0]
    rows_per = tokens // chunks
    kernel = functools.partial(attend_kernel, heads, head_dim, requests, span)
    flops = 4 * slot_count * span * PAGE * width
    return pl.pallas_call(
        kernel,
        out_shape=(
            jax.ShapeDtypeStruct((chunks, rows_per, width + 128), jnp.bfloat16),
            jax.ShapeDtypeStruct(kc.shape, kc.dtype),
            jax.ShapeDtypeStruct(vc.shape, vc.dtype),
        ),
        grid_spec=pltpu.PrefetchScalarGridSpec(
            num_scalar_prefetch=4,
            grid=(slot_count,),
            in_specs=[
                pl.BlockSpec((1, tokens, width), lambda s, *_: (0, 0, 0),
                             pipeline_mode=pl.Buffered(1)),
                pl.BlockSpec((1, PAGE, width), lambda s, rq, kd, lm, fr: (1, fr[s], 0)),
                pl.BlockSpec((1, PAGE, width), lambda s, rq, kd, lm, fr: (2, fr[s], 0)),
                pl.BlockSpec((1, PAGE, width), lambda s, *_: (s, 0, 0)),
                pl.BlockSpec((1, PAGE, width), lambda s, *_: (s, 0, 0)),
            ],
            out_specs=[
                pl.BlockSpec((chunks, rows_per, width + 128), lambda s, *_: (0, 0, 0)),
                pl.BlockSpec((1, PAGE, width), lambda s, *_: (s, 0, 0)),
                pl.BlockSpec((1, PAGE, width), lambda s, *_: (s, 0, 0)),
            ],
            scratch_shapes=[
                pltpu.VMEM((tokens, width), jnp.float32),
                pltpu.VMEM((tokens, 128), jnp.float32),
            ],
        ),
        compiler_params=pltpu.CompilerParams(
            dimension_semantics=("arbitrary",), vmem_limit_bytes=60 * 1024 * 1024
        ),
        cost_estimate=pl.CostEstimate(
            flops=flops,
            transcendentals=slot_count * span * PAGE * heads,
            bytes_accessed=tokens * width * 2 + 4 * kc.size * 2 + tokens * (width + 128) * 2,
        ),
    )(slot_request, slot_kind, slot_limit, slot_fresh, gathered, gathered, gathered, kc, vc)


def combine_kernel(heads, head_dim, recv_ref, w_ref, out_ref, o_acc, l_acc):
    chunks, rows_per, _ = recv_ref.shape
    width = heads * head_dim
    lanes = 128

    def peak_step(d, peak):
        return jnp.maximum(peak, recv_ref[d, :, width:].astype(jnp.float32))

    peak = lax.fori_loop(
        0, chunks, peak_step, jnp.full((rows_per, lanes), mask_score, jnp.float32)
    )
    o_acc[...] = jnp.zeros_like(o_acc)
    l_acc[...] = jnp.zeros_like(l_acc)

    def sum_step(d, carry):
        mld = recv_ref[d, :, width:].astype(jnp.float32)
        factor = jnp.exp(mld - peak)
        for h in range(heads):
            f_h = factor[:, h : h + 1]
            l_h = mld[:, heads + h : heads + h + 1] + mld[:, 2 * heads + h : 2 * heads + h + 1]
            l_acc[:, h : h + 1] += f_h * l_h
            cut = slice(h * head_dim, (h + 1) * head_dim)
            o_acc[:, cut] += f_h * recv_ref[d, :, cut].astype(jnp.float32)
        return carry

    lax.fori_loop(0, chunks, sum_step, 0)
    parts = []
    for h in range(heads):
        cut = slice(h * head_dim, (h + 1) * head_dim)
        parts.append((o_acc[:, cut] / l_acc[:, h : h + 1]).astype(jnp.bfloat16))
    attended = jnp.concatenate(parts, axis=1)
    out_ref[...] = lax.dot_general(
        attended, w_ref[0], (((1,), (1,)), ((), ())), preferred_element_type=jnp.float32
    ).astype(out_ref.dtype)


def combine_project(received, gathered, heads, head_dim):
    chunks, rows_per, _ = received.shape
    _, tokens, width = gathered.shape
    kernel = functools.partial(combine_kernel, heads, head_dim)
    return pl.pallas_call(
        kernel,
        out_shape=jax.ShapeDtypeStruct((rows_per, tokens), jnp.bfloat16),
        grid=(1,),
        in_specs=[
            pl.BlockSpec(received.shape, lambda i: (0, 0, 0)),
            pl.BlockSpec((1, tokens, width), lambda i: (3, 0, 0)),
        ],
        out_specs=pl.BlockSpec((rows_per, tokens), lambda i: (0, 0)),
        scratch_shapes=[
            pltpu.VMEM((rows_per, width), jnp.float32),
            pltpu.VMEM((rows_per, 128), jnp.float32),
        ],
        compiler_params=pltpu.CompilerParams(vmem_limit_bytes=48 * 1024 * 1024),
        cost_estimate=pl.CostEstimate(
            flops=2 * rows_per * tokens * width + 4 * received.size,
            transcendentals=chunks * rows_per * 128,
            bytes_accessed=received.size * 2 + tokens * width * 2 + rows_per * tokens * 2,
        ),
    )(received, gathered)


def per_device(
    queries,
    keys,
    values,
    key_cache,
    value_cache,
    cache_len,
    page_table,
    append_slots,
    out_weight,
    out_bias,
):
    tok_dev, head_count, head_dim = queries.shape
    width = head_count * head_dim
    requests = cache_len.shape[0]
    max_pages = page_table.shape[1]
    new_pages = append_slots.shape[1]
    span_len = new_pages * PAGE
    slot_count = key_cache.shape[0]
    page_devices = lax.axis_size("pages")
    device_at = lax.axis_index("pages")
    token_ids = device_at * tok_dev + jnp.arange(tok_dev, dtype=jnp.int32)
    request_ids = token_ids // span_len
    request_grid = jnp.arange(requests, dtype=jnp.int32)
    starts = jnp.sum(
        jnp.where(request_ids[:, None] == request_grid[None, :], cache_len[None, :], 0), axis=1
    )
    positions = (starts + token_ids % span_len).astype(jnp.float32)
    rotated_q = rotate(queries.astype(jnp.float32), positions).astype(jnp.bfloat16)
    rotated_k = rotate(keys.astype(jnp.float32), positions).astype(jnp.bfloat16)
    w_cols = out_weight.shape[1]
    w_plane = jnp.pad(out_weight.T, ((0, tok_dev - w_cols), (0, 0)))
    stacked = jnp.stack(
        [
            rotated_q.reshape(tok_dev, width),
            rotated_k.reshape(tok_dev, width),
            values.reshape(tok_dev, width),
            w_plane,
        ]
    )
    gathered = lax.all_gather(stacked, "pages", axis=1, tiled=True)
    my_slots = device_at * slot_count + jnp.arange(slot_count, dtype=jnp.int32)
    cached_hit = page_table.reshape(-1)[None, :] == my_slots[:, None]
    fresh_hit = append_slots.reshape(-1)[None, :] == my_slots[:, None]
    is_cached = jnp.any(cached_hit, axis=1)
    is_fresh = jnp.any(fresh_hit, axis=1)
    cached_index = jnp.sum(
        jnp.where(cached_hit, jnp.arange(requests * max_pages, dtype=jnp.int32)[None, :], 0), axis=1
    )
    fresh_index = jnp.sum(
        jnp.where(fresh_hit, jnp.arange(requests * new_pages, dtype=jnp.int32)[None, :], 0), axis=1
    )
    slot_request = jnp.where(is_fresh, fresh_index // new_pages, cached_index // max_pages)
    slot_page = jnp.where(is_fresh, fresh_index % new_pages, cached_index % max_pages)
    slot_length = jnp.sum(
        jnp.where(slot_request[:, None] == request_grid[None, :], cache_len[None, :], 0), axis=1
    )
    visible = is_cached & (slot_page * PAGE < slot_length)
    slot_kind = jnp.where(is_fresh, 2, jnp.where(visible, 1, 0)).astype(jnp.int32)
    slot_limit = jnp.where(is_fresh, slot_page * PAGE, -4 * span_len)
    packed, key_slots, value_slots = local_attention(
        slot_request,
        slot_kind,
        slot_limit,
        fresh_index,
        gathered,
        key_cache.reshape(slot_count, PAGE, width),
        value_cache.reshape(slot_count, PAGE, width),
        head_count,
        head_dim,
        requests,
        span_len,
        page_devices,
    )
    received = lax.all_to_all(packed, "pages", 0, 0, tiled=True)
    projected = combine_project(received, gathered, head_count, head_dim)
    projected = projected.reshape(tok_dev, page_devices, tok_dev)[:, :, :w_cols].reshape(
        tok_dev, page_devices * w_cols
    )
    key_out = key_slots.reshape(key_cache.shape)
    value_out = value_slots.reshape(value_cache.shape)
    summed = lax.psum_scatter(projected, "heads", scatter_dimension=1, tiled=True).astype(jnp.float32)
    hidden = (summed + out_bias[None, :]).astype(jnp.bfloat16)
    return (hidden, key_out, value_out)


def solution(mesh):
    placed = (
        P("pages", "heads", None),
        P("pages", "heads", None),
        P("pages", "heads", None),
        P("pages", None, "heads", None),
        P("pages", None, "heads", None),
        P(),
        P(),
        P(),
        P("heads", "pages"),
        P("heads"),
    )
    return jax.shard_map(
        per_device,
        mesh=mesh,
        in_specs=placed,
        out_specs=(
            P("pages", "heads"),
            P("pages", None, "heads", None),
            P("pages", None, "heads", None),
        ),
        check_vma=False,
    )
```

```python
import functools
import math

import jax
import jax.numpy as jnp
from jax import lax
from jax.experimental import pallas as pl
from jax.experimental.pallas import tpu as pltpu
from jax.sharding import PartitionSpec as P

ROT = 32
PAGE = 128
PAGES = ("chips", "core")


low_score = -1e30
mask_score = -(2.0 ** 100)


def rotate(vectors, positions):
    half_rot = ROT // 2
    inv_freq = 10000.0 ** (-2.0 * jnp.arange(half_rot, dtype=jnp.float32) / ROT)
    angles = positions[:, None] * inv_freq[None, :]
    cosine = jnp.cos(angles)[:, None, :]
    sine = jnp.sin(angles)[:, None, :]
    first_half = vectors[..., :half_rot]
    second_half = vectors[..., half_rot:ROT]
    return jnp.concatenate(
        [
            first_half * cosine - second_half * sine,
            second_half * cosine + first_half * sine,
            vectors[..., ROT:],
        ],
        axis=-1,
    )


def attend_kernel(
    heads, head_dim, requests, span,
    sreq_ref, skind_ref, slim_ref, sfresh_ref,
    q_ref, kf_ref, vf_ref, kc_ref, vc_ref,
    out_ref, ko_ref, vo_ref, acc_ref, ml_ref,
):
    step = pl.program_id(0)
    lanes = ml_ref.shape[1]
    width = heads * head_dim

    @pl.when(step == 0)
    def _init():
        acc_ref[...] = jnp.zeros_like(acc_ref)
        lane = lax.broadcasted_iota(jnp.int32, ml_ref.shape, 1)
        ml_ref[...] = jnp.where(lane < heads, mask_score, 0.0).astype(jnp.float32)

    request = sreq_ref[step]
    kind = skind_ref[step]
    limit = slim_ref[step]
    scale = 1.0 / math.sqrt(head_dim)

    def attend(k_ref, v_ref):
        base = pl.multiple_of(request * span, span)
        rows = lax.broadcasted_iota(jnp.int32, (span, PAGE), 0)
        cols = lax.broadcasted_iota(jnp.int32, (span, PAGE), 1)
        allowed = rows - cols >= limit
        lane = lax.broadcasted_iota(jnp.int32, (span, lanes), 1)
        ml = ml_ref[pl.ds(base, span), :]
        for h in range(heads):
            cut = slice(h * head_dim, (h + 1) * head_dim)
            q_h = q_ref[0, pl.ds(base, span), cut]
            k_h = k_ref[0, :, cut]
            v_h = v_ref[0, :, cut]
            scores = lax.dot_general(
                q_h, k_h, (((1,), (1,)), ((), ())), preferred_element_type=jnp.float32
            ) * scale
            scores = jnp.where(allowed, scores, mask_score)
            m_prev = ml[:, h : h + 1]
            l_prev = ml[:, heads + h : heads + h + 1]
            m_new = jnp.maximum(m_prev, jnp.max(scores, axis=1, keepdims=True))
            m_new = m_new.astype(jnp.bfloat16).astype(jnp.float32)
            alpha = jnp.exp(m_prev - m_new)
            weights = jnp.where(allowed, jnp.exp(scores - m_new), 0.0)
            l_new = alpha * l_prev + jnp.sum(weights, axis=1, keepdims=True)
            contrib = jnp.dot(
                weights.astype(jnp.bfloat16), v_h, preferred_element_type=jnp.float32
            )
            acc_ref[pl.ds(base, span), cut] = alpha * acc_ref[pl.ds(base, span), cut] + contrib
            ml = jnp.where(
                lane == h,
                m_new,
                jnp.where((lane == heads + h) | (lane == 2 * heads + h), l_new, ml),
            )
        ml_ref[pl.ds(base, span), :] = ml

    @pl.when(kind == 1)
    def _cached():
        attend(kc_ref, vc_ref)

    @pl.when(kind == 2)
    def _fresh():
        attend(kf_ref, vf_ref)

    @pl.when(kind == 2)
    def _store_fresh():
        ko_ref[...] = kf_ref[...]
        vo_ref[...] = vf_ref[...]

    @pl.when(kind != 2)
    def _store_cached():
        ko_ref[...] = kc_ref[...]
        vo_ref[...] = vc_ref[...]

    @pl.when(step == pl.num_programs(0) - 1)
    def _emit():
        chunks, rows_per, _ = out_ref.shape
        lane = lax.broadcasted_iota(jnp.int32, (rows_per, lanes), 1)
        for d in range(chunks):
            rows = pl.ds(d * rows_per, rows_per)
            out_ref[d, :, :width] = acc_ref[rows, :].astype(jnp.bfloat16)
            ml = ml_ref[rows, :]
            rounded = ml.astype(jnp.bfloat16).astype(jnp.float32)
            packed = jnp.where(
                lane < 2 * heads,
                rounded,
                jnp.where(lane < 3 * heads, ml - rounded, 0.0),
            )
            out_ref[d, :, width:] = packed.astype(jnp.bfloat16)


def local_attention(slot_request, slot_kind, slot_limit, slot_fresh, gathered, kc, vc,
                    heads, head_dim, requests, span, chunks):
    _, tokens, width = gathered.shape
    slot_count = kc.shape[0]
    rows_per = tokens // chunks
    kernel = functools.partial(attend_kernel, heads, head_dim, requests, span)
    flops = 4 * slot_count * span * PAGE * width
    return pl.pallas_call(
        kernel,
        out_shape=(
            jax.ShapeDtypeStruct((chunks, rows_per, width + 128), jnp.bfloat16),
            jax.ShapeDtypeStruct(kc.shape, kc.dtype),
            jax.ShapeDtypeStruct(vc.shape, vc.dtype),
        ),
        grid_spec=pltpu.PrefetchScalarGridSpec(
            num_scalar_prefetch=4,
            grid=(slot_count,),
            in_specs=[
                pl.BlockSpec((1, tokens, width), lambda s, *_: (0, 0, 0),
                             pipeline_mode=pl.Buffered(1)),
                pl.BlockSpec((1, PAGE, width), lambda s, rq, kd, lm, fr: (1, fr[s], 0)),
                pl.BlockSpec((1, PAGE, width), lambda s, rq, kd, lm, fr: (2, fr[s], 0)),
                pl.BlockSpec((1, PAGE, width), lambda s, *_: (s, 0, 0)),
                pl.BlockSpec((1, PAGE, width), lambda s, *_: (s, 0, 0)),
            ],
            out_specs=[
                pl.BlockSpec((chunks, rows_per, width + 128), lambda s, *_: (0, 0, 0)),
                pl.BlockSpec((1, PAGE, width), lambda s, *_: (s, 0, 0)),
                pl.BlockSpec((1, PAGE, width), lambda s, *_: (s, 0, 0)),
            ],
            scratch_shapes=[
                pltpu.VMEM((tokens, width), jnp.float32),
                pltpu.VMEM((tokens, 128), jnp.float32),
            ],
        ),
        compiler_params=pltpu.CompilerParams(
            dimension_semantics=("arbitrary",), vmem_limit_bytes=60 * 1024 * 1024
        ),
        cost_estimate=pl.CostEstimate(
            flops=flops,
            transcendentals=slot_count * span * PAGE * heads,
            bytes_accessed=tokens * width * 2 + 4 * kc.size * 2 + tokens * (width + 128) * 2,
        ),
    )(slot_request, slot_kind, slot_limit, slot_fresh, gathered, gathered, gathered, kc, vc)


def combine_kernel(heads, head_dim, recv_ref, w_ref, out_ref, o_acc, l_acc):
    chunks, rows_per, _ = recv_ref.shape
    width = heads * head_dim
    lanes = 128

    def peak_step(d, peak):
        return jnp.maximum(peak, recv_ref[d, :, width:].astype(jnp.float32))

    peak = lax.fori_loop(
        0, chunks, peak_step, jnp.full((rows_per, lanes), mask_score, jnp.float32)
    )
    o_acc[...] = jnp.zeros_like(o_acc)
    l_acc[...] = jnp.zeros_like(l_acc)

    def sum_step(d, carry):
        mld = recv_ref[d, :, width:].astype(jnp.float32)
        factor = jnp.exp(mld - peak)
        for h in range(heads):
            f_h = factor[:, h : h + 1]
            l_h = mld[:, heads + h : heads + h + 1] + mld[:, 2 * heads + h : 2 * heads + h + 1]
            l_acc[:, h : h + 1] += f_h * l_h
            cut = slice(h * head_dim, (h + 1) * head_dim)
            o_acc[:, cut] += f_h * recv_ref[d, :, cut].astype(jnp.float32)
        return carry

    lax.fori_loop(0, chunks, sum_step, 0)
    parts = []
    for h in range(heads):
        cut = slice(h * head_dim, (h + 1) * head_dim)
        parts.append((o_acc[:, cut] / l_acc[:, h : h + 1]).astype(jnp.bfloat16))
    attended = jnp.concatenate(parts, axis=1)
    out_ref[...] = lax.dot_general(
        attended, w_ref[0], (((1,), (1,)), ((), ())), preferred_element_type=jnp.float32
    ).astype(out_ref.dtype)


def combine_project(received, gathered, heads, head_dim):
    chunks, rows_per, _ = received.shape
    _, tokens, width = gathered.shape
    kernel = functools.partial(combine_kernel, heads, head_dim)
    return pl.pallas_call(
        kernel,
        out_shape=jax.ShapeDtypeStruct((rows_per, tokens), jnp.bfloat16),
        grid=(1,),
        in_specs=[
            pl.BlockSpec(received.shape, lambda i: (0, 0, 0)),
            pl.BlockSpec((1, tokens, width), lambda i: (3, 0, 0)),
        ],
        out_specs=pl.BlockSpec((rows_per, tokens), lambda i: (0, 0)),
        scratch_shapes=[
            pltpu.VMEM((rows_per, width), jnp.float32),
            pltpu.VMEM((rows_per, 128), jnp.float32),
        ],
        compiler_params=pltpu.CompilerParams(vmem_limit_bytes=48 * 1024 * 1024),
        cost_estimate=pl.CostEstimate(
            flops=2 * rows_per * tokens * width + 4 * received.size,
            transcendentals=chunks * rows_per * 128,
            bytes_accessed=received.size * 2 + tokens * width * 2 + rows_per * tokens * 2,
        ),
    )(received, gathered)


def pair_merge_kernel(heads, head_dim, packed_hbm, out_ref, mine, theirs, local_sem, send_sem, recv_sem):
    core = lax.axis_index("core")
    partner = 1 - core
    width = heads * head_dim
    lanes = 128
    chunks, rows_per, _ = out_ref.shape

    barrier = pltpu.get_barrier_semaphore()
    pl.semaphore_signal(barrier, inc=1, device_id={"core": partner}, device_id_type=pl.DeviceIdType.MESH)
    pl.semaphore_wait(barrier, 1)

    local = pltpu.make_async_copy(packed_hbm.at[:, core], mine, local_sem)
    local.start()
    remote = pltpu.make_async_remote_copy(
        src_ref=packed_hbm.at[:, partner],
        dst_ref=theirs,
        send_sem=send_sem,
        recv_sem=recv_sem,
        device_id={"core": partner},
        device_id_type=pl.DeviceIdType.MESH,
    )
    remote.start()
    local.wait()
    remote.wait()

    lane = lax.broadcasted_iota(jnp.int32, (rows_per, lanes), 1)

    def merge_step(c, carry):
        ml_a = mine[c, :, width:].astype(jnp.float32)
        ml_b = theirs[c, :, width:].astype(jnp.float32)
        peak = jnp.maximum(ml_a, ml_b)
        f_a = jnp.exp(ml_a - peak)
        f_b = jnp.exp(ml_b - peak)
        merged = jnp.zeros((rows_per, lanes), jnp.float32)
        for h in range(heads):
            cut = slice(h * head_dim, (h + 1) * head_dim)
            fa_h = f_a[:, h : h + 1]
            fb_h = f_b[:, h : h + 1]
            out_ref[c, :, cut] = (
                fa_h * mine[c, :, cut].astype(jnp.float32)
                + fb_h * theirs[c, :, cut].astype(jnp.float32)
            ).astype(out_ref.dtype)
            l_a = ml_a[:, heads + h : heads + h + 1] + ml_a[:, 2 * heads + h : 2 * heads + h + 1]
            l_b = ml_b[:, heads + h : heads + h + 1] + ml_b[:, 2 * heads + h : 2 * heads + h + 1]
            l_h = fa_h * l_a + fb_h * l_b
            l_hi = l_h.astype(jnp.bfloat16).astype(jnp.float32)
            merged = jnp.where(
                lane == h,
                peak[:, h : h + 1],
                jnp.where(
                    lane == heads + h,
                    l_hi,
                    jnp.where(lane == 2 * heads + h, l_h - l_hi, merged),
                ),
            )
        out_ref[c, :, width:] = merged.astype(out_ref.dtype)
        return carry

    lax.fori_loop(0, chunks, merge_step, 0)


def pair_merge(packed, heads, head_dim):
    devices, rows_per, lanes_all = packed.shape
    chips = devices // 2
    view = packed.reshape(chips, 2, rows_per, lanes_all)
    kernel = functools.partial(pair_merge_kernel, heads, head_dim)
    return pl.pallas_call(
        kernel,
        out_shape=jax.ShapeDtypeStruct((chips, rows_per, lanes_all), packed.dtype),
        in_specs=[pl.BlockSpec(memory_space=pl.ANY)],
        out_specs=pl.BlockSpec(memory_space=pltpu.VMEM),
        scratch_shapes=[
            pltpu.VMEM((chips, rows_per, lanes_all), packed.dtype),
            pltpu.VMEM((chips, rows_per, lanes_all), packed.dtype),
            pltpu.SemaphoreType.DMA(()),
            pltpu.SemaphoreType.DMA(()),
            pltpu.SemaphoreType.DMA(()),
        ],
        compiler_params=pltpu.CompilerParams(
            collective_id=0, has_side_effects=True, vmem_limit_bytes=40 * 1024 * 1024
        ),
        cost_estimate=pl.CostEstimate(
            flops=6 * chips * rows_per * lanes_all,
            transcendentals=2 * chips * rows_per * 128,
            bytes_accessed=3 * chips * rows_per * lanes_all * 2,
        ),
    )(view)


def per_device(
    queries,
    keys,
    values,
    key_cache,
    value_cache,
    cache_len,
    page_table,
    append_slots,
    out_weight,
    out_bias,
):
    tok_dev, head_count, head_dim = queries.shape
    width = head_count * head_dim
    requests = cache_len.shape[0]
    max_pages = page_table.shape[1]
    new_pages = append_slots.shape[1]
    span_len = new_pages * PAGE
    slot_count = key_cache.shape[0]
    page_devices = lax.axis_size(PAGES)
    device_at = lax.axis_index(PAGES)
    token_ids = device_at * tok_dev + jnp.arange(tok_dev, dtype=jnp.int32)
    request_ids = token_ids // span_len
    request_grid = jnp.arange(requests, dtype=jnp.int32)
    starts = jnp.sum(
        jnp.where(request_ids[:, None] == request_grid[None, :], cache_len[None, :], 0), axis=1
    )
    positions = (starts + token_ids % span_len).astype(jnp.float32)
    rotated_q = rotate(queries.astype(jnp.float32), positions).astype(jnp.bfloat16)
    rotated_k = rotate(keys.astype(jnp.float32), positions).astype(jnp.bfloat16)
    w_cols = out_weight.shape[1]
    w_plane = jnp.pad(out_weight.T, ((0, tok_dev - w_cols), (0, 0)))
    stacked = jnp.stack(
        [
            rotated_q.reshape(tok_dev, width),
            rotated_k.reshape(tok_dev, width),
            values.reshape(tok_dev, width),
            w_plane,
        ]
    )
    gathered = lax.all_gather(stacked, PAGES, axis=1, tiled=True)
    my_slots = device_at * slot_count + jnp.arange(slot_count, dtype=jnp.int32)
    cached_hit = page_table.reshape(-1)[None, :] == my_slots[:, None]
    fresh_hit = append_slots.reshape(-1)[None, :] == my_slots[:, None]
    is_cached = jnp.any(cached_hit, axis=1)
    is_fresh = jnp.any(fresh_hit, axis=1)
    cached_index = jnp.sum(
        jnp.where(cached_hit, jnp.arange(requests * max_pages, dtype=jnp.int32)[None, :], 0), axis=1
    )
    fresh_index = jnp.sum(
        jnp.where(fresh_hit, jnp.arange(requests * new_pages, dtype=jnp.int32)[None, :], 0), axis=1
    )
    slot_request = jnp.where(is_fresh, fresh_index // new_pages, cached_index // max_pages)
    slot_page = jnp.where(is_fresh, fresh_index % new_pages, cached_index % max_pages)
    slot_length = jnp.sum(
        jnp.where(slot_request[:, None] == request_grid[None, :], cache_len[None, :], 0), axis=1
    )
    visible = is_cached & (slot_page * PAGE < slot_length)
    slot_kind = jnp.where(is_fresh, 2, jnp.where(visible, 1, 0)).astype(jnp.int32)
    slot_limit = jnp.where(is_fresh, slot_page * PAGE, -4 * span_len)
    packed, key_slots, value_slots = local_attention(
        slot_request,
        slot_kind,
        slot_limit,
        fresh_index,
        gathered,
        key_cache.reshape(slot_count, PAGE, width),
        value_cache.reshape(slot_count, PAGE, width),
        head_count,
        head_dim,
        requests,
        span_len,
        page_devices,
    )
    paired = pair_merge(packed, head_count, head_dim)
    received = lax.all_to_all(paired, "chips", 0, 0, tiled=True)
    projected = combine_project(received, gathered, head_count, head_dim)
    projected = projected.reshape(tok_dev, page_devices, tok_dev)[:, :, :w_cols].reshape(
        tok_dev, page_devices * w_cols
    )
    key_out = key_slots.reshape(key_cache.shape)
    value_out = value_slots.reshape(value_cache.shape)
    summed = lax.psum_scatter(projected, "heads", scatter_dimension=1, tiled=True).astype(jnp.float32)
    hidden = (summed + out_bias[None, :]).astype(jnp.bfloat16)
    return (hidden, key_out, value_out)


def solution(mesh):
    heads_n, pages_n = mesh.devices.shape
    split = jax.sharding.Mesh(
        mesh.devices.reshape(heads_n, pages_n // 2, 2), ("heads", "chips", "core")
    )
    placed = (
        P(PAGES, "heads", None),
        P(PAGES, "heads", None),
        P(PAGES, "heads", None),
        P(PAGES, None, "heads", None),
        P(PAGES, None, "heads", None),
        P(),
        P(),
        P(),
        P("heads", PAGES),
        P("heads"),
    )
    return jax.shard_map(
        per_device,
        mesh=split,
        in_specs=placed,
        out_specs=(
            P(PAGES, "heads"),
            P(PAGES, None, "heads", None),
            P(PAGES, None, "heads", None),
        ),
        check_vma=False,
    )
```

```python
import functools
import math

import jax
import jax.numpy as jnp
from jax import lax
from jax.experimental import pallas as pl
from jax.experimental.pallas import tpu as pltpu
from jax.sharding import PartitionSpec as P

ROT = 32
PAGE = 128
PAGES = ("chips", "core")


low_score = -1e30
mask_score = -(2.0 ** 100)


def rotate(vectors, positions):
    half_rot = ROT // 2
    inv_freq = 10000.0 ** (-2.0 * jnp.arange(half_rot, dtype=jnp.float32) / ROT)
    angles = positions[:, None] * inv_freq[None, :]
    cosine = jnp.cos(angles)[:, None, :]
    sine = jnp.sin(angles)[:, None, :]
    first_half = vectors[..., :half_rot]
    second_half = vectors[..., half_rot:ROT]
    return jnp.concatenate(
        [
            first_half * cosine - second_half * sine,
            second_half * cosine + first_half * sine,
            vectors[..., ROT:],
        ],
        axis=-1,
    )


def attend_kernel(
    heads, head_dim, requests, span,
    sreq_ref, skind_ref, slim_ref, sfresh_ref,
    q_ref, kf_ref, vf_ref, kc_ref, vc_ref,
    out_ref, ko_ref, vo_ref, acc_ref, ml_ref,
):
    step = pl.program_id(0)
    lanes = ml_ref.shape[1]
    width = heads * head_dim

    @pl.when(step == 0)
    def _init():
        acc_ref[...] = jnp.zeros_like(acc_ref)
        lane = lax.broadcasted_iota(jnp.int32, ml_ref.shape, 1)
        ml_ref[...] = jnp.where(lane < heads, mask_score, 0.0).astype(jnp.float32)

    request = sreq_ref[step]
    kind = skind_ref[step]
    limit = slim_ref[step]
    scale = 1.0 / math.sqrt(head_dim)

    def attend(k_ref, v_ref):
        base = pl.multiple_of(request * span, span)
        rows = lax.broadcasted_iota(jnp.int32, (span, PAGE), 0)
        cols = lax.broadcasted_iota(jnp.int32, (span, PAGE), 1)
        allowed = rows - cols >= limit
        lane = lax.broadcasted_iota(jnp.int32, (span, lanes), 1)
        ml = ml_ref[pl.ds(base, span), :]
        for h in range(heads):
            cut = slice(h * head_dim, (h + 1) * head_dim)
            q_h = q_ref[0, pl.ds(base, span), cut]
            k_h = k_ref[0, :, cut]
            v_h = v_ref[0, :, cut]
            scores = lax.dot_general(
                q_h, k_h, (((1,), (1,)), ((), ())), preferred_element_type=jnp.float32
            ) * scale
            scores = jnp.where(allowed, scores, mask_score)
            m_prev = ml[:, h : h + 1]
            l_prev = ml[:, heads + h : heads + h + 1]
            m_new = jnp.maximum(m_prev, jnp.max(scores, axis=1, keepdims=True))
            m_new = m_new.astype(jnp.bfloat16).astype(jnp.float32)
            alpha = jnp.exp(m_prev - m_new)
            weights = jnp.where(allowed, jnp.exp(scores - m_new), 0.0)
            l_new = alpha * l_prev + jnp.sum(weights, axis=1, keepdims=True)
            contrib = jnp.dot(
                weights.astype(jnp.bfloat16), v_h, preferred_element_type=jnp.float32
            )
            acc_ref[pl.ds(base, span), cut] = alpha * acc_ref[pl.ds(base, span), cut] + contrib
            ml = jnp.where(
                lane == h,
                m_new,
                jnp.where((lane == heads + h) | (lane == 2 * heads + h), l_new, ml),
            )
        ml_ref[pl.ds(base, span), :] = ml

    @pl.when(kind == 1)
    def _cached():
        attend(kc_ref, vc_ref)

    @pl.when(kind == 2)
    def _fresh():
        attend(kf_ref, vf_ref)

    @pl.when(kind == 2)
    def _store_fresh():
        ko_ref[...] = kf_ref[...]
        vo_ref[...] = vf_ref[...]

    @pl.when(kind != 2)
    def _store_cached():
        ko_ref[...] = kc_ref[...]
        vo_ref[...] = vc_ref[...]

    @pl.when(step == pl.num_programs(0) - 1)
    def _emit():
        chunks, rows_per, _ = out_ref.shape
        lane = lax.broadcasted_iota(jnp.int32, (rows_per, lanes), 1)
        for d in range(chunks):
            rows = pl.ds(d * rows_per, rows_per)
            out_ref[d, :, :width] = acc_ref[rows, :].astype(jnp.bfloat16)
            ml = ml_ref[rows, :]
            rounded = ml.astype(jnp.bfloat16).astype(jnp.float32)
            packed = jnp.where(
                lane < 2 * heads,
                rounded,
                jnp.where(lane < 3 * heads, ml - rounded, 0.0),
            )
            out_ref[d, :, width:] = packed.astype(jnp.bfloat16)


def local_attention(slot_request, slot_kind, slot_limit, slot_fresh, gathered, kc, vc,
                    heads, head_dim, requests, span, chunks):
    _, tokens, width = gathered.shape
    slot_count = kc.shape[0]
    rows_per = tokens // chunks
    kernel = functools.partial(attend_kernel, heads, head_dim, requests, span)
    flops = 4 * slot_count * span * PAGE * width
    return pl.pallas_call(
        kernel,
        out_shape=(
            jax.ShapeDtypeStruct((chunks, rows_per, width + 128), jnp.bfloat16),
            jax.ShapeDtypeStruct(kc.shape, kc.dtype),
            jax.ShapeDtypeStruct(vc.shape, vc.dtype),
        ),
        grid_spec=pltpu.PrefetchScalarGridSpec(
            num_scalar_prefetch=4,
            grid=(slot_count,),
            in_specs=[
                pl.BlockSpec((1, tokens, width), lambda s, *_: (0, 0, 0),
                             pipeline_mode=pl.Buffered(1)),
                pl.BlockSpec((1, PAGE, width), lambda s, rq, kd, lm, fr: (1, fr[s], 0)),
                pl.BlockSpec((1, PAGE, width), lambda s, rq, kd, lm, fr: (2, fr[s], 0)),
                pl.BlockSpec((1, PAGE, width), lambda s, *_: (s, 0, 0)),
                pl.BlockSpec((1, PAGE, width), lambda s, *_: (s, 0, 0)),
            ],
            out_specs=[
                pl.BlockSpec((chunks, rows_per, width + 128), lambda s, *_: (0, 0, 0)),
                pl.BlockSpec((1, PAGE, width), lambda s, *_: (s, 0, 0)),
                pl.BlockSpec((1, PAGE, width), lambda s, *_: (s, 0, 0)),
            ],
            scratch_shapes=[
                pltpu.VMEM((tokens, width), jnp.float32),
                pltpu.VMEM((tokens, 128), jnp.float32),
            ],
        ),
        compiler_params=pltpu.CompilerParams(
            dimension_semantics=("arbitrary",), vmem_limit_bytes=60 * 1024 * 1024
        ),
        cost_estimate=pl.CostEstimate(
            flops=flops,
            transcendentals=slot_count * span * PAGE * heads,
            bytes_accessed=tokens * width * 2 + 4 * kc.size * 2 + tokens * (width + 128) * 2,
        ),
    )(slot_request, slot_kind, slot_limit, slot_fresh, gathered, gathered, gathered, kc, vc)


def combine_kernel(heads, head_dim, recv_ref, w_ref, out_ref, o_acc, l_acc):
    chunks, rows_per, _ = recv_ref.shape
    width = heads * head_dim
    lanes = 128

    def peak_step(d, peak):
        return jnp.maximum(peak, recv_ref[d, :, width:].astype(jnp.float32))

    peak = lax.fori_loop(
        0, chunks, peak_step, jnp.full((rows_per, lanes), mask_score, jnp.float32)
    )
    o_acc[...] = jnp.zeros_like(o_acc)
    l_acc[...] = jnp.zeros_like(l_acc)

    def sum_step(d, carry):
        mld = recv_ref[d, :, width:].astype(jnp.float32)
        factor = jnp.exp(mld - peak)
        for h in range(heads):
            f_h = factor[:, h : h + 1]
            l_h = mld[:, heads + h : heads + h + 1] + mld[:, 2 * heads + h : 2 * heads + h + 1]
            l_acc[:, h : h + 1] += f_h * l_h
            cut = slice(h * head_dim, (h + 1) * head_dim)
            o_acc[:, cut] += f_h * recv_ref[d, :, cut].astype(jnp.float32)
        return carry

    lax.fori_loop(0, chunks, sum_step, 0)
    parts = []
    for h in range(heads):
        cut = slice(h * head_dim, (h + 1) * head_dim)
        parts.append((o_acc[:, cut] / l_acc[:, h : h + 1]).astype(jnp.bfloat16))
    attended = jnp.concatenate(parts, axis=1)
    out_ref[...] = lax.dot_general(
        attended, w_ref[0], (((1,), (1,)), ((), ())), preferred_element_type=jnp.float32
    ).astype(out_ref.dtype)


def combine_project(received, gathered, heads, head_dim):
    chunks, rows_per, _ = received.shape
    _, tokens, width = gathered.shape
    kernel = functools.partial(combine_kernel, heads, head_dim)
    return pl.pallas_call(
        kernel,
        out_shape=jax.ShapeDtypeStruct((rows_per, tokens), jnp.bfloat16),
        grid=(1,),
        in_specs=[
            pl.BlockSpec(received.shape, lambda i: (0, 0, 0)),
            pl.BlockSpec((1, tokens, width), lambda i: (3, 0, 0)),
        ],
        out_specs=pl.BlockSpec((rows_per, tokens), lambda i: (0, 0)),
        scratch_shapes=[
            pltpu.VMEM((rows_per, width), jnp.float32),
            pltpu.VMEM((rows_per, 128), jnp.float32),
        ],
        compiler_params=pltpu.CompilerParams(vmem_limit_bytes=48 * 1024 * 1024),
        cost_estimate=pl.CostEstimate(
            flops=2 * rows_per * tokens * width + 4 * received.size,
            transcendentals=chunks * rows_per * 128,
            bytes_accessed=received.size * 2 + tokens * width * 2 + rows_per * tokens * 2,
        ),
    )(received, gathered)


def pair_merge_kernel(heads, head_dim, packed_hbm, out_ref, mine, theirs, local_sem, send_sem, recv_sem):
    core = lax.axis_index("core")
    partner = 1 - core
    width = heads * head_dim
    lanes = 128
    chunks, rows_per, _ = out_ref.shape

    barrier = pltpu.get_barrier_semaphore()
    pl.semaphore_signal(barrier, inc=1, device_id={"core": partner}, device_id_type=pl.DeviceIdType.MESH)
    pl.semaphore_wait(barrier, 1)

    local = pltpu.make_async_copy(packed_hbm.at[:, core], mine, local_sem)
    local.start()
    remote = pltpu.make_async_remote_copy(
        src_ref=packed_hbm.at[:, partner],
        dst_ref=theirs,
        send_sem=send_sem,
        recv_sem=recv_sem,
        device_id={"core": partner},
        device_id_type=pl.DeviceIdType.MESH,
    )
    remote.start()
    local.wait()
    remote.wait()

    lane = lax.broadcasted_iota(jnp.int32, (rows_per, lanes), 1)

    def merge_step(c, carry):
        ml_a = mine[c, :, width:].astype(jnp.float32)
        ml_b = theirs[c, :, width:].astype(jnp.float32)
        peak = jnp.maximum(ml_a, ml_b)
        f_a = jnp.exp(ml_a - peak)
        f_b = jnp.exp(ml_b - peak)
        merged = jnp.zeros((rows_per, lanes), jnp.float32)
        for h in range(heads):
            cut = slice(h * head_dim, (h + 1) * head_dim)
            fa_h = f_a[:, h : h + 1]
            fb_h = f_b[:, h : h + 1]
            out_ref[c, :, cut] = (
                fa_h * mine[c, :, cut].astype(jnp.float32)
                + fb_h * theirs[c, :, cut].astype(jnp.float32)
            ).astype(out_ref.dtype)
            l_a = ml_a[:, heads + h : heads + h + 1] + ml_a[:, 2 * heads + h : 2 * heads + h + 1]
            l_b = ml_b[:, heads + h : heads + h + 1] + ml_b[:, 2 * heads + h : 2 * heads + h + 1]
            l_h = fa_h * l_a + fb_h * l_b
            l_hi = l_h.astype(jnp.bfloat16).astype(jnp.float32)
            merged = jnp.where(
                lane == h,
                peak[:, h : h + 1],
                jnp.where(
                    lane == heads + h,
                    l_hi,
                    jnp.where(lane == 2 * heads + h, l_h - l_hi, merged),
                ),
            )
        out_ref[c, :, width:] = merged.astype(out_ref.dtype)
        return carry

    lax.fori_loop(0, chunks, merge_step, 0)


def pair_merge(packed, heads, head_dim):
    devices, rows_per, lanes_all = packed.shape
    chips = devices // 2
    view = packed.reshape(chips, 2, rows_per, lanes_all)
    kernel = functools.partial(pair_merge_kernel, heads, head_dim)
    return pl.pallas_call(
        kernel,
        out_shape=jax.ShapeDtypeStruct((chips, rows_per, lanes_all), packed.dtype),
        in_specs=[pl.BlockSpec(memory_space=pl.ANY)],
        out_specs=pl.BlockSpec(memory_space=pltpu.VMEM),
        scratch_shapes=[
            pltpu.VMEM((chips, rows_per, lanes_all), packed.dtype),
            pltpu.VMEM((chips, rows_per, lanes_all), packed.dtype),
            pltpu.SemaphoreType.DMA(()),
            pltpu.SemaphoreType.DMA(()),
            pltpu.SemaphoreType.DMA(()),
        ],
        compiler_params=pltpu.CompilerParams(
            collective_id=0, has_side_effects=True, vmem_limit_bytes=40 * 1024 * 1024
        ),
        cost_estimate=pl.CostEstimate(
            flops=6 * chips * rows_per * lanes_all,
            transcendentals=2 * chips * rows_per * 128,
            bytes_accessed=3 * chips * rows_per * lanes_all * 2,
        ),
    )(view)


def per_device(
    queries,
    keys,
    values,
    key_cache,
    value_cache,
    cache_len,
    page_table,
    append_slots,
    out_weight,
    out_bias,
):
    tok_dev, head_count, head_dim = queries.shape
    width = head_count * head_dim
    requests = cache_len.shape[0]
    max_pages = page_table.shape[1]
    new_pages = append_slots.shape[1]
    span_len = new_pages * PAGE
    slot_count = key_cache.shape[0]
    page_devices = lax.axis_size(PAGES)
    device_at = lax.axis_index(PAGES)
    token_ids = device_at * tok_dev + jnp.arange(tok_dev, dtype=jnp.int32)
    request_ids = token_ids // span_len
    request_grid = jnp.arange(requests, dtype=jnp.int32)
    starts = jnp.sum(
        jnp.where(request_ids[:, None] == request_grid[None, :], cache_len[None, :], 0), axis=1
    )
    positions = (starts + token_ids % span_len).astype(jnp.float32)
    rotated_q = rotate(queries.astype(jnp.float32), positions).astype(jnp.bfloat16)
    rotated_k = rotate(keys.astype(jnp.float32), positions).astype(jnp.bfloat16)
    w_cols = out_weight.shape[1]
    w_plane = jnp.pad(out_weight.T, ((0, tok_dev - w_cols), (0, 0)))
    stacked = jnp.stack(
        [
            rotated_q.reshape(tok_dev, width),
            rotated_k.reshape(tok_dev, width),
            values.reshape(tok_dev, width),
            w_plane,
        ]
    )
    planes = stacked.shape[0]
    chip_rows = lax.all_gather(stacked, "core", axis=1, tiled=True)
    my_planes = lax.dynamic_slice_in_dim(
        chip_rows, lax.axis_index("core") * (planes // 2), planes // 2, axis=0
    )
    half = lax.all_gather(my_planes, "chips", axis=1, tiled=True)
    gathered = lax.all_gather(half, "core", axis=0, tiled=True)
    my_slots = device_at * slot_count + jnp.arange(slot_count, dtype=jnp.int32)
    cached_hit = page_table.reshape(-1)[None, :] == my_slots[:, None]
    fresh_hit = append_slots.reshape(-1)[None, :] == my_slots[:, None]
    is_cached = jnp.any(cached_hit, axis=1)
    is_fresh = jnp.any(fresh_hit, axis=1)
    cached_index = jnp.sum(
        jnp.where(cached_hit, jnp.arange(requests * max_pages, dtype=jnp.int32)[None, :], 0), axis=1
    )
    fresh_index = jnp.sum(
        jnp.where(fresh_hit, jnp.arange(requests * new_pages, dtype=jnp.int32)[None, :], 0), axis=1
    )
    slot_request = jnp.where(is_fresh, fresh_index // new_pages, cached_index // max_pages)
    slot_page = jnp.where(is_fresh, fresh_index % new_pages, cached_index % max_pages)
    slot_length = jnp.sum(
        jnp.where(slot_request[:, None] == request_grid[None, :], cache_len[None, :], 0), axis=1
    )
    visible = is_cached & (slot_page * PAGE < slot_length)
    slot_kind = jnp.where(is_fresh, 2, jnp.where(visible, 1, 0)).astype(jnp.int32)
    slot_limit = jnp.where(is_fresh, slot_page * PAGE, -4 * span_len)
    packed, key_slots, value_slots = local_attention(
        slot_request,
        slot_kind,
        slot_limit,
        fresh_index,
        gathered,
        key_cache.reshape(slot_count, PAGE, width),
        value_cache.reshape(slot_count, PAGE, width),
        head_count,
        head_dim,
        requests,
        span_len,
        page_devices,
    )
    paired = pair_merge(packed, head_count, head_dim)
    received = lax.all_to_all(paired, "chips", 0, 0, tiled=True)
    projected = combine_project(received, gathered, head_count, head_dim)
    projected = projected.reshape(tok_dev, page_devices, tok_dev)[:, :, :w_cols].reshape(
        tok_dev, page_devices * w_cols
    )
    key_out = key_slots.reshape(key_cache.shape)
    value_out = value_slots.reshape(value_cache.shape)
    summed = lax.psum_scatter(projected, "heads", scatter_dimension=1, tiled=True).astype(jnp.float32)
    hidden = (summed + out_bias[None, :]).astype(jnp.bfloat16)
    return (hidden, key_out, value_out)


def solution(mesh):
    heads_n, pages_n = mesh.devices.shape
    split = jax.sharding.Mesh(
        mesh.devices.reshape(heads_n, pages_n // 2, 2), ("heads", "chips", "core")
    )
    placed = (
        P(PAGES, "heads", None),
        P(PAGES, "heads", None),
        P(PAGES, "heads", None),
        P(PAGES, None, "heads", None),
        P(PAGES, None, "heads", None),
        P(),
        P(),
        P(),
        P("heads", PAGES),
        P("heads"),
    )
    return jax.shard_map(
        per_device,
        mesh=split,
        in_specs=placed,
        out_specs=(
            P(PAGES, "heads"),
            P(PAGES, None, "heads", None),
            P(PAGES, None, "heads", None),
        ),
        check_vma=False,
    )
```

```python
import functools
import math

import jax
import jax.numpy as jnp
from jax import lax
from jax.experimental import pallas as pl
from jax.experimental.pallas import tpu as pltpu
from jax.sharding import PartitionSpec as P

ROT = 32
PAGE = 128
PAGES = ("chips", "core")


low_score = -1e30
mask_score = -(2.0 ** 100)


def rotate(vectors, positions):
    half_rot = ROT // 2
    inv_freq = 10000.0 ** (-2.0 * jnp.arange(half_rot, dtype=jnp.float32) / ROT)
    angles = positions[:, None] * inv_freq[None, :]
    cosine = jnp.cos(angles)[:, None, :]
    sine = jnp.sin(angles)[:, None, :]
    first_half = vectors[..., :half_rot]
    second_half = vectors[..., half_rot:ROT]
    return jnp.concatenate(
        [
            first_half * cosine - second_half * sine,
            second_half * cosine + first_half * sine,
            vectors[..., ROT:],
        ],
        axis=-1,
    )


def attend_kernel(
    heads, head_dim, requests, span,
    sreq_ref, skind_ref, slim_ref, sfresh_ref,
    q_ref, kf_ref, vf_ref, kc_ref, vc_ref,
    out_ref, ko_ref, vo_ref, acc_ref, ml_ref,
):
    step = pl.program_id(0)
    lanes = ml_ref.shape[1]
    width = heads * head_dim

    @pl.when(step == 0)
    def _init():
        acc_ref[...] = jnp.zeros_like(acc_ref)
        lane = lax.broadcasted_iota(jnp.int32, ml_ref.shape, 1)
        ml_ref[...] = jnp.where(lane < heads, mask_score, 0.0).astype(jnp.float32)

    request = sreq_ref[step]
    kind = skind_ref[step]
    limit = slim_ref[step]
    scale = 1.0 / math.sqrt(head_dim)

    def attend(k_ref, v_ref, masked):
        base = pl.multiple_of(request * span, span)
        if masked:
            rows = lax.broadcasted_iota(jnp.int32, (span, PAGE), 0)
            cols = lax.broadcasted_iota(jnp.int32, (span, PAGE), 1)
            allowed = rows - cols >= limit
        lane = lax.broadcasted_iota(jnp.int32, (span, lanes), 1)
        ml = ml_ref[pl.ds(base, span), :]
        for h in range(heads):
            cut = slice(h * head_dim, (h + 1) * head_dim)
            q_h = q_ref[0, pl.ds(base, span), cut]
            k_h = k_ref[0, :, cut]
            v_h = v_ref[0, :, cut]
            scores = lax.dot_general(
                q_h, k_h, (((1,), (1,)), ((), ())), preferred_element_type=jnp.float32
            ) * scale
            if masked:
                scores = jnp.where(allowed, scores, mask_score)
            m_prev = ml[:, h : h + 1]
            l_prev = ml[:, heads + h : heads + h + 1]
            m_new = jnp.maximum(m_prev, jnp.max(scores, axis=1, keepdims=True))
            m_new = m_new.astype(jnp.bfloat16).astype(jnp.float32)
            alpha = jnp.exp(m_prev - m_new)
            weights = jnp.exp(scores - m_new)
            if masked:
                weights = jnp.where(allowed, weights, 0.0)
            l_new = alpha * l_prev + jnp.sum(weights, axis=1, keepdims=True)
            contrib = jnp.dot(
                weights.astype(jnp.bfloat16), v_h, preferred_element_type=jnp.float32
            )
            acc_ref[pl.ds(base, span), cut] = alpha * acc_ref[pl.ds(base, span), cut] + contrib
            ml = jnp.where(
                lane == h,
                m_new,
                jnp.where((lane == heads + h) | (lane == 2 * heads + h), l_new, ml),
            )
        ml_ref[pl.ds(base, span), :] = ml

    @pl.when(kind == 1)
    def _cached():
        attend(kc_ref, vc_ref, False)

    @pl.when(kind == 2)
    def _fresh():
        attend(kf_ref, vf_ref, True)

    @pl.when(kind == 2)
    def _store_fresh():
        ko_ref[...] = kf_ref[...]
        vo_ref[...] = vf_ref[...]

    @pl.when(kind != 2)
    def _store_cached():
        ko_ref[...] = kc_ref[...]
        vo_ref[...] = vc_ref[...]

    @pl.when(step == pl.num_programs(0) - 1)
    def _emit():
        chunks, rows_per, _ = out_ref.shape
        lane = lax.broadcasted_iota(jnp.int32, (rows_per, lanes), 1)
        for d in range(chunks):
            rows = pl.ds(d * rows_per, rows_per)
            out_ref[d, :, :width] = acc_ref[rows, :].astype(jnp.bfloat16)
            ml = ml_ref[rows, :]
            rounded = ml.astype(jnp.bfloat16).astype(jnp.float32)
            packed = jnp.where(
                lane < 2 * heads,
                rounded,
                jnp.where(lane < 3 * heads, ml - rounded, 0.0),
            )
            out_ref[d, :, width:] = packed.astype(jnp.bfloat16)


def local_attention(slot_request, slot_kind, slot_limit, slot_fresh, gathered, kc, vc,
                    heads, head_dim, requests, span, chunks):
    _, tokens, width = gathered.shape
    slot_count = kc.shape[0]
    rows_per = tokens // chunks
    kernel = functools.partial(attend_kernel, heads, head_dim, requests, span)
    flops = 4 * slot_count * span * PAGE * width
    return pl.pallas_call(
        kernel,
        out_shape=(
            jax.ShapeDtypeStruct((chunks, rows_per, width + 128), jnp.bfloat16),
            jax.ShapeDtypeStruct(kc.shape, kc.dtype),
            jax.ShapeDtypeStruct(vc.shape, vc.dtype),
        ),
        grid_spec=pltpu.PrefetchScalarGridSpec(
            num_scalar_prefetch=4,
            grid=(slot_count,),
            in_specs=[
                pl.BlockSpec((1, tokens, width), lambda s, *_: (0, 0, 0),
                             pipeline_mode=pl.Buffered(1)),
                pl.BlockSpec((1, PAGE, width), lambda s, rq, kd, lm, fr: (1, fr[s], 0)),
                pl.BlockSpec((1, PAGE, width), lambda s, rq, kd, lm, fr: (2, fr[s], 0)),
                pl.BlockSpec((1, PAGE, width), lambda s, *_: (s, 0, 0)),
                pl.BlockSpec((1, PAGE, width), lambda s, *_: (s, 0, 0)),
            ],
            out_specs=[
                pl.BlockSpec((chunks, rows_per, width + 128), lambda s, *_: (0, 0, 0)),
                pl.BlockSpec((1, PAGE, width), lambda s, *_: (s, 0, 0)),
                pl.BlockSpec((1, PAGE, width), lambda s, *_: (s, 0, 0)),
            ],
            scratch_shapes=[
                pltpu.VMEM((tokens, width), jnp.float32),
                pltpu.VMEM((tokens, 128), jnp.float32),
            ],
        ),
        compiler_params=pltpu.CompilerParams(
            dimension_semantics=("arbitrary",), vmem_limit_bytes=60 * 1024 * 1024
        ),
        cost_estimate=pl.CostEstimate(
            flops=flops,
            transcendentals=slot_count * span * PAGE * heads,
            bytes_accessed=tokens * width * 2 + 4 * kc.size * 2 + tokens * (width + 128) * 2,
        ),
    )(slot_request, slot_kind, slot_limit, slot_fresh, gathered, gathered, gathered, kc, vc)


def combine_kernel(heads, head_dim, recv_ref, w_ref, out_ref, o_acc, l_acc):
    chunks, rows_per, _ = recv_ref.shape
    width = heads * head_dim
    lanes = 128

    def peak_step(d, peak):
        return jnp.maximum(peak, recv_ref[d, :, width:].astype(jnp.float32))

    peak = lax.fori_loop(
        0, chunks, peak_step, jnp.full((rows_per, lanes), mask_score, jnp.float32)
    )
    o_acc[...] = jnp.zeros_like(o_acc)
    l_acc[...] = jnp.zeros_like(l_acc)

    def sum_step(d, carry):
        mld = recv_ref[d, :, width:].astype(jnp.float32)
        factor = jnp.exp(mld - peak)
        for h in range(heads):
            f_h = factor[:, h : h + 1]
            l_h = mld[:, heads + h : heads + h + 1] + mld[:, 2 * heads + h : 2 * heads + h + 1]
            l_acc[:, h : h + 1] += f_h * l_h
            cut = slice(h * head_dim, (h + 1) * head_dim)
            o_acc[:, cut] += f_h * recv_ref[d, :, cut].astype(jnp.float32)
        return carry

    lax.fori_loop(0, chunks, sum_step, 0)
    parts = []
    for h in range(heads):
        cut = slice(h * head_dim, (h + 1) * head_dim)
        parts.append((o_acc[:, cut] / l_acc[:, h : h + 1]).astype(jnp.bfloat16))
    attended = jnp.concatenate(parts, axis=1)
    out_ref[...] = lax.dot_general(
        attended, w_ref[0], (((1,), (1,)), ((), ())), preferred_element_type=jnp.float32
    ).astype(out_ref.dtype)


def combine_project(received, gathered, heads, head_dim):
    chunks, rows_per, _ = received.shape
    _, tokens, width = gathered.shape
    kernel = functools.partial(combine_kernel, heads, head_dim)
    return pl.pallas_call(
        kernel,
        out_shape=jax.ShapeDtypeStruct((rows_per, tokens), jnp.bfloat16),
        grid=(1,),
        in_specs=[
            pl.BlockSpec(received.shape, lambda i: (0, 0, 0)),
            pl.BlockSpec((1, tokens, width), lambda i: (3, 0, 0)),
        ],
        out_specs=pl.BlockSpec((rows_per, tokens), lambda i: (0, 0)),
        scratch_shapes=[
            pltpu.VMEM((rows_per, width), jnp.float32),
            pltpu.VMEM((rows_per, 128), jnp.float32),
        ],
        compiler_params=pltpu.CompilerParams(vmem_limit_bytes=48 * 1024 * 1024),
        cost_estimate=pl.CostEstimate(
            flops=2 * rows_per * tokens * width + 4 * received.size,
            transcendentals=chunks * rows_per * 128,
            bytes_accessed=received.size * 2 + tokens * width * 2 + rows_per * tokens * 2,
        ),
    )(received, gathered)


def pair_merge_kernel(heads, head_dim, packed_hbm, out_ref, mine, theirs, local_sem, send_sem, recv_sem):
    core = lax.axis_index("core")
    partner = 1 - core
    width = heads * head_dim
    lanes = 128
    chunks, rows_per, _ = out_ref.shape

    barrier = pltpu.get_barrier_semaphore()
    pl.semaphore_signal(barrier, inc=1, device_id={"core": partner}, device_id_type=pl.DeviceIdType.MESH)
    pl.semaphore_wait(barrier, 1)

    local = pltpu.make_async_copy(packed_hbm.at[:, core], mine, local_sem)
    local.start()
    remote = pltpu.make_async_remote_copy(
        src_ref=packed_hbm.at[:, partner],
        dst_ref=theirs,
        send_sem=send_sem,
        recv_sem=recv_sem,
        device_id={"core": partner},
        device_id_type=pl.DeviceIdType.MESH,
    )
    remote.start()
    local.wait()
    remote.wait()

    lane = lax.broadcasted_iota(jnp.int32, (rows_per, lanes), 1)

    def merge_step(c, carry):
        ml_a = mine[c, :, width:].astype(jnp.float32)
        ml_b = theirs[c, :, width:].astype(jnp.float32)
        peak = jnp.maximum(ml_a, ml_b)
        f_a = jnp.exp(ml_a - peak)
        f_b = jnp.exp(ml_b - peak)
        merged = jnp.zeros((rows_per, lanes), jnp.float32)
        for h in range(heads):
            cut = slice(h * head_dim, (h + 1) * head_dim)
            fa_h = f_a[:, h : h + 1]
            fb_h = f_b[:, h : h + 1]
            out_ref[c, :, cut] = (
                fa_h * mine[c, :, cut].astype(jnp.float32)
                + fb_h * theirs[c, :, cut].astype(jnp.float32)
            ).astype(out_ref.dtype)
            l_a = ml_a[:, heads + h : heads + h + 1] + ml_a[:, 2 * heads + h : 2 * heads + h + 1]
            l_b = ml_b[:, heads + h : heads + h + 1] + ml_b[:, 2 * heads + h : 2 * heads + h + 1]
            l_h = fa_h * l_a + fb_h * l_b
            l_hi = l_h.astype(jnp.bfloat16).astype(jnp.float32)
            merged = jnp.where(
                lane == h,
                peak[:, h : h + 1],
                jnp.where(
                    lane == heads + h,
                    l_hi,
                    jnp.where(lane == 2 * heads + h, l_h - l_hi, merged),
                ),
            )
        out_ref[c, :, width:] = merged.astype(out_ref.dtype)
        return carry

    lax.fori_loop(0, chunks, merge_step, 0)


def pair_merge(packed, heads, head_dim):
    devices, rows_per, lanes_all = packed.shape
    chips = devices // 2
    view = packed.reshape(chips, 2, rows_per, lanes_all)
    kernel = functools.partial(pair_merge_kernel, heads, head_dim)
    return pl.pallas_call(
        kernel,
        out_shape=jax.ShapeDtypeStruct((chips, rows_per, lanes_all), packed.dtype),
        in_specs=[pl.BlockSpec(memory_space=pl.ANY)],
        out_specs=pl.BlockSpec(memory_space=pltpu.VMEM),
        scratch_shapes=[
            pltpu.VMEM((chips, rows_per, lanes_all), packed.dtype),
            pltpu.VMEM((chips, rows_per, lanes_all), packed.dtype),
            pltpu.SemaphoreType.DMA(()),
            pltpu.SemaphoreType.DMA(()),
            pltpu.SemaphoreType.DMA(()),
        ],
        compiler_params=pltpu.CompilerParams(
            collective_id=0, has_side_effects=True, vmem_limit_bytes=40 * 1024 * 1024
        ),
        cost_estimate=pl.CostEstimate(
            flops=6 * chips * rows_per * lanes_all,
            transcendentals=2 * chips * rows_per * 128,
            bytes_accessed=3 * chips * rows_per * lanes_all * 2,
        ),
    )(view)


def per_device(
    queries,
    keys,
    values,
    key_cache,
    value_cache,
    cache_len,
    page_table,
    append_slots,
    out_weight,
    out_bias,
):
    tok_dev, head_count, head_dim = queries.shape
    width = head_count * head_dim
    requests = cache_len.shape[0]
    max_pages = page_table.shape[1]
    new_pages = append_slots.shape[1]
    span_len = new_pages * PAGE
    slot_count = key_cache.shape[0]
    page_devices = lax.axis_size(PAGES)
    device_at = lax.axis_index(PAGES)
    token_ids = device_at * tok_dev + jnp.arange(tok_dev, dtype=jnp.int32)
    request_ids = token_ids // span_len
    request_grid = jnp.arange(requests, dtype=jnp.int32)
    starts = jnp.sum(
        jnp.where(request_ids[:, None] == request_grid[None, :], cache_len[None, :], 0), axis=1
    )
    positions = (starts + token_ids % span_len).astype(jnp.float32)
    rotated_q = rotate(queries.astype(jnp.float32), positions).astype(jnp.bfloat16)
    rotated_k = rotate(keys.astype(jnp.float32), positions).astype(jnp.bfloat16)
    w_cols = out_weight.shape[1]
    w_plane = jnp.pad(out_weight.T, ((0, tok_dev - w_cols), (0, 0)))
    stacked = jnp.stack(
        [
            rotated_q.reshape(tok_dev, width),
            rotated_k.reshape(tok_dev, width),
            values.reshape(tok_dev, width),
            w_plane,
        ]
    )
    gathered = lax.all_gather(stacked, PAGES, axis=1, tiled=True)
    my_slots = device_at * slot_count + jnp.arange(slot_count, dtype=jnp.int32)
    cached_hit = page_table.reshape(-1)[None, :] == my_slots[:, None]
    fresh_hit = append_slots.reshape(-1)[None, :] == my_slots[:, None]
    is_cached = jnp.any(cached_hit, axis=1)
    is_fresh = jnp.any(fresh_hit, axis=1)
    cached_index = jnp.sum(
        jnp.where(cached_hit, jnp.arange(requests * max_pages, dtype=jnp.int32)[None, :], 0), axis=1
    )
    fresh_index = jnp.sum(
        jnp.where(fresh_hit, jnp.arange(requests * new_pages, dtype=jnp.int32)[None, :], 0), axis=1
    )
    slot_request = jnp.where(is_fresh, fresh_index // new_pages, cached_index // max_pages)
    slot_page = jnp.where(is_fresh, fresh_index % new_pages, cached_index % max_pages)
    slot_length = jnp.sum(
        jnp.where(slot_request[:, None] == request_grid[None, :], cache_len[None, :], 0), axis=1
    )
    visible = is_cached & (slot_page * PAGE < slot_length)
    slot_kind = jnp.where(is_fresh, 2, jnp.where(visible, 1, 0)).astype(jnp.int32)
    slot_limit = jnp.where(is_fresh, slot_page * PAGE, -4 * span_len)
    packed, key_slots, value_slots = local_attention(
        slot_request,
        slot_kind,
        slot_limit,
        fresh_index,
        gathered,
        key_cache.reshape(slot_count, PAGE, width),
        value_cache.reshape(slot_count, PAGE, width),
        head_count,
        head_dim,
        requests,
        span_len,
        page_devices,
    )
    paired = pair_merge(packed, head_count, head_dim)
    received = lax.all_to_all(paired, "chips", 0, 0, tiled=True)
    projected = combine_project(received, gathered, head_count, head_dim)
    projected = projected.reshape(tok_dev, page_devices, tok_dev)[:, :, :w_cols].reshape(
        tok_dev, page_devices * w_cols
    )
    key_out = key_slots.reshape(key_cache.shape)
    value_out = value_slots.reshape(value_cache.shape)
    summed = lax.psum_scatter(projected, "heads", scatter_dimension=1, tiled=True).astype(jnp.float32)
    hidden = (summed + out_bias[None, :]).astype(jnp.bfloat16)
    return (hidden, key_out, value_out)


def solution(mesh):
    heads_n, pages_n = mesh.devices.shape
    split = jax.sharding.Mesh(
        mesh.devices.reshape(heads_n, pages_n // 2, 2), ("heads", "chips", "core")
    )
    placed = (
        P(PAGES, "heads", None),
        P(PAGES, "heads", None),
        P(PAGES, "heads", None),
        P(PAGES, None, "heads", None),
        P(PAGES, None, "heads", None),
        P(),
        P(),
        P(),
        P("heads", PAGES),
        P("heads"),
    )
    return jax.shard_map(
        per_device,
        mesh=split,
        in_specs=placed,
        out_specs=(
            P(PAGES, "heads"),
            P(PAGES, None, "heads", None),
            P(PAGES, None, "heads", None),
        ),
        check_vma=False,
    )
```

```python
import functools
import math

import jax
import jax.numpy as jnp
from jax import lax
from jax.experimental import pallas as pl
from jax.experimental.pallas import tpu as pltpu
from jax.sharding import PartitionSpec as P

ROT = 32
PAGE = 128
PAGES = ("chips", "core")


low_score = -1e30
mask_score = -(2.0 ** 100)


def rotate(vectors, positions):
    half_rot = ROT // 2
    inv_freq = 10000.0 ** (-2.0 * jnp.arange(half_rot, dtype=jnp.float32) / ROT)
    angles = positions[:, None] * inv_freq[None, :]
    cosine = jnp.cos(angles)[:, None, :]
    sine = jnp.sin(angles)[:, None, :]
    first_half = vectors[..., :half_rot]
    second_half = vectors[..., half_rot:ROT]
    return jnp.concatenate(
        [
            first_half * cosine - second_half * sine,
            second_half * cosine + first_half * sine,
            vectors[..., ROT:],
        ],
        axis=-1,
    )


def attend_kernel(
    heads, head_dim, requests, span,
    sreq_ref, skind_ref, slim_ref, sfresh_ref,
    q_ref, kf_ref, vf_ref, kc_ref, vc_ref,
    out_ref, ko_ref, vo_ref, acc_t, stats, tok_ref, ml_ref,
):
    step = pl.program_id(0)
    lanes = ml_ref.shape[1]
    width = heads * head_dim

    @pl.when(step == 0)
    def _init():
        acc_t[...] = jnp.zeros_like(acc_t)
        row = lax.broadcasted_iota(jnp.int32, stats.shape, 1)
        stats[...] = jnp.where(row < heads, mask_score, 0.0).astype(jnp.float32)

    request = sreq_ref[step]
    kind = skind_ref[step]
    limit = slim_ref[step]
    scale = 1.0 / math.sqrt(head_dim)

    def attend(k_ref, v_ref, masked):
        base = pl.multiple_of(request * span, span)
        if masked:
            keys_at = lax.broadcasted_iota(jnp.int32, (PAGE, span), 0)
            queries_at = lax.broadcasted_iota(jnp.int32, (PAGE, span), 1)
            allowed = queries_at - keys_at >= limit
        v_t = v_ref[0].astype(jnp.float32).T.astype(jnp.bfloat16)
        for h in range(heads):
            cut = slice(h * head_dim, (h + 1) * head_dim)
            q_h = q_ref[0, pl.ds(base, span), cut]
            k_h = k_ref[0, :, cut]
            scores = lax.dot_general(
                k_h, q_h, (((1,), (1,)), ((), ())), preferred_element_type=jnp.float32
            ) * scale
            if masked:
                scores = jnp.where(allowed, scores, mask_score)
            m_prev = stats[request, h : h + 1, :]
            l_prev = stats[request, heads + h : heads + h + 1, :]
            m_new = jnp.maximum(m_prev, jnp.max(scores, axis=0, keepdims=True))
            m_new = m_new.astype(jnp.bfloat16).astype(jnp.float32)
            alpha = jnp.exp(m_prev - m_new)
            weights = jnp.exp(scores - m_new)
            if masked:
                weights = jnp.where(allowed, weights, 0.0)
            l_new = alpha * l_prev + jnp.sum(weights, axis=0, keepdims=True)
            contrib = jnp.dot(
                v_t[cut, :], weights.astype(jnp.bfloat16), preferred_element_type=jnp.float32
            )
            slot = request * heads + h
            acc_t[slot] = alpha * acc_t[slot] + contrib
            stats[request, h : h + 1, :] = m_new
            stats[request, heads + h : heads + h + 1, :] = l_new
            stats[request, 2 * heads + h : 2 * heads + h + 1, :] = l_new

    @pl.when(kind == 1)
    def _cached():
        attend(kc_ref, vc_ref, False)

    @pl.when(kind == 2)
    def _fresh():
        attend(kf_ref, vf_ref, True)

    @pl.when(kind == 2)
    def _store_fresh():
        ko_ref[...] = kf_ref[...]
        vo_ref[...] = vf_ref[...]

    @pl.when(kind != 2)
    def _store_cached():
        ko_ref[...] = kc_ref[...]
        vo_ref[...] = vc_ref[...]

    @pl.when(step == pl.num_programs(0) - 1)
    def _emit():
        stat_rows = stats.shape[1]
        for r in range(requests):
            rows = pl.ds(r * span, span)
            for h in range(heads):
                tok_ref[rows, h * head_dim : (h + 1) * head_dim] = acc_t[r * heads + h].T
            block = jnp.concatenate(
                [stats[r], jnp.zeros((lanes - stat_rows, span), jnp.float32)], axis=0
            )
            ml_ref[rows, :] = block.T
        chunks, rows_per, _ = out_ref.shape
        lane = lax.broadcasted_iota(jnp.int32, (rows_per, lanes), 1)
        for d in range(chunks):
            rows = pl.ds(d * rows_per, rows_per)
            out_ref[d, :, :width] = tok_ref[rows, :].astype(jnp.bfloat16)
            ml = ml_ref[rows, :]
            rounded = ml.astype(jnp.bfloat16).astype(jnp.float32)
            packed = jnp.where(
                lane < 2 * heads,
                rounded,
                jnp.where(lane < 3 * heads, ml - rounded, 0.0),
            )
            out_ref[d, :, width:] = packed.astype(jnp.bfloat16)


def local_attention(slot_request, slot_kind, slot_limit, slot_fresh, gathered, kc, vc,
                    heads, head_dim, requests, span, chunks):
    _, tokens, width = gathered.shape
    slot_count = kc.shape[0]
    rows_per = tokens // chunks
    kernel = functools.partial(attend_kernel, heads, head_dim, requests, span)
    flops = 4 * slot_count * span * PAGE * width
    return pl.pallas_call(
        kernel,
        out_shape=(
            jax.ShapeDtypeStruct((chunks, rows_per, width + 128), jnp.bfloat16),
            jax.ShapeDtypeStruct(kc.shape, kc.dtype),
            jax.ShapeDtypeStruct(vc.shape, vc.dtype),
        ),
        grid_spec=pltpu.PrefetchScalarGridSpec(
            num_scalar_prefetch=4,
            grid=(slot_count,),
            in_specs=[
                pl.BlockSpec((1, tokens, width), lambda s, *_: (0, 0, 0),
                             pipeline_mode=pl.Buffered(1)),
                pl.BlockSpec((1, PAGE, width), lambda s, rq, kd, lm, fr: (1, fr[s], 0)),
                pl.BlockSpec((1, PAGE, width), lambda s, rq, kd, lm, fr: (2, fr[s], 0)),
                pl.BlockSpec((1, PAGE, width), lambda s, *_: (s, 0, 0)),
                pl.BlockSpec((1, PAGE, width), lambda s, *_: (s, 0, 0)),
            ],
            out_specs=[
                pl.BlockSpec((chunks, rows_per, width + 128), lambda s, *_: (0, 0, 0)),
                pl.BlockSpec((1, PAGE, width), lambda s, *_: (s, 0, 0)),
                pl.BlockSpec((1, PAGE, width), lambda s, *_: (s, 0, 0)),
            ],
            scratch_shapes=[
                pltpu.VMEM((requests * heads, head_dim, span), jnp.float32),
                pltpu.VMEM((requests, 16, span), jnp.float32),
                pltpu.VMEM((tokens, width), jnp.float32),
                pltpu.VMEM((tokens, 128), jnp.float32),
            ],
        ),
        compiler_params=pltpu.CompilerParams(
            dimension_semantics=("arbitrary",), vmem_limit_bytes=62 * 1024 * 1024
        ),
        cost_estimate=pl.CostEstimate(
            flops=flops,
            transcendentals=slot_count * span * PAGE * heads,
            bytes_accessed=tokens * width * 2 + 4 * kc.size * 2 + tokens * (width + 128) * 2,
        ),
    )(slot_request, slot_kind, slot_limit, slot_fresh, gathered, gathered, gathered, kc, vc)


def combine_kernel(heads, head_dim, recv_ref, w_ref, out_ref, o_acc, l_acc):
    chunks, rows_per, _ = recv_ref.shape
    width = heads * head_dim
    lanes = 128

    def peak_step(d, peak):
        return jnp.maximum(peak, recv_ref[d, :, width:].astype(jnp.float32))

    peak = lax.fori_loop(
        0, chunks, peak_step, jnp.full((rows_per, lanes), mask_score, jnp.float32)
    )
    o_acc[...] = jnp.zeros_like(o_acc)
    l_acc[...] = jnp.zeros_like(l_acc)

    def sum_step(d, carry):
        mld = recv_ref[d, :, width:].astype(jnp.float32)
        factor = jnp.exp(mld - peak)
        for h in range(heads):
            f_h = factor[:, h : h + 1]
            l_h = mld[:, heads + h : heads + h + 1] + mld[:, 2 * heads + h : 2 * heads + h + 1]
            l_acc[:, h : h + 1] += f_h * l_h
            cut = slice(h * head_dim, (h + 1) * head_dim)
            o_acc[:, cut] += f_h * recv_ref[d, :, cut].astype(jnp.float32)
        return carry

    lax.fori_loop(0, chunks, sum_step, 0)
    parts = []
    for h in range(heads):
        cut = slice(h * head_dim, (h + 1) * head_dim)
        parts.append((o_acc[:, cut] / l_acc[:, h : h + 1]).astype(jnp.bfloat16))
    attended = jnp.concatenate(parts, axis=1)
    out_ref[...] = lax.dot_general(
        attended, w_ref[0], (((1,), (1,)), ((), ())), preferred_element_type=jnp.float32
    ).astype(out_ref.dtype)


def combine_project(received, gathered, heads, head_dim):
    chunks, rows_per, _ = received.shape
    _, tokens, width = gathered.shape
    kernel = functools.partial(combine_kernel, heads, head_dim)
    return pl.pallas_call(
        kernel,
        out_shape=jax.ShapeDtypeStruct((rows_per, tokens), jnp.bfloat16),
        grid=(1,),
        in_specs=[
            pl.BlockSpec(received.shape, lambda i: (0, 0, 0)),
            pl.BlockSpec((1, tokens, width), lambda i: (3, 0, 0)),
        ],
        out_specs=pl.BlockSpec((rows_per, tokens), lambda i: (0, 0)),
        scratch_shapes=[
            pltpu.VMEM((rows_per, width), jnp.float32),
            pltpu.VMEM((rows_per, 128), jnp.float32),
        ],
        compiler_params=pltpu.CompilerParams(vmem_limit_bytes=48 * 1024 * 1024),
        cost_estimate=pl.CostEstimate(
            flops=2 * rows_per * tokens * width + 4 * received.size,
            transcendentals=chunks * rows_per * 128,
            bytes_accessed=received.size * 2 + tokens * width * 2 + rows_per * tokens * 2,
        ),
    )(received, gathered)


def pair_merge_kernel(heads, head_dim, packed_hbm, out_ref, mine, theirs, local_sem, send_sem, recv_sem):
    core = lax.axis_index("core")
    partner = 1 - core
    width = heads * head_dim
    lanes = 128
    chunks, rows_per, _ = out_ref.shape

    barrier = pltpu.get_barrier_semaphore()
    pl.semaphore_signal(barrier, inc=1, device_id={"core": partner}, device_id_type=pl.DeviceIdType.MESH)
    pl.semaphore_wait(barrier, 1)

    local = pltpu.make_async_copy(packed_hbm.at[:, core], mine, local_sem)
    local.start()
    remote = pltpu.make_async_remote_copy(
        src_ref=packed_hbm.at[:, partner],
        dst_ref=theirs,
        send_sem=send_sem,
        recv_sem=recv_sem,
        device_id={"core": partner},
        device_id_type=pl.DeviceIdType.MESH,
    )
    remote.start()
    local.wait()
    remote.wait()

    lane = lax.broadcasted_iota(jnp.int32, (rows_per, lanes), 1)

    def merge_step(c, carry):
        ml_a = mine[c, :, width:].astype(jnp.float32)
        ml_b = theirs[c, :, width:].astype(jnp.float32)
        peak = jnp.maximum(ml_a, ml_b)
        f_a = jnp.exp(ml_a - peak)
        f_b = jnp.exp(ml_b - peak)
        merged = jnp.zeros((rows_per, lanes), jnp.float32)
        for h in range(heads):
            cut = slice(h * head_dim, (h + 1) * head_dim)
            fa_h = f_a[:, h : h + 1]
            fb_h = f_b[:, h : h + 1]
            out_ref[c, :, cut] = (
                fa_h * mine[c, :, cut].astype(jnp.float32)
                + fb_h * theirs[c, :, cut].astype(jnp.float32)
            ).astype(out_ref.dtype)
            l_a = ml_a[:, heads + h : heads + h + 1] + ml_a[:, 2 * heads + h : 2 * heads + h + 1]
            l_b = ml_b[:, heads + h : heads + h + 1] + ml_b[:, 2 * heads + h : 2 * heads + h + 1]
            l_h = fa_h * l_a + fb_h * l_b
            l_hi = l_h.astype(jnp.bfloat16).astype(jnp.float32)
            merged = jnp.where(
                lane == h,
                peak[:, h : h + 1],
                jnp.where(
                    lane == heads + h,
                    l_hi,
                    jnp.where(lane == 2 * heads + h, l_h - l_hi, merged),
                ),
            )
        out_ref[c, :, width:] = merged.astype(out_ref.dtype)
        return carry

    lax.fori_loop(0, chunks, merge_step, 0)


def pair_merge(packed, heads, head_dim):
    devices, rows_per, lanes_all = packed.shape
    chips = devices // 2
    view = packed.reshape(chips, 2, rows_per, lanes_all)
    kernel = functools.partial(pair_merge_kernel, heads, head_dim)
    return pl.pallas_call(
        kernel,
        out_shape=jax.ShapeDtypeStruct((chips, rows_per, lanes_all), packed.dtype),
        in_specs=[pl.BlockSpec(memory_space=pl.ANY)],
        out_specs=pl.BlockSpec(memory_space=pltpu.VMEM),
        scratch_shapes=[
            pltpu.VMEM((chips, rows_per, lanes_all), packed.dtype),
            pltpu.VMEM((chips, rows_per, lanes_all), packed.dtype),
            pltpu.SemaphoreType.DMA(()),
            pltpu.SemaphoreType.DMA(()),
            pltpu.SemaphoreType.DMA(()),
        ],
        compiler_params=pltpu.CompilerParams(
            collective_id=0, has_side_effects=True, vmem_limit_bytes=40 * 1024 * 1024
        ),
        cost_estimate=pl.CostEstimate(
            flops=6 * chips * rows_per * lanes_all,
            transcendentals=2 * chips * rows_per * 128,
            bytes_accessed=3 * chips * rows_per * lanes_all * 2,
        ),
    )(view)


def per_device(
    queries,
    keys,
    values,
    key_cache,
    value_cache,
    cache_len,
    page_table,
    append_slots,
    out_weight,
    out_bias,
):
    tok_dev, head_count, head_dim = queries.shape
    width = head_count * head_dim
    requests = cache_len.shape[0]
    max_pages = page_table.shape[1]
    new_pages = append_slots.shape[1]
    span_len = new_pages * PAGE
    slot_count = key_cache.shape[0]
    page_devices = lax.axis_size(PAGES)
    device_at = lax.axis_index(PAGES)
    token_ids = device_at * tok_dev + jnp.arange(tok_dev, dtype=jnp.int32)
    request_ids = token_ids // span_len
    request_grid = jnp.arange(requests, dtype=jnp.int32)
    starts = jnp.sum(
        jnp.where(request_ids[:, None] == request_grid[None, :], cache_len[None, :], 0), axis=1
    )
    positions = (starts + token_ids % span_len).astype(jnp.float32)
    rotated_q = rotate(queries.astype(jnp.float32), positions).astype(jnp.bfloat16)
    rotated_k = rotate(keys.astype(jnp.float32), positions).astype(jnp.bfloat16)
    w_cols = out_weight.shape[1]
    w_plane = jnp.pad(out_weight.T, ((0, tok_dev - w_cols), (0, 0)))
    stacked = jnp.stack(
        [
            rotated_q.reshape(tok_dev, width),
            rotated_k.reshape(tok_dev, width),
            values.reshape(tok_dev, width),
            w_plane,
        ]
    )
    gathered = lax.all_gather(stacked, PAGES, axis=1, tiled=True)
    my_slots = device_at * slot_count + jnp.arange(slot_count, dtype=jnp.int32)
    cached_hit = page_table.reshape(-1)[None, :] == my_slots[:, None]
    fresh_hit = append_slots.reshape(-1)[None, :] == my_slots[:, None]
    is_cached = jnp.any(cached_hit, axis=1)
    is_fresh = jnp.any(fresh_hit, axis=1)
    cached_index = jnp.sum(
        jnp.where(cached_hit, jnp.arange(requests * max_pages, dtype=jnp.int32)[None, :], 0), axis=1
    )
    fresh_index = jnp.sum(
        jnp.where(fresh_hit, jnp.arange(requests * new_pages, dtype=jnp.int32)[None, :], 0), axis=1
    )
    slot_request = jnp.where(is_fresh, fresh_index // new_pages, cached_index // max_pages)
    slot_page = jnp.where(is_fresh, fresh_index % new_pages, cached_index % max_pages)
    slot_length = jnp.sum(
        jnp.where(slot_request[:, None] == request_grid[None, :], cache_len[None, :], 0), axis=1
    )
    visible = is_cached & (slot_page * PAGE < slot_length)
    slot_kind = jnp.where(is_fresh, 2, jnp.where(visible, 1, 0)).astype(jnp.int32)
    slot_limit = jnp.where(is_fresh, slot_page * PAGE, -4 * span_len)
    packed, key_slots, value_slots = local_attention(
        slot_request,
        slot_kind,
        slot_limit,
        fresh_index,
        gathered,
        key_cache.reshape(slot_count, PAGE, width),
        value_cache.reshape(slot_count, PAGE, width),
        head_count,
        head_dim,
        requests,
        span_len,
        page_devices,
    )
    paired = pair_merge(packed, head_count, head_dim)
    received = lax.all_to_all(paired, "chips", 0, 0, tiled=True)
    projected = combine_project(received, gathered, head_count, head_dim)
    projected = projected.reshape(tok_dev, page_devices, tok_dev)[:, :, :w_cols].reshape(
        tok_dev, page_devices * w_cols
    )
    key_out = key_slots.reshape(key_cache.shape)
    value_out = value_slots.reshape(value_cache.shape)
    summed = lax.psum_scatter(projected, "heads", scatter_dimension=1, tiled=True).astype(jnp.float32)
    hidden = (summed + out_bias[None, :]).astype(jnp.bfloat16)
    return (hidden, key_out, value_out)


def solution(mesh):
    heads_n, pages_n = mesh.devices.shape
    split = jax.sharding.Mesh(
        mesh.devices.reshape(heads_n, pages_n // 2, 2), ("heads", "chips", "core")
    )
    placed = (
        P(PAGES, "heads", None),
        P(PAGES, "heads", None),
        P(PAGES, "heads", None),
        P(PAGES, None, "heads", None),
        P(PAGES, None, "heads", None),
        P(),
        P(),
        P(),
        P("heads", PAGES),
        P("heads"),
    )
    return jax.shard_map(
        per_device,
        mesh=split,
        in_specs=placed,
        out_specs=(
            P(PAGES, "heads"),
            P(PAGES, None, "heads", None),
            P(PAGES, None, "heads", None),
        ),
        check_vma=False,
    )
```

```python
import functools
import math

import jax
import jax.numpy as jnp
from jax import lax
from jax.experimental import pallas as pl
from jax.experimental.pallas import tpu as pltpu
from jax.sharding import PartitionSpec as P

ROT = 32
PAGE = 128
PAGES = ("chips", "core")


low_score = -1e30
mask_score = -(2.0 ** 100)


def rotate(vectors, positions):
    half_rot = ROT // 2
    inv_freq = 10000.0 ** (-2.0 * jnp.arange(half_rot, dtype=jnp.float32) / ROT)
    angles = positions[:, None] * inv_freq[None, :]
    cosine = jnp.cos(angles)[:, None, :]
    sine = jnp.sin(angles)[:, None, :]
    first_half = vectors[..., :half_rot]
    second_half = vectors[..., half_rot:ROT]
    return jnp.concatenate(
        [
            first_half * cosine - second_half * sine,
            second_half * cosine + first_half * sine,
            vectors[..., ROT:],
        ],
        axis=-1,
    )


def attend_kernel(
    heads, head_dim, requests, span,
    sreq_ref, skind_ref, slim_ref, sfresh_ref,
    q_ref, kf_ref, vf_ref, kc_ref, vc_ref,
    out_ref, ko_ref, vo_ref, acc_t, stats, tok_ref, ml_ref,
):
    step = pl.program_id(0)
    lanes = ml_ref.shape[1]
    width = heads * head_dim

    @pl.when(step == 0)
    def _init():
        acc_t[...] = jnp.zeros_like(acc_t)
        row = lax.broadcasted_iota(jnp.int32, stats.shape, 1)
        stats[...] = jnp.where(row < heads, mask_score, 0.0).astype(jnp.float32)

    request = sreq_ref[step]
    kind = skind_ref[step]
    limit = slim_ref[step]
    scale = 1.0 / math.sqrt(head_dim)

    def attend(k_ref, v_ref, masked):
        base = pl.multiple_of(request * span, span)
        if masked:
            keys_at = lax.broadcasted_iota(jnp.int32, (PAGE, span), 0)
            queries_at = lax.broadcasted_iota(jnp.int32, (PAGE, span), 1)
            allowed = queries_at - keys_at >= limit
        v_t = v_ref[0].astype(jnp.float32).T.astype(jnp.bfloat16)
        for h in range(heads):
            cut = slice(h * head_dim, (h + 1) * head_dim)
            q_h = q_ref[0, pl.ds(base, span), cut]
            k_h = k_ref[0, :, cut]
            scores = lax.dot_general(
                k_h, q_h, (((1,), (1,)), ((), ())), preferred_element_type=jnp.float32
            ) * scale
            if masked:
                scores = jnp.where(allowed, scores, mask_score)
            m_prev = stats[request, h : h + 1, :]
            l_prev = stats[request, heads + h : heads + h + 1, :]
            m_new = jnp.maximum(m_prev, jnp.max(scores, axis=0, keepdims=True))
            m_new = m_new.astype(jnp.bfloat16).astype(jnp.float32)
            alpha = jnp.exp(m_prev - m_new)
            weights = jnp.exp(scores - m_new)
            if masked:
                weights = jnp.where(allowed, weights, 0.0)
            l_new = alpha * l_prev + jnp.sum(weights, axis=0, keepdims=True)
            contrib = jnp.dot(
                v_t[cut, :], weights.astype(jnp.bfloat16), preferred_element_type=jnp.float32
            )
            slot = request * heads + h
            acc_t[slot] = alpha * acc_t[slot] + contrib
            stats[request, h : h + 1, :] = m_new
            stats[request, heads + h : heads + h + 1, :] = l_new
            stats[request, 2 * heads + h : 2 * heads + h + 1, :] = l_new

    @pl.when(kind == 1)
    def _cached():
        attend(kc_ref, vc_ref, False)

    @pl.when(kind == 2)
    def _fresh():
        attend(kf_ref, vf_ref, True)

    @pl.when(kind == 2)
    def _store_fresh():
        ko_ref[...] = kf_ref[...]
        vo_ref[...] = vf_ref[...]

    @pl.when(kind != 2)
    def _store_cached():
        ko_ref[...] = kc_ref[...]
        vo_ref[...] = vc_ref[...]

    @pl.when(step == pl.num_programs(0) - 1)
    def _emit():
        stat_rows = stats.shape[1]
        for r in range(requests):
            rows = pl.ds(r * span, span)
            for h in range(heads):
                tok_ref[rows, h * head_dim : (h + 1) * head_dim] = acc_t[r * heads + h].T
            block = jnp.concatenate(
                [stats[r], jnp.zeros((lanes - stat_rows, span), jnp.float32)], axis=0
            )
            ml_ref[rows, :] = block.T
        chunks, rows_per, _ = out_ref.shape
        lane = lax.broadcasted_iota(jnp.int32, (rows_per, lanes), 1)
        for d in range(chunks):
            rows = pl.ds(d * rows_per, rows_per)
            out_ref[d, :, :width] = tok_ref[rows, :].astype(jnp.bfloat16)
            ml = ml_ref[rows, :]
            rounded = ml.astype(jnp.bfloat16).astype(jnp.float32)
            packed = jnp.where(
                lane < 2 * heads,
                rounded,
                jnp.where(lane < 3 * heads, ml - rounded, 0.0),
            )
            out_ref[d, :, width:] = packed.astype(jnp.bfloat16)


def local_attention(slot_request, slot_kind, slot_limit, slot_fresh, gathered, kc, vc,
                    heads, head_dim, requests, span, chunks):
    _, tokens, width = gathered.shape
    slot_count = kc.shape[0]
    rows_per = tokens // chunks
    kernel = functools.partial(attend_kernel, heads, head_dim, requests, span)
    flops = 4 * slot_count * span * PAGE * width
    return pl.pallas_call(
        kernel,
        out_shape=(
            jax.ShapeDtypeStruct((chunks, rows_per, width + 128), jnp.bfloat16),
            jax.ShapeDtypeStruct(kc.shape, kc.dtype),
            jax.ShapeDtypeStruct(vc.shape, vc.dtype),
        ),
        grid_spec=pltpu.PrefetchScalarGridSpec(
            num_scalar_prefetch=4,
            grid=(slot_count,),
            in_specs=[
                pl.BlockSpec((1, tokens, width), lambda s, *_: (0, 0, 0),
                             pipeline_mode=pl.Buffered(1)),
                pl.BlockSpec((1, PAGE, width), lambda s, rq, kd, lm, fr: (1, fr[s], 0)),
                pl.BlockSpec((1, PAGE, width), lambda s, rq, kd, lm, fr: (2, fr[s], 0)),
                pl.BlockSpec((1, PAGE, width), lambda s, *_: (s, 0, 0)),
                pl.BlockSpec((1, PAGE, width), lambda s, *_: (s, 0, 0)),
            ],
            out_specs=[
                pl.BlockSpec((chunks, rows_per, width + 128), lambda s, *_: (0, 0, 0)),
                pl.BlockSpec((1, PAGE, width), lambda s, *_: (s, 0, 0)),
                pl.BlockSpec((1, PAGE, width), lambda s, *_: (s, 0, 0)),
            ],
            scratch_shapes=[
                pltpu.VMEM((requests * heads, head_dim, span), jnp.float32),
                pltpu.VMEM((requests, 16, span), jnp.float32),
                pltpu.VMEM((tokens, width), jnp.float32),
                pltpu.VMEM((tokens, 128), jnp.float32),
            ],
        ),
        compiler_params=pltpu.CompilerParams(
            dimension_semantics=("arbitrary",), vmem_limit_bytes=62 * 1024 * 1024
        ),
        cost_estimate=pl.CostEstimate(
            flops=flops,
            transcendentals=slot_count * span * PAGE * heads,
            bytes_accessed=tokens * width * 2 + 4 * kc.size * 2 + tokens * (width + 128) * 2,
        ),
    )(slot_request, slot_kind, slot_limit, slot_fresh, gathered, gathered, gathered, kc, vc)


def combine_kernel(heads, head_dim, recv_ref, w_ref, out_ref, o_acc, l_acc):
    chunks, rows_per, _ = recv_ref.shape
    width = heads * head_dim
    lanes = 128

    def peak_step(d, peak):
        return jnp.maximum(peak, recv_ref[d, :, width:].astype(jnp.float32))

    peak = lax.fori_loop(
        0, chunks, peak_step, jnp.full((rows_per, lanes), mask_score, jnp.float32)
    )
    o_acc[...] = jnp.zeros_like(o_acc)
    l_acc[...] = jnp.zeros_like(l_acc)

    def sum_step(d, carry):
        mld = recv_ref[d, :, width:].astype(jnp.float32)
        factor = jnp.exp(mld - peak)
        for h in range(heads):
            f_h = factor[:, h : h + 1]
            l_h = mld[:, heads + h : heads + h + 1] + mld[:, 2 * heads + h : 2 * heads + h + 1]
            l_acc[:, h : h + 1] += f_h * l_h
            cut = slice(h * head_dim, (h + 1) * head_dim)
            o_acc[:, cut] += f_h * recv_ref[d, :, cut].astype(jnp.float32)
        return carry

    lax.fori_loop(0, chunks, sum_step, 0)
    parts = []
    for h in range(heads):
        cut = slice(h * head_dim, (h + 1) * head_dim)
        parts.append((o_acc[:, cut] / l_acc[:, h : h + 1]).astype(jnp.bfloat16))
    attended = jnp.concatenate(parts, axis=1)
    out_ref[...] = lax.dot_general(
        attended, w_ref[0], (((1,), (1,)), ((), ())), preferred_element_type=jnp.float32
    ).astype(out_ref.dtype)


def combine_project(received, gathered, heads, head_dim):
    chunks, rows_per, _ = received.shape
    _, tokens, width = gathered.shape
    kernel = functools.partial(combine_kernel, heads, head_dim)
    return pl.pallas_call(
        kernel,
        out_shape=jax.ShapeDtypeStruct((rows_per, tokens), jnp.bfloat16),
        grid=(1,),
        in_specs=[
            pl.BlockSpec(received.shape, lambda i: (0, 0, 0)),
            pl.BlockSpec((1, tokens, width), lambda i: (3, 0, 0)),
        ],
        out_specs=pl.BlockSpec((rows_per, tokens), lambda i: (0, 0)),
        scratch_shapes=[
            pltpu.VMEM((rows_per, width), jnp.float32),
            pltpu.VMEM((rows_per, 128), jnp.float32),
        ],
        compiler_params=pltpu.CompilerParams(vmem_limit_bytes=48 * 1024 * 1024),
        cost_estimate=pl.CostEstimate(
            flops=2 * rows_per * tokens * width + 4 * received.size,
            transcendentals=chunks * rows_per * 128,
            bytes_accessed=received.size * 2 + tokens * width * 2 + rows_per * tokens * 2,
        ),
    )(received, gathered)


def pair_merge_kernel(heads, head_dim, packed_hbm, out_ref, mine, theirs, local_sem, send_sem, recv_sem):
    core = lax.axis_index("core")
    partner = 1 - core
    width = heads * head_dim
    lanes = 128
    chunks, rows_per, _ = out_ref.shape

    barrier = pltpu.get_barrier_semaphore()
    pl.semaphore_signal(barrier, inc=1, device_id={"core": partner}, device_id_type=pl.DeviceIdType.MESH)
    pl.semaphore_wait(barrier, 1)

    local = pltpu.make_async_copy(packed_hbm.at[:, core], mine, local_sem)
    local.start()
    remote = pltpu.make_async_remote_copy(
        src_ref=packed_hbm.at[:, partner],
        dst_ref=theirs,
        send_sem=send_sem,
        recv_sem=recv_sem,
        device_id={"core": partner},
        device_id_type=pl.DeviceIdType.MESH,
    )
    remote.start()
    local.wait()
    remote.wait()

    lane = lax.broadcasted_iota(jnp.int32, (rows_per, lanes), 1)

    def merge_step(c, carry):
        ml_a = mine[c, :, width:].astype(jnp.float32)
        ml_b = theirs[c, :, width:].astype(jnp.float32)
        peak = jnp.maximum(ml_a, ml_b)
        f_a = jnp.exp(ml_a - peak)
        f_b = jnp.exp(ml_b - peak)
        merged = jnp.zeros((rows_per, lanes), jnp.float32)
        for h in range(heads):
            cut = slice(h * head_dim, (h + 1) * head_dim)
            fa_h = f_a[:, h : h + 1]
            fb_h = f_b[:, h : h + 1]
            out_ref[c, :, cut] = (
                fa_h * mine[c, :, cut].astype(jnp.float32)
                + fb_h * theirs[c, :, cut].astype(jnp.float32)
            ).astype(out_ref.dtype)
            l_a = ml_a[:, heads + h : heads + h + 1] + ml_a[:, 2 * heads + h : 2 * heads + h + 1]
            l_b = ml_b[:, heads + h : heads + h + 1] + ml_b[:, 2 * heads + h : 2 * heads + h + 1]
            l_h = fa_h * l_a + fb_h * l_b
            l_hi = l_h.astype(jnp.bfloat16).astype(jnp.float32)
            merged = jnp.where(
                lane == h,
                peak[:, h : h + 1],
                jnp.where(
                    lane == heads + h,
                    l_hi,
                    jnp.where(lane == 2 * heads + h, l_h - l_hi, merged),
                ),
            )
        out_ref[c, :, width:] = merged.astype(out_ref.dtype)
        return carry

    lax.fori_loop(0, chunks, merge_step, 0)


def pair_merge(packed, heads, head_dim):
    devices, rows_per, lanes_all = packed.shape
    chips = devices // 2
    view = packed.reshape(chips, 2, rows_per, lanes_all)
    kernel = functools.partial(pair_merge_kernel, heads, head_dim)
    return pl.pallas_call(
        kernel,
        out_shape=jax.ShapeDtypeStruct((chips, rows_per, lanes_all), packed.dtype),
        in_specs=[pl.BlockSpec(memory_space=pl.ANY)],
        out_specs=pl.BlockSpec(memory_space=pltpu.VMEM),
        scratch_shapes=[
            pltpu.VMEM((chips, rows_per, lanes_all), packed.dtype),
            pltpu.VMEM((chips, rows_per, lanes_all), packed.dtype),
            pltpu.SemaphoreType.DMA(()),
            pltpu.SemaphoreType.DMA(()),
            pltpu.SemaphoreType.DMA(()),
        ],
        compiler_params=pltpu.CompilerParams(
            collective_id=0, has_side_effects=True, vmem_limit_bytes=40 * 1024 * 1024
        ),
        cost_estimate=pl.CostEstimate(
            flops=6 * chips * rows_per * lanes_all,
            transcendentals=2 * chips * rows_per * 128,
            bytes_accessed=3 * chips * rows_per * lanes_all * 2,
        ),
    )(view)


def heads_sum_kernel(groups, block, proj_hbm, out_ref, own, received, own_sem, send_sems, recv_sems):
    group = lax.axis_index("heads")
    barrier = pltpu.get_barrier_semaphore()
    for k in range(1, groups):
        pl.semaphore_signal(
            barrier, inc=1, device_id={"heads": lax.rem(group + k, groups)},
            device_id_type=pl.DeviceIdType.MESH,
        )
    pl.semaphore_wait(barrier, groups - 1)
    local = pltpu.make_async_copy(
        proj_hbm.at[:, pl.ds(pl.multiple_of(group * block, 128), block)], own, own_sem
    )
    local.start()
    copies = []
    for k in range(1, groups):
        dest = lax.rem(group + k, groups)
        copy = pltpu.make_async_remote_copy(
            src_ref=proj_hbm.at[:, pl.ds(pl.multiple_of(dest * block, 128), block)],
            dst_ref=received.at[k - 1],
            send_sem=send_sems.at[k - 1],
            recv_sem=recv_sems.at[k - 1],
            device_id={"heads": dest},
            device_id_type=pl.DeviceIdType.MESH,
        )
        copy.start()
        copies.append(copy)
    local.wait()
    for copy in copies:
        copy.wait()
    total = own[...].astype(jnp.float32)
    for k in range(groups - 1):
        total = total + received[k].astype(jnp.float32)
    out_ref[...] = total


def heads_sum(projected, groups):
    rows, cols = projected.shape
    block = cols // groups
    kernel = functools.partial(heads_sum_kernel, groups, block)
    return pl.pallas_call(
        kernel,
        out_shape=jax.ShapeDtypeStruct((rows, block), jnp.float32),
        in_specs=[pl.BlockSpec(memory_space=pl.ANY)],
        out_specs=pl.BlockSpec(memory_space=pltpu.VMEM),
        scratch_shapes=[
            pltpu.VMEM((rows, block), projected.dtype),
            pltpu.VMEM((groups - 1, rows, block), projected.dtype),
            pltpu.SemaphoreType.DMA(()),
            pltpu.SemaphoreType.DMA((groups - 1,)),
            pltpu.SemaphoreType.DMA((groups - 1,)),
        ],
        compiler_params=pltpu.CompilerParams(collective_id=1, has_side_effects=True),
        cost_estimate=pl.CostEstimate(
            flops=groups * rows * block,
            transcendentals=0,
            bytes_accessed=groups * rows * block * 2 + rows * block * 4,
        ),
    )(projected)


def per_device(
    queries,
    keys,
    values,
    key_cache,
    value_cache,
    cache_len,
    page_table,
    append_slots,
    out_weight,
    out_bias,
):
    tok_dev, head_count, head_dim = queries.shape
    width = head_count * head_dim
    requests = cache_len.shape[0]
    max_pages = page_table.shape[1]
    new_pages = append_slots.shape[1]
    span_len = new_pages * PAGE
    slot_count = key_cache.shape[0]
    page_devices = lax.axis_size(PAGES)
    device_at = lax.axis_index(PAGES)
    token_ids = device_at * tok_dev + jnp.arange(tok_dev, dtype=jnp.int32)
    request_ids = token_ids // span_len
    request_grid = jnp.arange(requests, dtype=jnp.int32)
    starts = jnp.sum(
        jnp.where(request_ids[:, None] == request_grid[None, :], cache_len[None, :], 0), axis=1
    )
    positions = (starts + token_ids % span_len).astype(jnp.float32)
    rotated_q = rotate(queries.astype(jnp.float32), positions).astype(jnp.bfloat16)
    rotated_k = rotate(keys.astype(jnp.float32), positions).astype(jnp.bfloat16)
    w_cols = out_weight.shape[1]
    w_plane = jnp.pad(out_weight.T, ((0, tok_dev - w_cols), (0, 0)))
    stacked = jnp.stack(
        [
            rotated_q.reshape(tok_dev, width),
            rotated_k.reshape(tok_dev, width),
            values.reshape(tok_dev, width),
            w_plane,
        ]
    )
    gathered = lax.all_gather(stacked, PAGES, axis=1, tiled=True)
    my_slots = device_at * slot_count + jnp.arange(slot_count, dtype=jnp.int32)
    cached_hit = page_table.reshape(-1)[None, :] == my_slots[:, None]
    fresh_hit = append_slots.reshape(-1)[None, :] == my_slots[:, None]
    is_cached = jnp.any(cached_hit, axis=1)
    is_fresh = jnp.any(fresh_hit, axis=1)
    cached_index = jnp.sum(
        jnp.where(cached_hit, jnp.arange(requests * max_pages, dtype=jnp.int32)[None, :], 0), axis=1
    )
    fresh_index = jnp.sum(
        jnp.where(fresh_hit, jnp.arange(requests * new_pages, dtype=jnp.int32)[None, :], 0), axis=1
    )
    slot_request = jnp.where(is_fresh, fresh_index // new_pages, cached_index // max_pages)
    slot_page = jnp.where(is_fresh, fresh_index % new_pages, cached_index % max_pages)
    slot_length = jnp.sum(
        jnp.where(slot_request[:, None] == request_grid[None, :], cache_len[None, :], 0), axis=1
    )
    visible = is_cached & (slot_page * PAGE < slot_length)
    slot_kind = jnp.where(is_fresh, 2, jnp.where(visible, 1, 0)).astype(jnp.int32)
    slot_limit = jnp.where(is_fresh, slot_page * PAGE, -4 * span_len)
    packed, key_slots, value_slots = local_attention(
        slot_request,
        slot_kind,
        slot_limit,
        fresh_index,
        gathered,
        key_cache.reshape(slot_count, PAGE, width),
        value_cache.reshape(slot_count, PAGE, width),
        head_count,
        head_dim,
        requests,
        span_len,
        page_devices,
    )
    paired = pair_merge(packed, head_count, head_dim)
    received = lax.all_to_all(paired, "chips", 0, 0, tiled=True)
    projected = combine_project(received, gathered, head_count, head_dim)
    head_groups = lax.axis_size("heads")
    summed = heads_sum(projected, head_groups)
    summed = summed.reshape(tok_dev, page_devices // head_groups, tok_dev)[:, :, :w_cols].reshape(
        tok_dev, (page_devices // head_groups) * w_cols
    )
    key_out = key_slots.reshape(key_cache.shape)
    value_out = value_slots.reshape(value_cache.shape)
    hidden = (summed + out_bias[None, :]).astype(jnp.bfloat16)
    return (hidden, key_out, value_out)


def solution(mesh):
    heads_n, pages_n = mesh.devices.shape
    split = jax.sharding.Mesh(
        mesh.devices.reshape(heads_n, pages_n // 2, 2), ("heads", "chips", "core")
    )
    placed = (
        P(PAGES, "heads", None),
        P(PAGES, "heads", None),
        P(PAGES, "heads", None),
        P(PAGES, None, "heads", None),
        P(PAGES, None, "heads", None),
        P(),
        P(),
        P(),
        P("heads", PAGES),
        P("heads"),
    )
    return jax.shard_map(
        per_device,
        mesh=split,
        in_specs=placed,
        out_specs=(
            P(PAGES, "heads"),
            P(PAGES, None, "heads", None),
            P(PAGES, None, "heads", None),
        ),
        check_vma=False,
    )
```

```python
import functools
import math

import jax
import jax.numpy as jnp
from jax import lax
from jax.experimental import pallas as pl
from jax.experimental.pallas import tpu as pltpu
from jax.sharding import PartitionSpec as P

ROT = 32
PAGE = 128
PAGES = ("z", "y", "core")


low_score = -1e30
mask_score = -(2.0 ** 100)


def rotate(vectors, positions):
    half_rot = ROT // 2
    inv_freq = 10000.0 ** (-2.0 * jnp.arange(half_rot, dtype=jnp.float32) / ROT)
    angles = positions[:, None] * inv_freq[None, :]
    cosine = jnp.cos(angles)[:, None, :]
    sine = jnp.sin(angles)[:, None, :]
    first_half = vectors[..., :half_rot]
    second_half = vectors[..., half_rot:ROT]
    return jnp.concatenate(
        [
            first_half * cosine - second_half * sine,
            second_half * cosine + first_half * sine,
            vectors[..., ROT:],
        ],
        axis=-1,
    )


def attend_kernel(
    heads, head_dim, requests, span,
    sreq_ref, skind_ref, slim_ref, sfresh_ref,
    q_ref, kf_ref, vf_ref, kc_ref, vc_ref,
    out_ref, ko_ref, vo_ref, acc_t, stats, tok_ref, ml_ref,
):
    step = pl.program_id(0)
    lanes = ml_ref.shape[1]
    width = heads * head_dim

    @pl.when(step == 0)
    def _init():
        acc_t[...] = jnp.zeros_like(acc_t)
        row = lax.broadcasted_iota(jnp.int32, stats.shape, 1)
        stats[...] = jnp.where(row < heads, mask_score, 0.0).astype(jnp.float32)

    request = sreq_ref[step]
    kind = skind_ref[step]
    limit = slim_ref[step]
    scale = 1.0 / math.sqrt(head_dim)

    def attend(k_ref, v_ref, masked):
        base = pl.multiple_of(request * span, span)
        if masked:
            keys_at = lax.broadcasted_iota(jnp.int32, (PAGE, span), 0)
            queries_at = lax.broadcasted_iota(jnp.int32, (PAGE, span), 1)
            allowed = queries_at - keys_at >= limit
        v_t = v_ref[0].astype(jnp.float32).T.astype(jnp.bfloat16)
        for h in range(heads):
            cut = slice(h * head_dim, (h + 1) * head_dim)
            q_h = q_ref[0, pl.ds(base, span), cut]
            k_h = k_ref[0, :, cut]
            scores = lax.dot_general(
                k_h, q_h, (((1,), (1,)), ((), ())), preferred_element_type=jnp.float32
            ) * scale
            if masked:
                scores = jnp.where(allowed, scores, mask_score)
            m_prev = stats[request, h : h + 1, :]
            l_prev = stats[request, heads + h : heads + h + 1, :]
            m_new = jnp.maximum(m_prev, jnp.max(scores, axis=0, keepdims=True))
            m_new = m_new.astype(jnp.bfloat16).astype(jnp.float32)
            alpha = jnp.exp(m_prev - m_new)
            weights = jnp.exp(scores - m_new)
            if masked:
                weights = jnp.where(allowed, weights, 0.0)
            l_new = alpha * l_prev + jnp.sum(weights, axis=0, keepdims=True)
            contrib = jnp.dot(
                v_t[cut, :], weights.astype(jnp.bfloat16), preferred_element_type=jnp.float32
            )
            slot = request * heads + h
            acc_t[slot] = alpha * acc_t[slot] + contrib
            stats[request, h : h + 1, :] = m_new
            stats[request, heads + h : heads + h + 1, :] = l_new
            stats[request, 2 * heads + h : 2 * heads + h + 1, :] = l_new

    @pl.when(kind == 1)
    def _cached():
        attend(kc_ref, vc_ref, False)

    @pl.when(kind == 2)
    def _fresh():
        attend(kf_ref, vf_ref, True)

    @pl.when(kind == 2)
    def _store_fresh():
        ko_ref[...] = kf_ref[...]
        vo_ref[...] = vf_ref[...]

    @pl.when(kind != 2)
    def _store_cached():
        ko_ref[...] = kc_ref[...]
        vo_ref[...] = vc_ref[...]

    @pl.when(step == pl.num_programs(0) - 1)
    def _emit():
        stat_rows = stats.shape[1]
        for r in range(requests):
            rows = pl.ds(r * span, span)
            for h in range(heads):
                tok_ref[rows, h * head_dim : (h + 1) * head_dim] = acc_t[r * heads + h].T
            block = jnp.concatenate(
                [stats[r], jnp.zeros((lanes - stat_rows, span), jnp.float32)], axis=0
            )
            ml_ref[rows, :] = block.T
        chunks, rows_per, _ = out_ref.shape
        lane = lax.broadcasted_iota(jnp.int32, (rows_per, lanes), 1)
        for d in range(chunks):
            rows = pl.ds(d * rows_per, rows_per)
            out_ref[d, :, :width] = tok_ref[rows, :].astype(jnp.bfloat16)
            ml = ml_ref[rows, :]
            rounded = ml.astype(jnp.bfloat16).astype(jnp.float32)
            packed = jnp.where(
                lane < 2 * heads,
                rounded,
                jnp.where(lane < 3 * heads, ml - rounded, 0.0),
            )
            out_ref[d, :, width:] = packed.astype(jnp.bfloat16)


def local_attention(slot_request, slot_kind, slot_limit, slot_fresh, gathered, kc, vc,
                    heads, head_dim, requests, span, chunks):
    _, tokens, width = gathered.shape
    slot_count = kc.shape[0]
    rows_per = tokens // chunks
    kernel = functools.partial(attend_kernel, heads, head_dim, requests, span)
    flops = 4 * slot_count * span * PAGE * width
    return pl.pallas_call(
        kernel,
        out_shape=(
            jax.ShapeDtypeStruct((chunks, rows_per, width + 128), jnp.bfloat16),
            jax.ShapeDtypeStruct(kc.shape, kc.dtype),
            jax.ShapeDtypeStruct(vc.shape, vc.dtype),
        ),
        grid_spec=pltpu.PrefetchScalarGridSpec(
            num_scalar_prefetch=4,
            grid=(slot_count,),
            in_specs=[
                pl.BlockSpec((1, tokens, width), lambda s, *_: (0, 0, 0),
                             pipeline_mode=pl.Buffered(1)),
                pl.BlockSpec((1, PAGE, width), lambda s, rq, kd, lm, fr: (1, fr[s], 0)),
                pl.BlockSpec((1, PAGE, width), lambda s, rq, kd, lm, fr: (2, fr[s], 0)),
                pl.BlockSpec((1, PAGE, width), lambda s, *_: (s, 0, 0)),
                pl.BlockSpec((1, PAGE, width), lambda s, *_: (s, 0, 0)),
            ],
            out_specs=[
                pl.BlockSpec((chunks, rows_per, width + 128), lambda s, *_: (0, 0, 0)),
                pl.BlockSpec((1, PAGE, width), lambda s, *_: (s, 0, 0)),
                pl.BlockSpec((1, PAGE, width), lambda s, *_: (s, 0, 0)),
            ],
            scratch_shapes=[
                pltpu.VMEM((requests * heads, head_dim, span), jnp.float32),
                pltpu.VMEM((requests, 16, span), jnp.float32),
                pltpu.VMEM((tokens, width), jnp.float32),
                pltpu.VMEM((tokens, 128), jnp.float32),
            ],
        ),
        compiler_params=pltpu.CompilerParams(
            dimension_semantics=("arbitrary",), vmem_limit_bytes=62 * 1024 * 1024
        ),
        cost_estimate=pl.CostEstimate(
            flops=flops,
            transcendentals=slot_count * span * PAGE * heads,
            bytes_accessed=tokens * width * 2 + 4 * kc.size * 2 + tokens * (width + 128) * 2,
        ),
    )(slot_request, slot_kind, slot_limit, slot_fresh, gathered, gathered, gathered, kc, vc)


def combine_kernel(heads, head_dim, recv_ref, w_ref, out_ref, o_acc, l_acc):
    chunks, rows_per, _ = recv_ref.shape
    width = heads * head_dim
    lanes = 128

    def peak_step(d, peak):
        return jnp.maximum(peak, recv_ref[d, :, width:].astype(jnp.float32))

    peak = lax.fori_loop(
        0, chunks, peak_step, jnp.full((rows_per, lanes), mask_score, jnp.float32)
    )
    o_acc[...] = jnp.zeros_like(o_acc)
    l_acc[...] = jnp.zeros_like(l_acc)

    def sum_step(d, carry):
        mld = recv_ref[d, :, width:].astype(jnp.float32)
        factor = jnp.exp(mld - peak)
        for h in range(heads):
            f_h = factor[:, h : h + 1]
            l_h = mld[:, heads + h : heads + h + 1] + mld[:, 2 * heads + h : 2 * heads + h + 1]
            l_acc[:, h : h + 1] += f_h * l_h
            cut = slice(h * head_dim, (h + 1) * head_dim)
            o_acc[:, cut] += f_h * recv_ref[d, :, cut].astype(jnp.float32)
        return carry

    lax.fori_loop(0, chunks, sum_step, 0)
    parts = []
    for h in range(heads):
        cut = slice(h * head_dim, (h + 1) * head_dim)
        parts.append((o_acc[:, cut] / l_acc[:, h : h + 1]).astype(jnp.bfloat16))
    attended = jnp.concatenate(parts, axis=1)
    out_ref[...] = lax.dot_general(
        attended, w_ref[0], (((1,), (1,)), ((), ())), preferred_element_type=jnp.float32
    ).astype(out_ref.dtype)


def combine_project(received, gathered, heads, head_dim):
    chunks, rows_per, _ = received.shape
    _, tokens, width = gathered.shape
    kernel = functools.partial(combine_kernel, heads, head_dim)
    return pl.pallas_call(
        kernel,
        out_shape=jax.ShapeDtypeStruct((rows_per, tokens), jnp.bfloat16),
        grid=(1,),
        in_specs=[
            pl.BlockSpec(received.shape, lambda i: (0, 0, 0)),
            pl.BlockSpec((1, tokens, width), lambda i: (3, 0, 0)),
        ],
        out_specs=pl.BlockSpec((rows_per, tokens), lambda i: (0, 0)),
        scratch_shapes=[
            pltpu.VMEM((rows_per, width), jnp.float32),
            pltpu.VMEM((rows_per, 128), jnp.float32),
        ],
        compiler_params=pltpu.CompilerParams(vmem_limit_bytes=48 * 1024 * 1024),
        cost_estimate=pl.CostEstimate(
            flops=2 * rows_per * tokens * width + 4 * received.size,
            transcendentals=chunks * rows_per * 128,
            bytes_accessed=received.size * 2 + tokens * width * 2 + rows_per * tokens * 2,
        ),
    )(received, gathered)


def pair_merge_kernel(heads, head_dim, packed_hbm, out_ref, mine, theirs, local_sem, send_sem, recv_sem):
    core = lax.axis_index("core")
    partner = 1 - core
    width = heads * head_dim
    lanes = 128
    chunks, rows_per, _ = out_ref.shape

    barrier = pltpu.get_barrier_semaphore()
    pl.semaphore_signal(barrier, inc=1, device_id={"core": partner}, device_id_type=pl.DeviceIdType.MESH)
    pl.semaphore_wait(barrier, 1)

    local = pltpu.make_async_copy(packed_hbm.at[:, core], mine, local_sem)
    local.start()
    remote = pltpu.make_async_remote_copy(
        src_ref=packed_hbm.at[:, partner],
        dst_ref=theirs,
        send_sem=send_sem,
        recv_sem=recv_sem,
        device_id={"core": partner},
        device_id_type=pl.DeviceIdType.MESH,
    )
    remote.start()
    local.wait()
    remote.wait()

    lane = lax.broadcasted_iota(jnp.int32, (rows_per, lanes), 1)

    def merge_step(c, carry):
        ml_a = mine[c, :, width:].astype(jnp.float32)
        ml_b = theirs[c, :, width:].astype(jnp.float32)
        peak = jnp.maximum(ml_a, ml_b)
        f_a = jnp.exp(ml_a - peak)
        f_b = jnp.exp(ml_b - peak)
        merged = jnp.zeros((rows_per, lanes), jnp.float32)
        for h in range(heads):
            cut = slice(h * head_dim, (h + 1) * head_dim)
            fa_h = f_a[:, h : h + 1]
            fb_h = f_b[:, h : h + 1]
            out_ref[c, :, cut] = (
                fa_h * mine[c, :, cut].astype(jnp.float32)
                + fb_h * theirs[c, :, cut].astype(jnp.float32)
            ).astype(out_ref.dtype)
            l_a = ml_a[:, heads + h : heads + h + 1] + ml_a[:, 2 * heads + h : 2 * heads + h + 1]
            l_b = ml_b[:, heads + h : heads + h + 1] + ml_b[:, 2 * heads + h : 2 * heads + h + 1]
            l_h = fa_h * l_a + fb_h * l_b
            l_hi = l_h.astype(jnp.bfloat16).astype(jnp.float32)
            merged = jnp.where(
                lane == h,
                peak[:, h : h + 1],
                jnp.where(
                    lane == heads + h,
                    l_hi,
                    jnp.where(lane == 2 * heads + h, l_h - l_hi, merged),
                ),
            )
        out_ref[c, :, width:] = merged.astype(out_ref.dtype)
        return carry

    lax.fori_loop(0, chunks, merge_step, 0)


def pair_merge(packed, heads, head_dim):
    devices, rows_per, lanes_all = packed.shape
    chips = devices // 2
    view = packed.reshape(chips, 2, rows_per, lanes_all)
    kernel = functools.partial(pair_merge_kernel, heads, head_dim)
    return pl.pallas_call(
        kernel,
        out_shape=jax.ShapeDtypeStruct((chips, rows_per, lanes_all), packed.dtype),
        in_specs=[pl.BlockSpec(memory_space=pl.ANY)],
        out_specs=pl.BlockSpec(memory_space=pltpu.VMEM),
        scratch_shapes=[
            pltpu.VMEM((chips, rows_per, lanes_all), packed.dtype),
            pltpu.VMEM((chips, rows_per, lanes_all), packed.dtype),
            pltpu.SemaphoreType.DMA(()),
            pltpu.SemaphoreType.DMA(()),
            pltpu.SemaphoreType.DMA(()),
        ],
        compiler_params=pltpu.CompilerParams(
            collective_id=0, has_side_effects=True, vmem_limit_bytes=40 * 1024 * 1024
        ),
        cost_estimate=pl.CostEstimate(
            flops=6 * chips * rows_per * lanes_all,
            transcendentals=2 * chips * rows_per * 128,
            bytes_accessed=3 * chips * rows_per * lanes_all * 2,
        ),
    )(view)


def heads_sum_kernel(groups, block, proj_hbm, out_ref, own, received, own_sem, send_sems, recv_sems):
    group = lax.axis_index("heads")
    barrier = pltpu.get_barrier_semaphore()
    for k in range(1, groups):
        pl.semaphore_signal(
            barrier, inc=1, device_id={"heads": lax.rem(group + k, groups)},
            device_id_type=pl.DeviceIdType.MESH,
        )
    pl.semaphore_wait(barrier, groups - 1)
    local = pltpu.make_async_copy(
        proj_hbm.at[:, pl.ds(pl.multiple_of(group * block, 128), block)], own, own_sem
    )
    local.start()
    copies = []
    for k in range(1, groups):
        dest = lax.rem(group + k, groups)
        copy = pltpu.make_async_remote_copy(
            src_ref=proj_hbm.at[:, pl.ds(pl.multiple_of(dest * block, 128), block)],
            dst_ref=received.at[k - 1],
            send_sem=send_sems.at[k - 1],
            recv_sem=recv_sems.at[k - 1],
            device_id={"heads": dest},
            device_id_type=pl.DeviceIdType.MESH,
        )
        copy.start()
        copies.append(copy)
    local.wait()
    for copy in copies:
        copy.wait()
    total = own[...].astype(jnp.float32)
    for k in range(groups - 1):
        total = total + received[k].astype(jnp.float32)
    out_ref[...] = total


def heads_sum(projected, groups):
    rows, cols = projected.shape
    block = cols // groups
    kernel = functools.partial(heads_sum_kernel, groups, block)
    return pl.pallas_call(
        kernel,
        out_shape=jax.ShapeDtypeStruct((rows, block), jnp.float32),
        in_specs=[pl.BlockSpec(memory_space=pl.ANY)],
        out_specs=pl.BlockSpec(memory_space=pltpu.VMEM),
        scratch_shapes=[
            pltpu.VMEM((rows, block), projected.dtype),
            pltpu.VMEM((groups - 1, rows, block), projected.dtype),
            pltpu.SemaphoreType.DMA(()),
            pltpu.SemaphoreType.DMA((groups - 1,)),
            pltpu.SemaphoreType.DMA((groups - 1,)),
        ],
        compiler_params=pltpu.CompilerParams(collective_id=1, has_side_effects=True),
        cost_estimate=pl.CostEstimate(
            flops=groups * rows * block,
            transcendentals=0,
            bytes_accessed=groups * rows * block * 2 + rows * block * 4,
        ),
    )(projected)


def merge_parts_kernel(heads, head_dim, parts_ref, out_ref):
    chunks, parts, rows_per, _ = parts_ref.shape
    width = heads * head_dim
    lanes = 128
    lane = lax.broadcasted_iota(jnp.int32, (rows_per, lanes), 1)

    def merge_step(c, carry):
        stats = [parts_ref[c, j, :, width:].astype(jnp.float32) for j in range(parts)]
        peak = stats[0]
        for j in range(1, parts):
            peak = jnp.maximum(peak, stats[j])
        factors = [jnp.exp(st - peak) for st in stats]
        merged = jnp.zeros((rows_per, lanes), jnp.float32)
        for h in range(heads):
            cut = slice(h * head_dim, (h + 1) * head_dim)
            o_h = jnp.zeros((rows_per, head_dim), jnp.float32)
            l_h = jnp.zeros((rows_per, 1), jnp.float32)
            for j in range(parts):
                f_h = factors[j][:, h : h + 1]
                o_h = o_h + f_h * parts_ref[c, j, :, cut].astype(jnp.float32)
                l_j = (
                    stats[j][:, heads + h : heads + h + 1]
                    + stats[j][:, 2 * heads + h : 2 * heads + h + 1]
                )
                l_h = l_h + f_h * l_j
            out_ref[c, :, cut] = o_h.astype(out_ref.dtype)
            l_hi = l_h.astype(jnp.bfloat16).astype(jnp.float32)
            merged = jnp.where(
                lane == h,
                peak[:, h : h + 1],
                jnp.where(
                    lane == heads + h,
                    l_hi,
                    jnp.where(lane == 2 * heads + h, l_h - l_hi, merged),
                ),
            )
        out_ref[c, :, width:] = merged.astype(out_ref.dtype)
        return carry

    lax.fori_loop(0, chunks, merge_step, 0)


def merge_parts(parts_in, heads, head_dim):
    chunks, parts, rows_per, lanes_all = parts_in.shape
    kernel = functools.partial(merge_parts_kernel, heads, head_dim)
    return pl.pallas_call(
        kernel,
        out_shape=jax.ShapeDtypeStruct((chunks, rows_per, lanes_all), parts_in.dtype),
        grid=(1,),
        in_specs=[pl.BlockSpec(parts_in.shape, lambda i: (0, 0, 0, 0))],
        out_specs=pl.BlockSpec((chunks, rows_per, lanes_all), lambda i: (0, 0, 0)),
        compiler_params=pltpu.CompilerParams(vmem_limit_bytes=32 * 1024 * 1024),
        cost_estimate=pl.CostEstimate(
            flops=4 * parts_in.size,
            transcendentals=chunks * parts * rows_per * 128,
            bytes_accessed=parts_in.size * 2 + chunks * rows_per * lanes_all * 2,
        ),
    )(parts_in)


def per_device(
    queries,
    keys,
    values,
    key_cache,
    value_cache,
    cache_len,
    page_table,
    append_slots,
    out_weight,
    out_bias,
):
    tok_dev, head_count, head_dim = queries.shape
    width = head_count * head_dim
    requests = cache_len.shape[0]
    max_pages = page_table.shape[1]
    new_pages = append_slots.shape[1]
    span_len = new_pages * PAGE
    slot_count = key_cache.shape[0]
    page_devices = lax.axis_size(PAGES)
    device_at = lax.axis_index(PAGES)
    token_ids = device_at * tok_dev + jnp.arange(tok_dev, dtype=jnp.int32)
    request_ids = token_ids // span_len
    request_grid = jnp.arange(requests, dtype=jnp.int32)
    starts = jnp.sum(
        jnp.where(request_ids[:, None] == request_grid[None, :], cache_len[None, :], 0), axis=1
    )
    positions = (starts + token_ids % span_len).astype(jnp.float32)
    rotated_q = rotate(queries.astype(jnp.float32), positions).astype(jnp.bfloat16)
    rotated_k = rotate(keys.astype(jnp.float32), positions).astype(jnp.bfloat16)
    w_cols = out_weight.shape[1]
    w_plane = jnp.pad(out_weight.T, ((0, tok_dev - w_cols), (0, 0)))
    stacked = jnp.stack(
        [
            rotated_q.reshape(tok_dev, width),
            rotated_k.reshape(tok_dev, width),
            values.reshape(tok_dev, width),
            w_plane,
        ]
    )
    gathered = lax.all_gather(stacked, PAGES, axis=1, tiled=True)
    my_slots = device_at * slot_count + jnp.arange(slot_count, dtype=jnp.int32)
    cached_hit = page_table.reshape(-1)[None, :] == my_slots[:, None]
    fresh_hit = append_slots.reshape(-1)[None, :] == my_slots[:, None]
    is_cached = jnp.any(cached_hit, axis=1)
    is_fresh = jnp.any(fresh_hit, axis=1)
    cached_index = jnp.sum(
        jnp.where(cached_hit, jnp.arange(requests * max_pages, dtype=jnp.int32)[None, :], 0), axis=1
    )
    fresh_index = jnp.sum(
        jnp.where(fresh_hit, jnp.arange(requests * new_pages, dtype=jnp.int32)[None, :], 0), axis=1
    )
    slot_request = jnp.where(is_fresh, fresh_index // new_pages, cached_index // max_pages)
    slot_page = jnp.where(is_fresh, fresh_index % new_pages, cached_index % max_pages)
    slot_length = jnp.sum(
        jnp.where(slot_request[:, None] == request_grid[None, :], cache_len[None, :], 0), axis=1
    )
    visible = is_cached & (slot_page * PAGE < slot_length)
    slot_kind = jnp.where(is_fresh, 2, jnp.where(visible, 1, 0)).astype(jnp.int32)
    slot_limit = jnp.where(is_fresh, slot_page * PAGE, -4 * span_len)
    packed, key_slots, value_slots = local_attention(
        slot_request,
        slot_kind,
        slot_limit,
        fresh_index,
        gathered,
        key_cache.reshape(slot_count, PAGE, width),
        value_cache.reshape(slot_count, PAGE, width),
        head_count,
        head_dim,
        requests,
        span_len,
        page_devices,
    )
    paired = pair_merge(packed, head_count, head_dim)
    z_n = lax.axis_size("z")
    y_n = lax.axis_size("y")
    by_y = paired.reshape(z_n, y_n, tok_dev, paired.shape[-1])
    from_y = lax.all_to_all(by_y, "y", 1, 1, tiled=True)
    merged = merge_parts(from_y, head_count, head_dim)
    received = lax.all_to_all(merged, "z", 0, 0, tiled=True)
    projected = combine_project(received, gathered, head_count, head_dim)
    head_groups = lax.axis_size("heads")
    summed = heads_sum(projected, head_groups)
    summed = summed.reshape(tok_dev, page_devices // head_groups, tok_dev)[:, :, :w_cols].reshape(
        tok_dev, (page_devices // head_groups) * w_cols
    )
    key_out = key_slots.reshape(key_cache.shape)
    value_out = value_slots.reshape(value_cache.shape)
    hidden = (summed + out_bias[None, :]).astype(jnp.bfloat16)
    return (hidden, key_out, value_out)


def solution(mesh):
    heads_n, pages_n = mesh.devices.shape
    z_n = pages_n // 8
    split = jax.sharding.Mesh(
        mesh.devices.reshape(heads_n, z_n, 4, 2), ("heads", "z", "y", "core")
    )
    placed = (
        P(PAGES, "heads", None),
        P(PAGES, "heads", None),
        P(PAGES, "heads", None),
        P(PAGES, None, "heads", None),
        P(PAGES, None, "heads", None),
        P(),
        P(),
        P(),
        P("heads", PAGES),
        P("heads"),
    )
    return jax.shard_map(
        per_device,
        mesh=split,
        in_specs=placed,
        out_specs=(
            P(PAGES, "heads"),
            P(PAGES, None, "heads", None),
            P(PAGES, None, "heads", None),
        ),
        check_vma=False,
    )
```

```python
import functools
import math

import jax
import jax.numpy as jnp
from jax import lax
from jax.experimental import pallas as pl
from jax.experimental.pallas import tpu as pltpu
from jax.sharding import PartitionSpec as P

ROT = 32
PAGE = 128
PAGES = ("z", "y", "core")


low_score = -1e30
mask_score = -(2.0 ** 100)


def rotate(vectors, positions):
    half_rot = ROT // 2
    inv_freq = 10000.0 ** (-2.0 * jnp.arange(half_rot, dtype=jnp.float32) / ROT)
    angles = positions[:, None] * inv_freq[None, :]
    cosine = jnp.cos(angles)[:, None, :]
    sine = jnp.sin(angles)[:, None, :]
    first_half = vectors[..., :half_rot]
    second_half = vectors[..., half_rot:ROT]
    return jnp.concatenate(
        [
            first_half * cosine - second_half * sine,
            second_half * cosine + first_half * sine,
            vectors[..., ROT:],
        ],
        axis=-1,
    )


def attend_kernel(
    heads, head_dim, requests, span,
    sreq_ref, skind_ref, slim_ref, sfresh_ref,
    q_ref, kf_ref, vf_ref, kc_ref, vc_ref,
    out_ref, ko_ref, vo_ref, acc_t, stats, tok_ref, ml_ref,
):
    step = pl.program_id(0)
    lanes = ml_ref.shape[1]
    width = heads * head_dim

    @pl.when(step == 0)
    def _init():
        acc_t[...] = jnp.zeros_like(acc_t)
        row = lax.broadcasted_iota(jnp.int32, stats.shape, 1)
        stats[...] = jnp.where(row < heads, mask_score, 0.0).astype(jnp.float32)

    request = sreq_ref[step]
    kind = skind_ref[step]
    limit = slim_ref[step]
    scale = 1.0 / math.sqrt(head_dim)

    def attend(k_ref, v_ref, masked):
        base = pl.multiple_of(request * span, span)
        if masked:
            keys_at = lax.broadcasted_iota(jnp.int32, (PAGE, span), 0)
            queries_at = lax.broadcasted_iota(jnp.int32, (PAGE, span), 1)
            allowed = queries_at - keys_at >= limit
        v_t = v_ref[0].astype(jnp.float32).T.astype(jnp.bfloat16)
        for h in range(heads):
            cut = slice(h * head_dim, (h + 1) * head_dim)
            q_h = q_ref[0, pl.ds(base, span), cut]
            k_h = k_ref[0, :, cut]
            scores = lax.dot_general(
                k_h, q_h, (((1,), (1,)), ((), ())), preferred_element_type=jnp.float32
            ) * scale
            if masked:
                scores = jnp.where(allowed, scores, mask_score)
            m_prev = stats[request, h : h + 1, :]
            l_prev = stats[request, heads + h : heads + h + 1, :]
            m_new = jnp.maximum(m_prev, jnp.max(scores, axis=0, keepdims=True))
            m_new = m_new.astype(jnp.bfloat16).astype(jnp.float32)
            alpha = jnp.exp(m_prev - m_new)
            weights = jnp.exp(scores - m_new)
            if masked:
                weights = jnp.where(allowed, weights, 0.0)
            l_new = alpha * l_prev + jnp.sum(weights, axis=0, keepdims=True)
            contrib = jnp.dot(
                v_t[cut, :], weights.astype(jnp.bfloat16), preferred_element_type=jnp.float32
            )
            slot = request * heads + h
            acc_t[slot] = alpha * acc_t[slot] + contrib
            stats[request, h : h + 1, :] = m_new
            stats[request, heads + h : heads + h + 1, :] = l_new
            stats[request, 2 * heads + h : 2 * heads + h + 1, :] = l_new

    @pl.when(kind == 1)
    def _cached():
        attend(kc_ref, vc_ref, False)

    @pl.when(kind == 2)
    def _fresh():
        attend(kf_ref, vf_ref, True)

    @pl.when(kind == 2)
    def _store_fresh():
        ko_ref[...] = kf_ref[...]
        vo_ref[...] = vf_ref[...]

    @pl.when(kind != 2)
    def _store_cached():
        ko_ref[...] = kc_ref[...]
        vo_ref[...] = vc_ref[...]

    @pl.when(step == pl.num_programs(0) - 1)
    def _emit():
        stat_rows = stats.shape[1]
        for r in range(requests):
            rows = pl.ds(r * span, span)
            for h in range(heads):
                tok_ref[rows, h * head_dim : (h + 1) * head_dim] = acc_t[r * heads + h].T
            block = jnp.concatenate(
                [stats[r], jnp.zeros((lanes - stat_rows, span), jnp.float32)], axis=0
            )
            ml_ref[rows, :] = block.T
        chunks, rows_per, _ = out_ref.shape
        lane = lax.broadcasted_iota(jnp.int32, (rows_per, lanes), 1)
        for d in range(chunks):
            rows = pl.ds(d * rows_per, rows_per)
            out_ref[d, :, :width] = tok_ref[rows, :].astype(jnp.bfloat16)
            ml = ml_ref[rows, :]
            rounded = ml.astype(jnp.bfloat16).astype(jnp.float32)
            packed = jnp.where(
                lane < 2 * heads,
                rounded,
                jnp.where(lane < 3 * heads, ml - rounded, 0.0),
            )
            out_ref[d, :, width:] = packed.astype(jnp.bfloat16)


def local_attention(slot_request, slot_kind, slot_limit, slot_fresh, gathered, kc, vc,
                    heads, head_dim, requests, span, chunks):
    _, tokens, width = gathered.shape
    slot_count = kc.shape[0]
    rows_per = tokens // chunks
    kernel = functools.partial(attend_kernel, heads, head_dim, requests, span)
    flops = 4 * slot_count * span * PAGE * width
    return pl.pallas_call(
        kernel,
        out_shape=(
            jax.ShapeDtypeStruct((chunks, rows_per, width + 128), jnp.bfloat16),
            jax.ShapeDtypeStruct(kc.shape, kc.dtype),
            jax.ShapeDtypeStruct(vc.shape, vc.dtype),
        ),
        grid_spec=pltpu.PrefetchScalarGridSpec(
            num_scalar_prefetch=4,
            grid=(slot_count,),
            in_specs=[
                pl.BlockSpec((1, tokens, width), lambda s, *_: (0, 0, 0),
                             pipeline_mode=pl.Buffered(1)),
                pl.BlockSpec((1, PAGE, width), lambda s, rq, kd, lm, fr: (1, fr[s], 0)),
                pl.BlockSpec((1, PAGE, width), lambda s, rq, kd, lm, fr: (2, fr[s], 0)),
                pl.BlockSpec((1, PAGE, width), lambda s, *_: (s, 0, 0)),
                pl.BlockSpec((1, PAGE, width), lambda s, *_: (s, 0, 0)),
            ],
            out_specs=[
                pl.BlockSpec((chunks, rows_per, width + 128), lambda s, *_: (0, 0, 0)),
                pl.BlockSpec((1, PAGE, width), lambda s, *_: (s, 0, 0)),
                pl.BlockSpec((1, PAGE, width), lambda s, *_: (s, 0, 0)),
            ],
            scratch_shapes=[
                pltpu.VMEM((requests * heads, head_dim, span), jnp.float32),
                pltpu.VMEM((requests, 16, span), jnp.float32),
                pltpu.VMEM((tokens, width), jnp.float32),
                pltpu.VMEM((tokens, 128), jnp.float32),
            ],
        ),
        compiler_params=pltpu.CompilerParams(
            dimension_semantics=("arbitrary",), vmem_limit_bytes=62 * 1024 * 1024
        ),
        cost_estimate=pl.CostEstimate(
            flops=flops,
            transcendentals=slot_count * span * PAGE * heads,
            bytes_accessed=tokens * width * 2 + 4 * kc.size * 2 + tokens * (width + 128) * 2,
        ),
    )(slot_request, slot_kind, slot_limit, slot_fresh, gathered, gathered, gathered, kc, vc)


def combine_kernel(heads, head_dim, recv_ref, w_ref, out_ref, o_acc, l_acc):
    chunks, rows_per, _ = recv_ref.shape
    width = heads * head_dim
    lanes = 128

    def peak_step(d, peak):
        return jnp.maximum(peak, recv_ref[d, :, width:].astype(jnp.float32))

    peak = lax.fori_loop(
        0, chunks, peak_step, jnp.full((rows_per, lanes), mask_score, jnp.float32)
    )
    o_acc[...] = jnp.zeros_like(o_acc)
    l_acc[...] = jnp.zeros_like(l_acc)

    def sum_step(d, carry):
        mld = recv_ref[d, :, width:].astype(jnp.float32)
        factor = jnp.exp(mld - peak)
        for h in range(heads):
            f_h = factor[:, h : h + 1]
            l_h = mld[:, heads + h : heads + h + 1] + mld[:, 2 * heads + h : 2 * heads + h + 1]
            l_acc[:, h : h + 1] += f_h * l_h
            cut = slice(h * head_dim, (h + 1) * head_dim)
            o_acc[:, cut] += f_h * recv_ref[d, :, cut].astype(jnp.float32)
        return carry

    lax.fori_loop(0, chunks, sum_step, 0)
    parts = []
    for h in range(heads):
        cut = slice(h * head_dim, (h + 1) * head_dim)
        parts.append((o_acc[:, cut] / l_acc[:, h : h + 1]).astype(jnp.bfloat16))
    attended = jnp.concatenate(parts, axis=1)
    out_ref[...] = lax.dot_general(
        attended, w_ref[0], (((1,), (1,)), ((), ())), preferred_element_type=jnp.float32
    ).astype(out_ref.dtype)


def combine_project(received, gathered, heads, head_dim):
    chunks, rows_per, _ = received.shape
    _, tokens, width = gathered.shape
    kernel = functools.partial(combine_kernel, heads, head_dim)
    return pl.pallas_call(
        kernel,
        out_shape=jax.ShapeDtypeStruct((rows_per, tokens), jnp.bfloat16),
        grid=(1,),
        in_specs=[
            pl.BlockSpec(received.shape, lambda i: (0, 0, 0)),
            pl.BlockSpec((1, tokens, width), lambda i: (0, 0, 0)),
        ],
        out_specs=pl.BlockSpec((rows_per, tokens), lambda i: (0, 0)),
        scratch_shapes=[
            pltpu.VMEM((rows_per, width), jnp.float32),
            pltpu.VMEM((rows_per, 128), jnp.float32),
        ],
        compiler_params=pltpu.CompilerParams(vmem_limit_bytes=48 * 1024 * 1024),
        cost_estimate=pl.CostEstimate(
            flops=2 * rows_per * tokens * width + 4 * received.size,
            transcendentals=chunks * rows_per * 128,
            bytes_accessed=received.size * 2 + tokens * width * 2 + rows_per * tokens * 2,
        ),
    )(received, gathered)


def pair_merge_kernel(heads, head_dim, packed_hbm, out_ref, mine, theirs, local_sem, send_sem, recv_sem):
    core = lax.axis_index("core")
    partner = 1 - core
    width = heads * head_dim
    lanes = 128
    chunks, rows_per, _ = out_ref.shape

    barrier = pltpu.get_barrier_semaphore()
    pl.semaphore_signal(barrier, inc=1, device_id={"core": partner}, device_id_type=pl.DeviceIdType.MESH)
    pl.semaphore_wait(barrier, 1)

    local = pltpu.make_async_copy(packed_hbm.at[:, core], mine, local_sem)
    local.start()
    remote = pltpu.make_async_remote_copy(
        src_ref=packed_hbm.at[:, partner],
        dst_ref=theirs,
        send_sem=send_sem,
        recv_sem=recv_sem,
        device_id={"core": partner},
        device_id_type=pl.DeviceIdType.MESH,
    )
    remote.start()
    local.wait()
    remote.wait()

    lane = lax.broadcasted_iota(jnp.int32, (rows_per, lanes), 1)

    def merge_step(c, carry):
        ml_a = mine[c, :, width:].astype(jnp.float32)
        ml_b = theirs[c, :, width:].astype(jnp.float32)
        peak = jnp.maximum(ml_a, ml_b)
        f_a = jnp.exp(ml_a - peak)
        f_b = jnp.exp(ml_b - peak)
        merged = jnp.zeros((rows_per, lanes), jnp.float32)
        for h in range(heads):
            cut = slice(h * head_dim, (h + 1) * head_dim)
            fa_h = f_a[:, h : h + 1]
            fb_h = f_b[:, h : h + 1]
            out_ref[c, :, cut] = (
                fa_h * mine[c, :, cut].astype(jnp.float32)
                + fb_h * theirs[c, :, cut].astype(jnp.float32)
            ).astype(out_ref.dtype)
            l_a = ml_a[:, heads + h : heads + h + 1] + ml_a[:, 2 * heads + h : 2 * heads + h + 1]
            l_b = ml_b[:, heads + h : heads + h + 1] + ml_b[:, 2 * heads + h : 2 * heads + h + 1]
            l_h = fa_h * l_a + fb_h * l_b
            l_hi = l_h.astype(jnp.bfloat16).astype(jnp.float32)
            merged = jnp.where(
                lane == h,
                peak[:, h : h + 1],
                jnp.where(
                    lane == heads + h,
                    l_hi,
                    jnp.where(lane == 2 * heads + h, l_h - l_hi, merged),
                ),
            )
        out_ref[c, :, width:] = merged.astype(out_ref.dtype)
        return carry

    lax.fori_loop(0, chunks, merge_step, 0)


def pair_merge(packed, heads, head_dim):
    devices, rows_per, lanes_all = packed.shape
    chips = devices // 2
    view = packed.reshape(chips, 2, rows_per, lanes_all)
    kernel = functools.partial(pair_merge_kernel, heads, head_dim)
    return pl.pallas_call(
        kernel,
        out_shape=jax.ShapeDtypeStruct((chips, rows_per, lanes_all), packed.dtype),
        in_specs=[pl.BlockSpec(memory_space=pl.ANY)],
        out_specs=pl.BlockSpec(memory_space=pltpu.VMEM),
        scratch_shapes=[
            pltpu.VMEM((chips, rows_per, lanes_all), packed.dtype),
            pltpu.VMEM((chips, rows_per, lanes_all), packed.dtype),
            pltpu.SemaphoreType.DMA(()),
            pltpu.SemaphoreType.DMA(()),
            pltpu.SemaphoreType.DMA(()),
        ],
        compiler_params=pltpu.CompilerParams(
            collective_id=0, has_side_effects=True, vmem_limit_bytes=40 * 1024 * 1024
        ),
        cost_estimate=pl.CostEstimate(
            flops=6 * chips * rows_per * lanes_all,
            transcendentals=2 * chips * rows_per * 128,
            bytes_accessed=3 * chips * rows_per * lanes_all * 2,
        ),
    )(view)


def heads_sum_kernel(groups, block, proj_hbm, out_ref, own, received, own_sem, send_sems, recv_sems):
    group = lax.axis_index("heads")
    barrier = pltpu.get_barrier_semaphore()
    for k in range(1, groups):
        pl.semaphore_signal(
            barrier, inc=1, device_id={"heads": lax.rem(group + k, groups)},
            device_id_type=pl.DeviceIdType.MESH,
        )
    pl.semaphore_wait(barrier, groups - 1)
    local = pltpu.make_async_copy(
        proj_hbm.at[:, pl.ds(pl.multiple_of(group * block, 128), block)], own, own_sem
    )
    local.start()
    copies = []
    for k in range(1, groups):
        dest = lax.rem(group + k, groups)
        copy = pltpu.make_async_remote_copy(
            src_ref=proj_hbm.at[:, pl.ds(pl.multiple_of(dest * block, 128), block)],
            dst_ref=received.at[k - 1],
            send_sem=send_sems.at[k - 1],
            recv_sem=recv_sems.at[k - 1],
            device_id={"heads": dest},
            device_id_type=pl.DeviceIdType.MESH,
        )
        copy.start()
        copies.append(copy)
    local.wait()
    for copy in copies:
        copy.wait()
    total = own[...].astype(jnp.float32)
    for k in range(groups - 1):
        total = total + received[k].astype(jnp.float32)
    out_ref[...] = total


def heads_sum(projected, groups):
    rows, cols = projected.shape
    block = cols // groups
    kernel = functools.partial(heads_sum_kernel, groups, block)
    return pl.pallas_call(
        kernel,
        out_shape=jax.ShapeDtypeStruct((rows, block), jnp.float32),
        in_specs=[pl.BlockSpec(memory_space=pl.ANY)],
        out_specs=pl.BlockSpec(memory_space=pltpu.VMEM),
        scratch_shapes=[
            pltpu.VMEM((rows, block), projected.dtype),
            pltpu.VMEM((groups - 1, rows, block), projected.dtype),
            pltpu.SemaphoreType.DMA(()),
            pltpu.SemaphoreType.DMA((groups - 1,)),
            pltpu.SemaphoreType.DMA((groups - 1,)),
        ],
        compiler_params=pltpu.CompilerParams(collective_id=1, has_side_effects=True),
        cost_estimate=pl.CostEstimate(
            flops=groups * rows * block,
            transcendentals=0,
            bytes_accessed=groups * rows * block * 2 + rows * block * 4,
        ),
    )(projected)


def merge_parts_kernel(heads, head_dim, parts_ref, out_ref):
    chunks, parts, rows_per, _ = parts_ref.shape
    width = heads * head_dim
    lanes = 128
    lane = lax.broadcasted_iota(jnp.int32, (rows_per, lanes), 1)

    def merge_step(c, carry):
        stats = [parts_ref[c, j, :, width:].astype(jnp.float32) for j in range(parts)]
        peak = stats[0]
        for j in range(1, parts):
            peak = jnp.maximum(peak, stats[j])
        factors = [jnp.exp(st - peak) for st in stats]
        merged = jnp.zeros((rows_per, lanes), jnp.float32)
        for h in range(heads):
            cut = slice(h * head_dim, (h + 1) * head_dim)
            o_h = jnp.zeros((rows_per, head_dim), jnp.float32)
            l_h = jnp.zeros((rows_per, 1), jnp.float32)
            for j in range(parts):
                f_h = factors[j][:, h : h + 1]
                o_h = o_h + f_h * parts_ref[c, j, :, cut].astype(jnp.float32)
                l_j = (
                    stats[j][:, heads + h : heads + h + 1]
                    + stats[j][:, 2 * heads + h : 2 * heads + h + 1]
                )
                l_h = l_h + f_h * l_j
            out_ref[c, :, cut] = o_h.astype(out_ref.dtype)
            l_hi = l_h.astype(jnp.bfloat16).astype(jnp.float32)
            merged = jnp.where(
                lane == h,
                peak[:, h : h + 1],
                jnp.where(
                    lane == heads + h,
                    l_hi,
                    jnp.where(lane == 2 * heads + h, l_h - l_hi, merged),
                ),
            )
        out_ref[c, :, width:] = merged.astype(out_ref.dtype)
        return carry

    lax.fori_loop(0, chunks, merge_step, 0)


def merge_parts(parts_in, heads, head_dim):
    chunks, parts, rows_per, lanes_all = parts_in.shape
    kernel = functools.partial(merge_parts_kernel, heads, head_dim)
    return pl.pallas_call(
        kernel,
        out_shape=jax.ShapeDtypeStruct((chunks, rows_per, lanes_all), parts_in.dtype),
        grid=(1,),
        in_specs=[pl.BlockSpec(parts_in.shape, lambda i: (0, 0, 0, 0))],
        out_specs=pl.BlockSpec((chunks, rows_per, lanes_all), lambda i: (0, 0, 0)),
        compiler_params=pltpu.CompilerParams(vmem_limit_bytes=32 * 1024 * 1024),
        cost_estimate=pl.CostEstimate(
            flops=4 * parts_in.size,
            transcendentals=chunks * parts * rows_per * 128,
            bytes_accessed=parts_in.size * 2 + chunks * rows_per * lanes_all * 2,
        ),
    )(parts_in)


def per_device(
    queries,
    keys,
    values,
    key_cache,
    value_cache,
    cache_len,
    page_table,
    append_slots,
    out_weight,
    out_bias,
):
    tok_dev, head_count, head_dim = queries.shape
    width = head_count * head_dim
    requests = cache_len.shape[0]
    max_pages = page_table.shape[1]
    new_pages = append_slots.shape[1]
    span_len = new_pages * PAGE
    slot_count = key_cache.shape[0]
    page_devices = lax.axis_size(PAGES)
    device_at = lax.axis_index(PAGES)
    token_ids = device_at * tok_dev + jnp.arange(tok_dev, dtype=jnp.int32)
    request_ids = token_ids // span_len
    request_grid = jnp.arange(requests, dtype=jnp.int32)
    starts = jnp.sum(
        jnp.where(request_ids[:, None] == request_grid[None, :], cache_len[None, :], 0), axis=1
    )
    positions = (starts + token_ids % span_len).astype(jnp.float32)
    rotated_q = rotate(queries.astype(jnp.float32), positions).astype(jnp.bfloat16)
    rotated_k = rotate(keys.astype(jnp.float32), positions).astype(jnp.bfloat16)
    w_cols = out_weight.shape[1]
    w_plane = jnp.pad(out_weight.T, ((0, tok_dev - w_cols), (0, 0)))
    stacked = jnp.stack(
        [
            rotated_q.reshape(tok_dev, width),
            rotated_k.reshape(tok_dev, width),
            values.reshape(tok_dev, width),
        ]
    )
    w_all = lax.all_gather(w_plane[None], PAGES, axis=1, tiled=True)
    gathered = lax.all_gather(stacked, PAGES, axis=1, tiled=True)
    my_slots = device_at * slot_count + jnp.arange(slot_count, dtype=jnp.int32)
    cached_hit = page_table.reshape(-1)[None, :] == my_slots[:, None]
    fresh_hit = append_slots.reshape(-1)[None, :] == my_slots[:, None]
    is_cached = jnp.any(cached_hit, axis=1)
    is_fresh = jnp.any(fresh_hit, axis=1)
    cached_index = jnp.sum(
        jnp.where(cached_hit, jnp.arange(requests * max_pages, dtype=jnp.int32)[None, :], 0), axis=1
    )
    fresh_index = jnp.sum(
        jnp.where(fresh_hit, jnp.arange(requests * new_pages, dtype=jnp.int32)[None, :], 0), axis=1
    )
    slot_request = jnp.where(is_fresh, fresh_index // new_pages, cached_index // max_pages)
    slot_page = jnp.where(is_fresh, fresh_index % new_pages, cached_index % max_pages)
    slot_length = jnp.sum(
        jnp.where(slot_request[:, None] == request_grid[None, :], cache_len[None, :], 0), axis=1
    )
    visible = is_cached & (slot_page * PAGE < slot_length)
    slot_kind = jnp.where(is_fresh, 2, jnp.where(visible, 1, 0)).astype(jnp.int32)
    slot_limit = jnp.where(is_fresh, slot_page * PAGE, -4 * span_len)
    packed, key_slots, value_slots = local_attention(
        slot_request,
        slot_kind,
        slot_limit,
        fresh_index,
        gathered,
        key_cache.reshape(slot_count, PAGE, width),
        value_cache.reshape(slot_count, PAGE, width),
        head_count,
        head_dim,
        requests,
        span_len,
        page_devices,
    )
    paired = pair_merge(packed, head_count, head_dim)
    z_n = lax.axis_size("z")
    y_n = lax.axis_size("y")
    by_y = paired.reshape(z_n, y_n, tok_dev, paired.shape[-1])
    from_y = lax.all_to_all(by_y, "y", 1, 1, tiled=True)
    merged = merge_parts(from_y, head_count, head_dim)
    received = lax.all_to_all(merged, "z", 0, 0, tiled=True)
    projected = combine_project(received, w_all, head_count, head_dim)
    head_groups = lax.axis_size("heads")
    summed = heads_sum(projected, head_groups)
    summed = summed.reshape(tok_dev, page_devices // head_groups, tok_dev)[:, :, :w_cols].reshape(
        tok_dev, (page_devices // head_groups) * w_cols
    )
    key_out = key_slots.reshape(key_cache.shape)
    value_out = value_slots.reshape(value_cache.shape)
    hidden = (summed + out_bias[None, :]).astype(jnp.bfloat16)
    return (hidden, key_out, value_out)


def solution(mesh):
    heads_n, pages_n = mesh.devices.shape
    z_n = pages_n // 8
    split = jax.sharding.Mesh(
        mesh.devices.reshape(heads_n, z_n, 4, 2), ("heads", "z", "y", "core")
    )
    placed = (
        P(PAGES, "heads", None),
        P(PAGES, "heads", None),
        P(PAGES, "heads", None),
        P(PAGES, None, "heads", None),
        P(PAGES, None, "heads", None),
        P(),
        P(),
        P(),
        P("heads", PAGES),
        P("heads"),
    )
    return jax.shard_map(
        per_device,
        mesh=split,
        in_specs=placed,
        out_specs=(
            P(PAGES, "heads"),
            P(PAGES, None, "heads", None),
            P(PAGES, None, "heads", None),
        ),
        check_vma=False,
    )
```

```python
import functools
import math

import jax
import jax.numpy as jnp
from jax import lax
from jax.experimental import pallas as pl
from jax.experimental.pallas import tpu as pltpu
from jax.sharding import PartitionSpec as P

ROT = 32
PAGE = 128
PAGES = ("z", "y", "core")


low_score = -1e30
mask_score = -(2.0 ** 100)


def rotate(vectors, positions):
    half_rot = ROT // 2
    inv_freq = 10000.0 ** (-2.0 * jnp.arange(half_rot, dtype=jnp.float32) / ROT)
    angles = positions[:, None] * inv_freq[None, :]
    cosine = jnp.cos(angles)[:, None, :]
    sine = jnp.sin(angles)[:, None, :]
    first_half = vectors[..., :half_rot]
    second_half = vectors[..., half_rot:ROT]
    return jnp.concatenate(
        [
            first_half * cosine - second_half * sine,
            second_half * cosine + first_half * sine,
            vectors[..., ROT:],
        ],
        axis=-1,
    )


def attend_kernel(
    heads, head_dim, requests, span,
    sreq_ref, skind_ref, slim_ref, sfresh_ref,
    q_ref, kf_ref, vf_ref, kc_ref, vc_ref,
    out_ref, ko_ref, vo_ref, acc_t, stats, tok_ref, ml_ref,
):
    step = pl.program_id(0)
    lanes = ml_ref.shape[1]
    width = heads * head_dim

    @pl.when(step == 0)
    def _init():
        acc_t[...] = jnp.zeros_like(acc_t)
        row = lax.broadcasted_iota(jnp.int32, stats.shape, 1)
        stats[...] = jnp.where(row < heads, mask_score, 0.0).astype(jnp.float32)

    request = sreq_ref[step]
    kind = skind_ref[step]
    limit = slim_ref[step]
    scale = 1.0 / math.sqrt(head_dim)

    def attend(k_ref, v_ref, masked):
        base = pl.multiple_of(request * span, span)
        if masked:
            keys_at = lax.broadcasted_iota(jnp.int32, (PAGE, span), 0)
            queries_at = lax.broadcasted_iota(jnp.int32, (PAGE, span), 1)
            allowed = queries_at - keys_at >= limit
        v_t = v_ref[0].astype(jnp.float32).T.astype(jnp.bfloat16)
        for h in range(heads):
            cut = slice(h * head_dim, (h + 1) * head_dim)
            q_h = q_ref[0, pl.ds(base, span), cut]
            k_h = k_ref[0, :, cut]
            scores = lax.dot_general(
                k_h, q_h, (((1,), (1,)), ((), ())), preferred_element_type=jnp.float32
            ) * scale
            if masked:
                scores = jnp.where(allowed, scores, mask_score)
            m_prev = stats[request, h : h + 1, :]
            l_prev = stats[request, heads + h : heads + h + 1, :]
            m_new = jnp.maximum(m_prev, jnp.max(scores, axis=0, keepdims=True))
            m_new = m_new.astype(jnp.bfloat16).astype(jnp.float32)
            alpha = jnp.exp(m_prev - m_new)
            weights = jnp.exp(scores - m_new)
            if masked:
                weights = jnp.where(allowed, weights, 0.0)
            l_new = alpha * l_prev + jnp.sum(weights, axis=0, keepdims=True)
            contrib = jnp.dot(
                v_t[cut, :], weights.astype(jnp.bfloat16), preferred_element_type=jnp.float32
            )
            slot = request * heads + h
            acc_t[slot] = alpha * acc_t[slot] + contrib
            stats[request, h : h + 1, :] = m_new
            stats[request, heads + h : heads + h + 1, :] = l_new
            stats[request, 2 * heads + h : 2 * heads + h + 1, :] = l_new

    @pl.when(kind == 1)
    def _cached():
        attend(kc_ref, vc_ref, False)

    @pl.when(kind == 2)
    def _fresh():
        attend(kf_ref, vf_ref, True)

    @pl.when(kind == 2)
    def _store_fresh():
        ko_ref[...] = kf_ref[...]
        vo_ref[...] = vf_ref[...]

    @pl.when(kind != 2)
    def _store_cached():
        ko_ref[...] = kc_ref[...]
        vo_ref[...] = vc_ref[...]

    @pl.when(step == pl.num_programs(0) - 1)
    def _emit():
        stat_rows = stats.shape[1]
        for r in range(requests):
            rows = pl.ds(r * span, span)
            for h in range(heads):
                tok_ref[rows, h * head_dim : (h + 1) * head_dim] = acc_t[r * heads + h].T
            block = jnp.concatenate(
                [stats[r], jnp.zeros((lanes - stat_rows, span), jnp.float32)], axis=0
            )
            ml_ref[rows, :] = block.T
        chunks, rows_per, _ = out_ref.shape
        lane = lax.broadcasted_iota(jnp.int32, (rows_per, lanes), 1)
        for d in range(chunks):
            rows = pl.ds(d * rows_per, rows_per)
            out_ref[d, :, :width] = tok_ref[rows, :].astype(jnp.bfloat16)
            ml = ml_ref[rows, :]
            rounded = ml.astype(jnp.bfloat16).astype(jnp.float32)
            packed = jnp.where(
                lane < 2 * heads,
                rounded,
                jnp.where(lane < 3 * heads, ml - rounded, 0.0),
            )
            out_ref[d, :, width:] = packed.astype(jnp.bfloat16)


def local_attention(slot_request, slot_kind, slot_limit, slot_fresh, gathered, kc, vc,
                    heads, head_dim, requests, span, chunks):
    _, tokens, width = gathered.shape
    slot_count = kc.shape[0]
    rows_per = tokens // chunks
    kernel = functools.partial(attend_kernel, heads, head_dim, requests, span)
    flops = 4 * slot_count * span * PAGE * width
    return pl.pallas_call(
        kernel,
        out_shape=(
            jax.ShapeDtypeStruct((chunks, rows_per, width + 128), jnp.bfloat16),
            jax.ShapeDtypeStruct(kc.shape, kc.dtype),
            jax.ShapeDtypeStruct(vc.shape, vc.dtype),
        ),
        grid_spec=pltpu.PrefetchScalarGridSpec(
            num_scalar_prefetch=4,
            grid=(slot_count,),
            in_specs=[
                pl.BlockSpec((1, tokens, width), lambda s, *_: (0, 0, 0),
                             pipeline_mode=pl.Buffered(1)),
                pl.BlockSpec((1, PAGE, width), lambda s, rq, kd, lm, fr: (1, fr[s], 0)),
                pl.BlockSpec((1, PAGE, width), lambda s, rq, kd, lm, fr: (2, fr[s], 0)),
                pl.BlockSpec((1, PAGE, width), lambda s, *_: (s, 0, 0)),
                pl.BlockSpec((1, PAGE, width), lambda s, *_: (s, 0, 0)),
            ],
            out_specs=[
                pl.BlockSpec((chunks, rows_per, width + 128), lambda s, *_: (0, 0, 0)),
                pl.BlockSpec((1, PAGE, width), lambda s, *_: (s, 0, 0)),
                pl.BlockSpec((1, PAGE, width), lambda s, *_: (s, 0, 0)),
            ],
            scratch_shapes=[
                pltpu.VMEM((requests * heads, head_dim, span), jnp.float32),
                pltpu.VMEM((requests, 16, span), jnp.float32),
                pltpu.VMEM((tokens, width), jnp.float32),
                pltpu.VMEM((tokens, 128), jnp.float32),
            ],
        ),
        compiler_params=pltpu.CompilerParams(
            dimension_semantics=("arbitrary",), vmem_limit_bytes=62 * 1024 * 1024
        ),
        cost_estimate=pl.CostEstimate(
            flops=flops,
            transcendentals=slot_count * span * PAGE * heads,
            bytes_accessed=tokens * width * 2 + 4 * kc.size * 2 + tokens * (width + 128) * 2,
        ),
    )(slot_request, slot_kind, slot_limit, slot_fresh, gathered, gathered, gathered, kc, vc)


def combine_kernel(heads, head_dim, recv_ref, w_ref, out_ref, o_acc, l_acc):
    chunks, rows_per, _ = recv_ref.shape
    width = heads * head_dim
    lanes = 128

    def peak_step(d, peak):
        return jnp.maximum(peak, recv_ref[d, :, width:].astype(jnp.float32))

    peak = lax.fori_loop(
        0, chunks, peak_step, jnp.full((rows_per, lanes), mask_score, jnp.float32)
    )
    o_acc[...] = jnp.zeros_like(o_acc)
    l_acc[...] = jnp.zeros_like(l_acc)

    def sum_step(d, carry):
        mld = recv_ref[d, :, width:].astype(jnp.float32)
        factor = jnp.exp(mld - peak)
        for h in range(heads):
            f_h = factor[:, h : h + 1]
            l_h = mld[:, heads + h : heads + h + 1] + mld[:, 2 * heads + h : 2 * heads + h + 1]
            l_acc[:, h : h + 1] += f_h * l_h
            cut = slice(h * head_dim, (h + 1) * head_dim)
            o_acc[:, cut] += f_h * recv_ref[d, :, cut].astype(jnp.float32)
        return carry

    lax.fori_loop(0, chunks, sum_step, 0)
    parts = []
    for h in range(heads):
        cut = slice(h * head_dim, (h + 1) * head_dim)
        parts.append((o_acc[:, cut] / l_acc[:, h : h + 1]).astype(jnp.bfloat16))
    attended = jnp.concatenate(parts, axis=1)
    out_ref[...] = lax.dot_general(
        attended, w_ref[0], (((1,), (1,)), ((), ())), preferred_element_type=jnp.float32
    ).astype(out_ref.dtype)


def combine_project(received, gathered, heads, head_dim):
    chunks, rows_per, _ = received.shape
    _, tokens, width = gathered.shape
    kernel = functools.partial(combine_kernel, heads, head_dim)
    return pl.pallas_call(
        kernel,
        out_shape=jax.ShapeDtypeStruct((rows_per, tokens), jnp.bfloat16),
        grid=(1,),
        in_specs=[
            pl.BlockSpec(received.shape, lambda i: (0, 0, 0)),
            pl.BlockSpec((1, tokens, width), lambda i: (0, 0, 0)),
        ],
        out_specs=pl.BlockSpec((rows_per, tokens), lambda i: (0, 0)),
        scratch_shapes=[
            pltpu.VMEM((rows_per, width), jnp.float32),
            pltpu.VMEM((rows_per, 128), jnp.float32),
        ],
        compiler_params=pltpu.CompilerParams(vmem_limit_bytes=48 * 1024 * 1024),
        cost_estimate=pl.CostEstimate(
            flops=2 * rows_per * tokens * width + 4 * received.size,
            transcendentals=chunks * rows_per * 128,
            bytes_accessed=received.size * 2 + tokens * width * 2 + rows_per * tokens * 2,
        ),
    )(received, gathered)


def pair_merge_kernel(heads, head_dim, packed_hbm, out_ref, mine, theirs, local_sem, send_sem, recv_sem):
    core = lax.axis_index("core")
    partner = 1 - core
    width = heads * head_dim
    lanes = 128
    chunks, rows_per, _ = out_ref.shape

    barrier = pltpu.get_barrier_semaphore()
    pl.semaphore_signal(barrier, inc=1, device_id={"core": partner}, device_id_type=pl.DeviceIdType.MESH)
    pl.semaphore_wait(barrier, 1)

    local = pltpu.make_async_copy(packed_hbm.at[:, core], mine, local_sem)
    local.start()
    remote = pltpu.make_async_remote_copy(
        src_ref=packed_hbm.at[:, partner],
        dst_ref=theirs,
        send_sem=send_sem,
        recv_sem=recv_sem,
        device_id={"core": partner},
        device_id_type=pl.DeviceIdType.MESH,
    )
    remote.start()
    local.wait()
    remote.wait()

    lane = lax.broadcasted_iota(jnp.int32, (rows_per, lanes), 1)

    def merge_step(c, carry):
        ml_a = mine[c, :, width:].astype(jnp.float32)
        ml_b = theirs[c, :, width:].astype(jnp.float32)
        peak = jnp.maximum(ml_a, ml_b)
        f_a = jnp.exp(ml_a - peak)
        f_b = jnp.exp(ml_b - peak)
        merged = jnp.zeros((rows_per, lanes), jnp.float32)
        for h in range(heads):
            cut = slice(h * head_dim, (h + 1) * head_dim)
            fa_h = f_a[:, h : h + 1]
            fb_h = f_b[:, h : h + 1]
            out_ref[c, :, cut] = (
                fa_h * mine[c, :, cut].astype(jnp.float32)
                + fb_h * theirs[c, :, cut].astype(jnp.float32)
            ).astype(out_ref.dtype)
            l_a = ml_a[:, heads + h : heads + h + 1] + ml_a[:, 2 * heads + h : 2 * heads + h + 1]
            l_b = ml_b[:, heads + h : heads + h + 1] + ml_b[:, 2 * heads + h : 2 * heads + h + 1]
            l_h = fa_h * l_a + fb_h * l_b
            l_hi = l_h.astype(jnp.bfloat16).astype(jnp.float32)
            merged = jnp.where(
                lane == h,
                peak[:, h : h + 1],
                jnp.where(
                    lane == heads + h,
                    l_hi,
                    jnp.where(lane == 2 * heads + h, l_h - l_hi, merged),
                ),
            )
        out_ref[c, :, width:] = merged.astype(out_ref.dtype)
        return carry

    lax.fori_loop(0, chunks, merge_step, 0)


def pair_merge(packed, heads, head_dim):
    devices, rows_per, lanes_all = packed.shape
    chips = devices // 2
    view = packed.reshape(chips, 2, rows_per, lanes_all)
    kernel = functools.partial(pair_merge_kernel, heads, head_dim)
    return pl.pallas_call(
        kernel,
        out_shape=jax.ShapeDtypeStruct((chips, rows_per, lanes_all), packed.dtype),
        in_specs=[pl.BlockSpec(memory_space=pl.ANY)],
        out_specs=pl.BlockSpec(memory_space=pltpu.VMEM),
        scratch_shapes=[
            pltpu.VMEM((chips, rows_per, lanes_all), packed.dtype),
            pltpu.VMEM((chips, rows_per, lanes_all), packed.dtype),
            pltpu.SemaphoreType.DMA(()),
            pltpu.SemaphoreType.DMA(()),
            pltpu.SemaphoreType.DMA(()),
        ],
        compiler_params=pltpu.CompilerParams(
            collective_id=0, has_side_effects=True, vmem_limit_bytes=40 * 1024 * 1024
        ),
        cost_estimate=pl.CostEstimate(
            flops=6 * chips * rows_per * lanes_all,
            transcendentals=2 * chips * rows_per * 128,
            bytes_accessed=3 * chips * rows_per * lanes_all * 2,
        ),
    )(view)


def heads_sum_kernel(groups, block, proj_hbm, out_ref, own, received, own_sem, send_sems, recv_sems):
    group = lax.axis_index("heads")
    barrier = pltpu.get_barrier_semaphore()
    for k in range(1, groups):
        pl.semaphore_signal(
            barrier, inc=1, device_id={"heads": lax.rem(group + k, groups)},
            device_id_type=pl.DeviceIdType.MESH,
        )
    pl.semaphore_wait(barrier, groups - 1)
    local = pltpu.make_async_copy(
        proj_hbm.at[:, pl.ds(pl.multiple_of(group * block, 128), block)], own, own_sem
    )
    local.start()
    copies = []
    for k in range(1, groups):
        dest = lax.rem(group + k, groups)
        copy = pltpu.make_async_remote_copy(
            src_ref=proj_hbm.at[:, pl.ds(pl.multiple_of(dest * block, 128), block)],
            dst_ref=received.at[k - 1],
            send_sem=send_sems.at[k - 1],
            recv_sem=recv_sems.at[k - 1],
            device_id={"heads": dest},
            device_id_type=pl.DeviceIdType.MESH,
        )
        copy.start()
        copies.append(copy)
    local.wait()
    for copy in copies:
        copy.wait()
    total = own[...].astype(jnp.float32)
    for k in range(groups - 1):
        total = total + received[k].astype(jnp.float32)
    out_ref[...] = total


def heads_sum(projected, groups):
    rows, cols = projected.shape
    block = cols // groups
    kernel = functools.partial(heads_sum_kernel, groups, block)
    return pl.pallas_call(
        kernel,
        out_shape=jax.ShapeDtypeStruct((rows, block), jnp.float32),
        in_specs=[pl.BlockSpec(memory_space=pl.ANY)],
        out_specs=pl.BlockSpec(memory_space=pltpu.VMEM),
        scratch_shapes=[
            pltpu.VMEM((rows, block), projected.dtype),
            pltpu.VMEM((groups - 1, rows, block), projected.dtype),
            pltpu.SemaphoreType.DMA(()),
            pltpu.SemaphoreType.DMA((groups - 1,)),
            pltpu.SemaphoreType.DMA((groups - 1,)),
        ],
        compiler_params=pltpu.CompilerParams(collective_id=1, has_side_effects=True),
        cost_estimate=pl.CostEstimate(
            flops=groups * rows * block,
            transcendentals=0,
            bytes_accessed=groups * rows * block * 2 + rows * block * 4,
        ),
    )(projected)


def merge_chunk(heads, head_dim, parts, get_part, out_ref, c):
    rows_per = out_ref.shape[1]
    width = heads * head_dim
    lanes = 128
    lane = lax.broadcasted_iota(jnp.int32, (rows_per, lanes), 1)
    stats = [get_part(j, c, slice(width, width + lanes)).astype(jnp.float32) for j in range(parts)]
    peak = stats[0]
    for j in range(1, parts):
        peak = jnp.maximum(peak, stats[j])
    factors = [jnp.exp(st - peak) for st in stats]
    merged = jnp.zeros((rows_per, lanes), jnp.float32)
    for h in range(heads):
        cut = slice(h * head_dim, (h + 1) * head_dim)
        o_h = jnp.zeros((rows_per, head_dim), jnp.float32)
        l_h = jnp.zeros((rows_per, 1), jnp.float32)
        for j in range(parts):
            f_h = factors[j][:, h : h + 1]
            o_h = o_h + f_h * get_part(j, c, cut).astype(jnp.float32)
            l_j = (
                stats[j][:, heads + h : heads + h + 1]
                + stats[j][:, 2 * heads + h : 2 * heads + h + 1]
            )
            l_h = l_h + f_h * l_j
        out_ref[c, :, cut] = o_h.astype(out_ref.dtype)
        l_hi = l_h.astype(jnp.bfloat16).astype(jnp.float32)
        merged = jnp.where(
            lane == h,
            peak[:, h : h + 1],
            jnp.where(
                lane == heads + h,
                l_hi,
                jnp.where(lane == 2 * heads + h, l_h - l_hi, merged),
            ),
        )
    out_ref[c, :, width:] = merged.astype(out_ref.dtype)


def y_exchange_kernel(heads, head_dim, groups, src_hbm, out_ref, parts, own_sem, send_sems, recv_sems):
    me = lax.axis_index("y")
    chunks = out_ref.shape[0]
    barrier = pltpu.get_barrier_semaphore()
    for k in range(1, groups):
        pl.semaphore_signal(
            barrier, inc=1, device_id={"y": lax.rem(me + k, groups)},
            device_id_type=pl.DeviceIdType.MESH,
        )
    pl.semaphore_wait(barrier, groups - 1)
    local = pltpu.make_async_copy(src_hbm.at[:, me], parts.at[0], own_sem)
    local.start()
    copies = []
    for k in range(1, groups):
        dest = lax.rem(me + k, groups)
        copy = pltpu.make_async_remote_copy(
            src_ref=src_hbm.at[:, dest],
            dst_ref=parts.at[k],
            send_sem=send_sems.at[k - 1],
            recv_sem=recv_sems.at[k - 1],
            device_id={"y": dest},
            device_id_type=pl.DeviceIdType.MESH,
        )
        copy.start()
        copies.append(copy)
    local.wait()
    for copy in copies:
        copy.wait()

    def get_part(j, c, cut):
        return parts[j, c, :, cut]

    def step(c, carry):
        merge_chunk(heads, head_dim, groups, get_part, out_ref, c)
        return carry

    lax.fori_loop(0, chunks, step, 0)


def y_exchange(by_y, heads, head_dim):
    chunks, groups, rows_per, lanes_all = by_y.shape
    kernel = functools.partial(y_exchange_kernel, heads, head_dim, groups)
    return pl.pallas_call(
        kernel,
        out_shape=jax.ShapeDtypeStruct((chunks, rows_per, lanes_all), by_y.dtype),
        in_specs=[pl.BlockSpec(memory_space=pl.ANY)],
        out_specs=pl.BlockSpec(memory_space=pltpu.VMEM),
        scratch_shapes=[
            pltpu.VMEM((groups, chunks, rows_per, lanes_all), by_y.dtype),
            pltpu.SemaphoreType.DMA(()),
            pltpu.SemaphoreType.DMA((groups - 1,)),
            pltpu.SemaphoreType.DMA((groups - 1,)),
        ],
        compiler_params=pltpu.CompilerParams(
            collective_id=2, has_side_effects=True, vmem_limit_bytes=32 * 1024 * 1024
        ),
        cost_estimate=pl.CostEstimate(
            flops=4 * by_y.size,
            transcendentals=chunks * groups * rows_per * 128,
            bytes_accessed=2 * by_y.size * 2,
        ),
    )(by_y)


def per_device(
    queries,
    keys,
    values,
    key_cache,
    value_cache,
    cache_len,
    page_table,
    append_slots,
    out_weight,
    out_bias,
):
    tok_dev, head_count, head_dim = queries.shape
    width = head_count * head_dim
    requests = cache_len.shape[0]
    max_pages = page_table.shape[1]
    new_pages = append_slots.shape[1]
    span_len = new_pages * PAGE
    slot_count = key_cache.shape[0]
    page_devices = lax.axis_size(PAGES)
    device_at = lax.axis_index(PAGES)
    token_ids = device_at * tok_dev + jnp.arange(tok_dev, dtype=jnp.int32)
    request_ids = token_ids // span_len
    request_grid = jnp.arange(requests, dtype=jnp.int32)
    starts = jnp.sum(
        jnp.where(request_ids[:, None] == request_grid[None, :], cache_len[None, :], 0), axis=1
    )
    positions = (starts + token_ids % span_len).astype(jnp.float32)
    rotated_q = rotate(queries.astype(jnp.float32), positions).astype(jnp.bfloat16)
    rotated_k = rotate(keys.astype(jnp.float32), positions).astype(jnp.bfloat16)
    w_cols = out_weight.shape[1]
    w_plane = jnp.pad(out_weight.T, ((0, tok_dev - w_cols), (0, 0)))
    stacked = jnp.stack(
        [
            rotated_q.reshape(tok_dev, width),
            rotated_k.reshape(tok_dev, width),
            values.reshape(tok_dev, width),
        ]
    )
    w_all = lax.all_gather(w_plane[None], PAGES, axis=1, tiled=True)
    gathered = lax.all_gather(stacked, PAGES, axis=1, tiled=True)
    my_slots = device_at * slot_count + jnp.arange(slot_count, dtype=jnp.int32)
    cached_hit = page_table.reshape(-1)[None, :] == my_slots[:, None]
    fresh_hit = append_slots.reshape(-1)[None, :] == my_slots[:, None]
    is_cached = jnp.any(cached_hit, axis=1)
    is_fresh = jnp.any(fresh_hit, axis=1)
    cached_index = jnp.sum(
        jnp.where(cached_hit, jnp.arange(requests * max_pages, dtype=jnp.int32)[None, :], 0), axis=1
    )
    fresh_index = jnp.sum(
        jnp.where(fresh_hit, jnp.arange(requests * new_pages, dtype=jnp.int32)[None, :], 0), axis=1
    )
    slot_request = jnp.where(is_fresh, fresh_index // new_pages, cached_index // max_pages)
    slot_page = jnp.where(is_fresh, fresh_index % new_pages, cached_index % max_pages)
    slot_length = jnp.sum(
        jnp.where(slot_request[:, None] == request_grid[None, :], cache_len[None, :], 0), axis=1
    )
    visible = is_cached & (slot_page * PAGE < slot_length)
    slot_kind = jnp.where(is_fresh, 2, jnp.where(visible, 1, 0)).astype(jnp.int32)
    slot_limit = jnp.where(is_fresh, slot_page * PAGE, -4 * span_len)
    packed, key_slots, value_slots = local_attention(
        slot_request,
        slot_kind,
        slot_limit,
        fresh_index,
        gathered,
        key_cache.reshape(slot_count, PAGE, width),
        value_cache.reshape(slot_count, PAGE, width),
        head_count,
        head_dim,
        requests,
        span_len,
        page_devices,
    )
    paired = pair_merge(packed, head_count, head_dim)
    z_n = lax.axis_size("z")
    y_n = lax.axis_size("y")
    by_y = paired.reshape(z_n, y_n, tok_dev, paired.shape[-1])
    merged = y_exchange(by_y, head_count, head_dim)
    received = lax.all_to_all(merged, "z", 0, 0, tiled=True)
    projected = combine_project(received, w_all, head_count, head_dim)
    head_groups = lax.axis_size("heads")
    summed = heads_sum(projected, head_groups)
    summed = summed.reshape(tok_dev, page_devices // head_groups, tok_dev)[:, :, :w_cols].reshape(
        tok_dev, (page_devices // head_groups) * w_cols
    )
    key_out = key_slots.reshape(key_cache.shape)
    value_out = value_slots.reshape(value_cache.shape)
    hidden = (summed + out_bias[None, :]).astype(jnp.bfloat16)
    return (hidden, key_out, value_out)


def solution(mesh):
    heads_n, pages_n = mesh.devices.shape
    z_n = pages_n // 8
    split = jax.sharding.Mesh(
        mesh.devices.reshape(heads_n, z_n, 4, 2), ("heads", "z", "y", "core")
    )
    placed = (
        P(PAGES, "heads", None),
        P(PAGES, "heads", None),
        P(PAGES, "heads", None),
        P(PAGES, None, "heads", None),
        P(PAGES, None, "heads", None),
        P(),
        P(),
        P(),
        P("heads", PAGES),
        P("heads"),
    )
    return jax.shard_map(
        per_device,
        mesh=split,
        in_specs=placed,
        out_specs=(
            P(PAGES, "heads"),
            P(PAGES, None, "heads", None),
            P(PAGES, None, "heads", None),
        ),
        check_vma=False,
    )
```

```python
import functools
import math

import jax
import jax.numpy as jnp
from jax import lax
from jax.experimental import pallas as pl
from jax.experimental.pallas import tpu as pltpu
from jax.sharding import PartitionSpec as P

ROT = 32
PAGE = 128
PAGES = ("z", "y", "core")


low_score = -1e30
mask_score = -(2.0 ** 100)


def rotate(vectors, positions):
    half_rot = ROT // 2
    inv_freq = 10000.0 ** (-2.0 * jnp.arange(half_rot, dtype=jnp.float32) / ROT)
    angles = positions[:, None] * inv_freq[None, :]
    cosine = jnp.cos(angles)[:, None, :]
    sine = jnp.sin(angles)[:, None, :]
    first_half = vectors[..., :half_rot]
    second_half = vectors[..., half_rot:ROT]
    return jnp.concatenate(
        [
            first_half * cosine - second_half * sine,
            second_half * cosine + first_half * sine,
            vectors[..., ROT:],
        ],
        axis=-1,
    )


def attend_kernel(
    heads, head_dim, requests, span,
    sreq_ref, skind_ref, slim_ref, sfresh_ref,
    q_ref, kf_ref, vf_ref, kc_ref, vc_ref,
    out_ref, ko_ref, vo_ref, acc_t, stats, tok_ref, ml_ref,
):
    step = pl.program_id(0)
    lanes = ml_ref.shape[1]
    width = heads * head_dim

    @pl.when(step == 0)
    def _init():
        acc_t[...] = jnp.zeros_like(acc_t)
        row = lax.broadcasted_iota(jnp.int32, stats.shape, 1)
        stats[...] = jnp.where(row < heads, mask_score, 0.0).astype(jnp.float32)

    request = sreq_ref[step]
    kind = skind_ref[step]
    limit = slim_ref[step]
    scale = 1.0 / math.sqrt(head_dim)

    def attend(k_ref, v_ref, masked):
        base = pl.multiple_of(request * span, span)
        if masked:
            keys_at = lax.broadcasted_iota(jnp.int32, (PAGE, span), 0)
            queries_at = lax.broadcasted_iota(jnp.int32, (PAGE, span), 1)
            allowed = queries_at - keys_at >= limit
        v_t = v_ref[0].astype(jnp.float32).T.astype(jnp.bfloat16)
        for h in range(heads):
            cut = slice(h * head_dim, (h + 1) * head_dim)
            q_h = q_ref[0, pl.ds(base, span), cut]
            k_h = k_ref[0, :, cut]
            scores = lax.dot_general(
                k_h, q_h, (((1,), (1,)), ((), ())), preferred_element_type=jnp.float32
            ) * scale
            if masked:
                scores = jnp.where(allowed, scores, mask_score)
            m_prev = stats[request, h : h + 1, :]
            l_prev = stats[request, heads + h : heads + h + 1, :]
            m_new = jnp.maximum(m_prev, jnp.max(scores, axis=0, keepdims=True))
            m_new = m_new.astype(jnp.bfloat16).astype(jnp.float32)
            alpha = jnp.exp(m_prev - m_new)
            weights = jnp.exp(scores - m_new)
            if masked:
                weights = jnp.where(allowed, weights, 0.0)
            l_new = alpha * l_prev + jnp.sum(weights, axis=0, keepdims=True)
            contrib = jnp.dot(
                v_t[cut, :], weights.astype(jnp.bfloat16), preferred_element_type=jnp.float32
            )
            slot = request * heads + h
            acc_t[slot] = alpha * acc_t[slot] + contrib
            stats[request, h : h + 1, :] = m_new
            stats[request, heads + h : heads + h + 1, :] = l_new
            stats[request, 2 * heads + h : 2 * heads + h + 1, :] = l_new

    @pl.when(kind == 1)
    def _cached():
        attend(kc_ref, vc_ref, False)

    @pl.when(kind == 2)
    def _fresh():
        attend(kf_ref, vf_ref, True)

    @pl.when(kind == 2)
    def _store_fresh():
        ko_ref[...] = kf_ref[...]
        vo_ref[...] = vf_ref[...]

    @pl.when(kind != 2)
    def _store_cached():
        ko_ref[...] = kc_ref[...]
        vo_ref[...] = vc_ref[...]

    @pl.when(step == pl.num_programs(0) - 1)
    def _emit():
        stat_rows = stats.shape[1]
        for r in range(requests):
            rows = pl.ds(r * span, span)
            for h in range(heads):
                tok_ref[rows, h * head_dim : (h + 1) * head_dim] = acc_t[r * heads + h].T
            block = jnp.concatenate(
                [stats[r], jnp.zeros((lanes - stat_rows, span), jnp.float32)], axis=0
            )
            ml_ref[rows, :] = block.T
        chunks, rows_per, _ = out_ref.shape
        lane = lax.broadcasted_iota(jnp.int32, (rows_per, lanes), 1)
        for d in range(chunks):
            rows = pl.ds(d * rows_per, rows_per)
            out_ref[d, :, :width] = tok_ref[rows, :].astype(jnp.bfloat16)
            ml = ml_ref[rows, :]
            rounded = ml.astype(jnp.bfloat16).astype(jnp.float32)
            packed = jnp.where(
                lane < 2 * heads,
                rounded,
                jnp.where(lane < 3 * heads, ml - rounded, 0.0),
            )
            out_ref[d, :, width:] = packed.astype(jnp.bfloat16)


def local_attention(slot_request, slot_kind, slot_limit, slot_fresh, gathered, kc, vc,
                    heads, head_dim, requests, span, chunks):
    _, tokens, width = gathered.shape
    slot_count = kc.shape[0]
    rows_per = tokens // chunks
    kernel = functools.partial(attend_kernel, heads, head_dim, requests, span)
    flops = 4 * slot_count * span * PAGE * width
    return pl.pallas_call(
        kernel,
        out_shape=(
            jax.ShapeDtypeStruct((chunks, rows_per, width + 128), jnp.bfloat16),
            jax.ShapeDtypeStruct(kc.shape, kc.dtype),
            jax.ShapeDtypeStruct(vc.shape, vc.dtype),
        ),
        grid_spec=pltpu.PrefetchScalarGridSpec(
            num_scalar_prefetch=4,
            grid=(slot_count,),
            in_specs=[
                pl.BlockSpec((1, tokens, width), lambda s, *_: (0, 0, 0),
                             pipeline_mode=pl.Buffered(1)),
                pl.BlockSpec((1, PAGE, width), lambda s, rq, kd, lm, fr: (1, fr[s], 0)),
                pl.BlockSpec((1, PAGE, width), lambda s, rq, kd, lm, fr: (2, fr[s], 0)),
                pl.BlockSpec((1, PAGE, width), lambda s, *_: (s, 0, 0)),
                pl.BlockSpec((1, PAGE, width), lambda s, *_: (s, 0, 0)),
            ],
            out_specs=[
                pl.BlockSpec((chunks, rows_per, width + 128), lambda s, *_: (0, 0, 0)),
                pl.BlockSpec((1, PAGE, width), lambda s, *_: (s, 0, 0)),
                pl.BlockSpec((1, PAGE, width), lambda s, *_: (s, 0, 0)),
            ],
            scratch_shapes=[
                pltpu.VMEM((requests * heads, head_dim, span), jnp.float32),
                pltpu.VMEM((requests, 16, span), jnp.float32),
                pltpu.VMEM((tokens, width), jnp.float32),
                pltpu.VMEM((tokens, 128), jnp.float32),
            ],
        ),
        compiler_params=pltpu.CompilerParams(
            dimension_semantics=("arbitrary",), vmem_limit_bytes=62 * 1024 * 1024
        ),
        cost_estimate=pl.CostEstimate(
            flops=flops,
            transcendentals=slot_count * span * PAGE * heads,
            bytes_accessed=tokens * width * 2 + 4 * kc.size * 2 + tokens * (width + 128) * 2,
        ),
    )(slot_request, slot_kind, slot_limit, slot_fresh, gathered, gathered, gathered, kc, vc)


def combine_kernel(heads, head_dim, recv_ref, w_ref, out_ref, o_acc, l_acc):
    chunks, rows_per, _ = recv_ref.shape
    width = heads * head_dim
    lanes = 128

    def peak_step(d, peak):
        return jnp.maximum(peak, recv_ref[d, :, width:].astype(jnp.float32))

    peak = lax.fori_loop(
        0, chunks, peak_step, jnp.full((rows_per, lanes), mask_score, jnp.float32)
    )
    o_acc[...] = jnp.zeros_like(o_acc)
    l_acc[...] = jnp.zeros_like(l_acc)

    def sum_step(d, carry):
        mld = recv_ref[d, :, width:].astype(jnp.float32)
        factor = jnp.exp(mld - peak)
        for h in range(heads):
            f_h = factor[:, h : h + 1]
            l_h = mld[:, heads + h : heads + h + 1] + mld[:, 2 * heads + h : 2 * heads + h + 1]
            l_acc[:, h : h + 1] += f_h * l_h
            cut = slice(h * head_dim, (h + 1) * head_dim)
            o_acc[:, cut] += f_h * recv_ref[d, :, cut].astype(jnp.float32)
        return carry

    lax.fori_loop(0, chunks, sum_step, 0)
    parts = []
    for h in range(heads):
        cut = slice(h * head_dim, (h + 1) * head_dim)
        parts.append((o_acc[:, cut] / l_acc[:, h : h + 1]).astype(jnp.bfloat16))
    attended = jnp.concatenate(parts, axis=1)
    out_ref[...] = lax.dot_general(
        attended, w_ref[0], (((1,), (1,)), ((), ())), preferred_element_type=jnp.float32
    ).astype(out_ref.dtype)


def combine_project(received, gathered, heads, head_dim):
    chunks, rows_per, _ = received.shape
    _, tokens, width = gathered.shape
    kernel = functools.partial(combine_kernel, heads, head_dim)
    return pl.pallas_call(
        kernel,
        out_shape=jax.ShapeDtypeStruct((rows_per, tokens), jnp.bfloat16),
        grid=(1,),
        in_specs=[
            pl.BlockSpec(received.shape, lambda i: (0, 0, 0)),
            pl.BlockSpec((1, tokens, width), lambda i: (0, 0, 0)),
        ],
        out_specs=pl.BlockSpec((rows_per, tokens), lambda i: (0, 0)),
        scratch_shapes=[
            pltpu.VMEM((rows_per, width), jnp.float32),
            pltpu.VMEM((rows_per, 128), jnp.float32),
        ],
        compiler_params=pltpu.CompilerParams(vmem_limit_bytes=48 * 1024 * 1024),
        cost_estimate=pl.CostEstimate(
            flops=2 * rows_per * tokens * width + 4 * received.size,
            transcendentals=chunks * rows_per * 128,
            bytes_accessed=received.size * 2 + tokens * width * 2 + rows_per * tokens * 2,
        ),
    )(received, gathered)


def pair_merge_kernel(heads, head_dim, packed_hbm, out_ref, mine, theirs, local_sem, send_sem, recv_sem):
    core = lax.axis_index("core")
    partner = 1 - core
    width = heads * head_dim
    lanes = 128
    chunks, rows_per, _ = out_ref.shape

    barrier = pltpu.get_barrier_semaphore()
    pl.semaphore_signal(barrier, inc=1, device_id={"core": partner}, device_id_type=pl.DeviceIdType.MESH)
    pl.semaphore_wait(barrier, 1)

    local = pltpu.make_async_copy(packed_hbm.at[:, core], mine, local_sem)
    local.start()
    remote = pltpu.make_async_remote_copy(
        src_ref=packed_hbm.at[:, partner],
        dst_ref=theirs,
        send_sem=send_sem,
        recv_sem=recv_sem,
        device_id={"core": partner},
        device_id_type=pl.DeviceIdType.MESH,
    )
    remote.start()
    local.wait()
    remote.wait()

    lane = lax.broadcasted_iota(jnp.int32, (rows_per, lanes), 1)

    def merge_step(c, carry):
        ml_a = mine[c, :, width:].astype(jnp.float32)
        ml_b = theirs[c, :, width:].astype(jnp.float32)
        peak = jnp.maximum(ml_a, ml_b)
        f_a = jnp.exp(ml_a - peak)
        f_b = jnp.exp(ml_b - peak)
        merged = jnp.zeros((rows_per, lanes), jnp.float32)
        for h in range(heads):
            cut = slice(h * head_dim, (h + 1) * head_dim)
            fa_h = f_a[:, h : h + 1]
            fb_h = f_b[:, h : h + 1]
            out_ref[c, :, cut] = (
                fa_h * mine[c, :, cut].astype(jnp.float32)
                + fb_h * theirs[c, :, cut].astype(jnp.float32)
            ).astype(out_ref.dtype)
            l_a = ml_a[:, heads + h : heads + h + 1] + ml_a[:, 2 * heads + h : 2 * heads + h + 1]
            l_b = ml_b[:, heads + h : heads + h + 1] + ml_b[:, 2 * heads + h : 2 * heads + h + 1]
            l_h = fa_h * l_a + fb_h * l_b
            l_hi = l_h.astype(jnp.bfloat16).astype(jnp.float32)
            merged = jnp.where(
                lane == h,
                peak[:, h : h + 1],
                jnp.where(
                    lane == heads + h,
                    l_hi,
                    jnp.where(lane == 2 * heads + h, l_h - l_hi, merged),
                ),
            )
        out_ref[c, :, width:] = merged.astype(out_ref.dtype)
        return carry

    lax.fori_loop(0, chunks, merge_step, 0)


def pair_merge(packed, heads, head_dim):
    devices, rows_per, lanes_all = packed.shape
    chips = devices // 2
    view = packed.reshape(chips, 2, rows_per, lanes_all)
    kernel = functools.partial(pair_merge_kernel, heads, head_dim)
    return pl.pallas_call(
        kernel,
        out_shape=jax.ShapeDtypeStruct((chips, rows_per, lanes_all), packed.dtype),
        in_specs=[pl.BlockSpec(memory_space=pl.ANY)],
        out_specs=pl.BlockSpec(memory_space=pltpu.VMEM),
        scratch_shapes=[
            pltpu.VMEM((chips, rows_per, lanes_all), packed.dtype),
            pltpu.VMEM((chips, rows_per, lanes_all), packed.dtype),
            pltpu.SemaphoreType.DMA(()),
            pltpu.SemaphoreType.DMA(()),
            pltpu.SemaphoreType.DMA(()),
        ],
        compiler_params=pltpu.CompilerParams(
            collective_id=0, has_side_effects=True, vmem_limit_bytes=40 * 1024 * 1024
        ),
        cost_estimate=pl.CostEstimate(
            flops=6 * chips * rows_per * lanes_all,
            transcendentals=2 * chips * rows_per * 128,
            bytes_accessed=3 * chips * rows_per * lanes_all * 2,
        ),
    )(view)


def heads_sum_kernel(groups, block, proj_hbm, out_ref, own, received, own_sem, send_sems, recv_sems):
    group = lax.axis_index("heads")
    barrier = pltpu.get_barrier_semaphore()
    for k in range(1, groups):
        pl.semaphore_signal(
            barrier, inc=1, device_id={"heads": lax.rem(group + k, groups)},
            device_id_type=pl.DeviceIdType.MESH,
        )
    pl.semaphore_wait(barrier, groups - 1)
    local = pltpu.make_async_copy(
        proj_hbm.at[:, pl.ds(pl.multiple_of(group * block, 128), block)], own, own_sem
    )
    local.start()
    copies = []
    for k in range(1, groups):
        dest = lax.rem(group + k, groups)
        copy = pltpu.make_async_remote_copy(
            src_ref=proj_hbm.at[:, pl.ds(pl.multiple_of(dest * block, 128), block)],
            dst_ref=received.at[k - 1],
            send_sem=send_sems.at[k - 1],
            recv_sem=recv_sems.at[k - 1],
            device_id={"heads": dest},
            device_id_type=pl.DeviceIdType.MESH,
        )
        copy.start()
        copies.append(copy)
    local.wait()
    for copy in copies:
        copy.wait()
    total = own[...].astype(jnp.float32)
    for k in range(groups - 1):
        total = total + received[k].astype(jnp.float32)
    out_ref[...] = total


def heads_sum(projected, groups):
    rows, cols = projected.shape
    block = cols // groups
    kernel = functools.partial(heads_sum_kernel, groups, block)
    return pl.pallas_call(
        kernel,
        out_shape=jax.ShapeDtypeStruct((rows, block), jnp.float32),
        in_specs=[pl.BlockSpec(memory_space=pl.ANY)],
        out_specs=pl.BlockSpec(memory_space=pltpu.VMEM),
        scratch_shapes=[
            pltpu.VMEM((rows, block), projected.dtype),
            pltpu.VMEM((groups - 1, rows, block), projected.dtype),
            pltpu.SemaphoreType.DMA(()),
            pltpu.SemaphoreType.DMA((groups - 1,)),
            pltpu.SemaphoreType.DMA((groups - 1,)),
        ],
        compiler_params=pltpu.CompilerParams(collective_id=1, has_side_effects=True),
        cost_estimate=pl.CostEstimate(
            flops=groups * rows * block,
            transcendentals=0,
            bytes_accessed=groups * rows * block * 2 + rows * block * 4,
        ),
    )(projected)


def merge_chunk(heads, head_dim, parts, get_part, out_ref, c):
    rows_per = out_ref.shape[1]
    width = heads * head_dim
    lanes = 128
    lane = lax.broadcasted_iota(jnp.int32, (rows_per, lanes), 1)
    stats = [get_part(j, c, slice(width, width + lanes)).astype(jnp.float32) for j in range(parts)]
    peak = stats[0]
    for j in range(1, parts):
        peak = jnp.maximum(peak, stats[j])
    factors = [jnp.exp(st - peak) for st in stats]
    merged = jnp.zeros((rows_per, lanes), jnp.float32)
    for h in range(heads):
        cut = slice(h * head_dim, (h + 1) * head_dim)
        o_h = jnp.zeros((rows_per, head_dim), jnp.float32)
        l_h = jnp.zeros((rows_per, 1), jnp.float32)
        for j in range(parts):
            f_h = factors[j][:, h : h + 1]
            o_h = o_h + f_h * get_part(j, c, cut).astype(jnp.float32)
            l_j = (
                stats[j][:, heads + h : heads + h + 1]
                + stats[j][:, 2 * heads + h : 2 * heads + h + 1]
            )
            l_h = l_h + f_h * l_j
        out_ref[c, :, cut] = o_h.astype(out_ref.dtype)
        l_hi = l_h.astype(jnp.bfloat16).astype(jnp.float32)
        merged = jnp.where(
            lane == h,
            peak[:, h : h + 1],
            jnp.where(
                lane == heads + h,
                l_hi,
                jnp.where(lane == 2 * heads + h, l_h - l_hi, merged),
            ),
        )
    out_ref[c, :, width:] = merged.astype(out_ref.dtype)


def y_exchange_kernel(heads, head_dim, groups, src_hbm, out_ref, parts, own_sem, send_sems, recv_sems):
    me = lax.axis_index("y")
    chunks = out_ref.shape[0]
    barrier = pltpu.get_barrier_semaphore()
    for k in range(1, groups):
        pl.semaphore_signal(
            barrier, inc=1, device_id={"y": lax.rem(me + k, groups)},
            device_id_type=pl.DeviceIdType.MESH,
        )
    pl.semaphore_wait(barrier, groups - 1)
    local = pltpu.make_async_copy(src_hbm.at[:, me], parts.at[0], own_sem)
    local.start()
    copies = []
    for k in range(1, groups):
        dest = lax.rem(me + k, groups)
        copy = pltpu.make_async_remote_copy(
            src_ref=src_hbm.at[:, dest],
            dst_ref=parts.at[k],
            send_sem=send_sems.at[k - 1],
            recv_sem=recv_sems.at[k - 1],
            device_id={"y": dest},
            device_id_type=pl.DeviceIdType.MESH,
        )
        copy.start()
        copies.append(copy)
    local.wait()
    for copy in copies:
        copy.wait()

    def get_part(j, c, cut):
        return parts[j, c, :, cut]

    def step(c, carry):
        merge_chunk(heads, head_dim, groups, get_part, out_ref, c)
        return carry

    lax.fori_loop(0, chunks, step, 0)


def y_exchange(by_y, heads, head_dim):
    chunks, groups, rows_per, lanes_all = by_y.shape
    kernel = functools.partial(y_exchange_kernel, heads, head_dim, groups)
    return pl.pallas_call(
        kernel,
        out_shape=jax.ShapeDtypeStruct((chunks, rows_per, lanes_all), by_y.dtype),
        in_specs=[pl.BlockSpec(memory_space=pl.ANY)],
        out_specs=pl.BlockSpec(memory_space=pltpu.VMEM),
        scratch_shapes=[
            pltpu.VMEM((groups, chunks, rows_per, lanes_all), by_y.dtype),
            pltpu.SemaphoreType.DMA(()),
            pltpu.SemaphoreType.DMA((groups - 1,)),
            pltpu.SemaphoreType.DMA((groups - 1,)),
        ],
        compiler_params=pltpu.CompilerParams(
            collective_id=2, has_side_effects=True, vmem_limit_bytes=32 * 1024 * 1024
        ),
        cost_estimate=pl.CostEstimate(
            flops=4 * by_y.size,
            transcendentals=chunks * groups * rows_per * 128,
            bytes_accessed=2 * by_y.size * 2,
        ),
    )(by_y)


def z_combine_kernel(heads, head_dim, groups, src_hbm, w_ref, out_ref, parts, o_acc, l_acc,
                     own_sem, send_sems, recv_sems):
    me = lax.axis_index("z")
    barrier = pltpu.get_barrier_semaphore()
    for k in range(1, groups):
        pl.semaphore_signal(
            barrier, inc=1, device_id={"z": lax.rem(me + k, groups)},
            device_id_type=pl.DeviceIdType.MESH,
        )
    pl.semaphore_wait(barrier, groups - 1)
    local = pltpu.make_async_copy(src_hbm.at[me], parts.at[0], own_sem)
    local.start()
    copies = []
    for k in range(1, groups):
        dest = lax.rem(me + k, groups)
        copy = pltpu.make_async_remote_copy(
            src_ref=src_hbm.at[dest],
            dst_ref=parts.at[k],
            send_sem=send_sems.at[k - 1],
            recv_sem=recv_sems.at[k - 1],
            device_id={"z": dest},
            device_id_type=pl.DeviceIdType.MESH,
        )
        copy.start()
        copies.append(copy)
    local.wait()
    for copy in copies:
        copy.wait()
    combine_kernel(heads, head_dim, parts, w_ref, out_ref, o_acc, l_acc)


def z_combine(merged, w_all, heads, head_dim):
    groups, rows_per, lanes_all = merged.shape
    _, tokens, width = w_all.shape
    kernel = functools.partial(z_combine_kernel, heads, head_dim, groups)
    return pl.pallas_call(
        kernel,
        out_shape=jax.ShapeDtypeStruct((rows_per, tokens), jnp.bfloat16),
        in_specs=[
            pl.BlockSpec(memory_space=pl.ANY),
            pl.BlockSpec(memory_space=pltpu.VMEM),
        ],
        out_specs=pl.BlockSpec(memory_space=pltpu.VMEM),
        scratch_shapes=[
            pltpu.VMEM((groups, rows_per, lanes_all), merged.dtype),
            pltpu.VMEM((rows_per, width), jnp.float32),
            pltpu.VMEM((rows_per, 128), jnp.float32),
            pltpu.SemaphoreType.DMA(()),
            pltpu.SemaphoreType.DMA((groups - 1,)),
            pltpu.SemaphoreType.DMA((groups - 1,)),
        ],
        compiler_params=pltpu.CompilerParams(
            collective_id=3, has_side_effects=True, vmem_limit_bytes=48 * 1024 * 1024
        ),
        cost_estimate=pl.CostEstimate(
            flops=2 * rows_per * tokens * width + 4 * merged.size,
            transcendentals=groups * rows_per * 128,
            bytes_accessed=2 * merged.size * 2 + tokens * width * 2 + rows_per * tokens * 2,
        ),
    )(merged, w_all)


def per_device(
    queries,
    keys,
    values,
    key_cache,
    value_cache,
    cache_len,
    page_table,
    append_slots,
    out_weight,
    out_bias,
):
    tok_dev, head_count, head_dim = queries.shape
    width = head_count * head_dim
    requests = cache_len.shape[0]
    max_pages = page_table.shape[1]
    new_pages = append_slots.shape[1]
    span_len = new_pages * PAGE
    slot_count = key_cache.shape[0]
    page_devices = lax.axis_size(PAGES)
    device_at = lax.axis_index(PAGES)
    token_ids = device_at * tok_dev + jnp.arange(tok_dev, dtype=jnp.int32)
    request_ids = token_ids // span_len
    request_grid = jnp.arange(requests, dtype=jnp.int32)
    starts = jnp.sum(
        jnp.where(request_ids[:, None] == request_grid[None, :], cache_len[None, :], 0), axis=1
    )
    positions = (starts + token_ids % span_len).astype(jnp.float32)
    rotated_q = rotate(queries.astype(jnp.float32), positions).astype(jnp.bfloat16)
    rotated_k = rotate(keys.astype(jnp.float32), positions).astype(jnp.bfloat16)
    w_cols = out_weight.shape[1]
    w_plane = jnp.pad(out_weight.T, ((0, tok_dev - w_cols), (0, 0)))
    stacked = jnp.stack(
        [
            rotated_q.reshape(tok_dev, width),
            rotated_k.reshape(tok_dev, width),
            values.reshape(tok_dev, width),
        ]
    )
    w_all = lax.all_gather(w_plane[None], PAGES, axis=1, tiled=True)
    gathered = lax.all_gather(stacked, PAGES, axis=1, tiled=True)
    my_slots = device_at * slot_count + jnp.arange(slot_count, dtype=jnp.int32)
    cached_hit = page_table.reshape(-1)[None, :] == my_slots[:, None]
    fresh_hit = append_slots.reshape(-1)[None, :] == my_slots[:, None]
    is_cached = jnp.any(cached_hit, axis=1)
    is_fresh = jnp.any(fresh_hit, axis=1)
    cached_index = jnp.sum(
        jnp.where(cached_hit, jnp.arange(requests * max_pages, dtype=jnp.int32)[None, :], 0), axis=1
    )
    fresh_index = jnp.sum(
        jnp.where(fresh_hit, jnp.arange(requests * new_pages, dtype=jnp.int32)[None, :], 0), axis=1
    )
    slot_request = jnp.where(is_fresh, fresh_index // new_pages, cached_index // max_pages)
    slot_page = jnp.where(is_fresh, fresh_index % new_pages, cached_index % max_pages)
    slot_length = jnp.sum(
        jnp.where(slot_request[:, None] == request_grid[None, :], cache_len[None, :], 0), axis=1
    )
    visible = is_cached & (slot_page * PAGE < slot_length)
    slot_kind = jnp.where(is_fresh, 2, jnp.where(visible, 1, 0)).astype(jnp.int32)
    slot_limit = jnp.where(is_fresh, slot_page * PAGE, -4 * span_len)
    packed, key_slots, value_slots = local_attention(
        slot_request,
        slot_kind,
        slot_limit,
        fresh_index,
        gathered,
        key_cache.reshape(slot_count, PAGE, width),
        value_cache.reshape(slot_count, PAGE, width),
        head_count,
        head_dim,
        requests,
        span_len,
        page_devices,
    )
    paired = pair_merge(packed, head_count, head_dim)
    z_n = lax.axis_size("z")
    y_n = lax.axis_size("y")
    by_y = paired.reshape(z_n, y_n, tok_dev, paired.shape[-1])
    merged = y_exchange(by_y, head_count, head_dim)
    projected = z_combine(merged, w_all, head_count, head_dim)
    head_groups = lax.axis_size("heads")
    summed = heads_sum(projected, head_groups)
    summed = summed.reshape(tok_dev, page_devices // head_groups, tok_dev)[:, :, :w_cols].reshape(
        tok_dev, (page_devices // head_groups) * w_cols
    )
    key_out = key_slots.reshape(key_cache.shape)
    value_out = value_slots.reshape(value_cache.shape)
    hidden = (summed + out_bias[None, :]).astype(jnp.bfloat16)
    return (hidden, key_out, value_out)


def solution(mesh):
    heads_n, pages_n = mesh.devices.shape
    z_n = pages_n // 8
    split = jax.sharding.Mesh(
        mesh.devices.reshape(heads_n, z_n, 4, 2), ("heads", "z", "y", "core")
    )
    placed = (
        P(PAGES, "heads", None),
        P(PAGES, "heads", None),
        P(PAGES, "heads", None),
        P(PAGES, None, "heads", None),
        P(PAGES, None, "heads", None),
        P(),
        P(),
        P(),
        P("heads", PAGES),
        P("heads"),
    )
    return jax.shard_map(
        per_device,
        mesh=split,
        in_specs=placed,
        out_specs=(
            P(PAGES, "heads"),
            P(PAGES, None, "heads", None),
            P(PAGES, None, "heads", None),
        ),
        check_vma=False,
    )
```

```python
import functools
import math

import jax
import jax.numpy as jnp
from jax import lax
from jax.experimental import pallas as pl
from jax.experimental.pallas import tpu as pltpu
from jax.sharding import PartitionSpec as P

ROT = 32
PAGE = 128
PAGES = ("z", "y", "core")


low_score = -1e30
mask_score = -(2.0 ** 100)


def rotate(vectors, positions):
    half_rot = ROT // 2
    inv_freq = 10000.0 ** (-2.0 * jnp.arange(half_rot, dtype=jnp.float32) / ROT)
    angles = positions[:, None] * inv_freq[None, :]
    cosine = jnp.cos(angles)[:, None, :]
    sine = jnp.sin(angles)[:, None, :]
    first_half = vectors[..., :half_rot]
    second_half = vectors[..., half_rot:ROT]
    return jnp.concatenate(
        [
            first_half * cosine - second_half * sine,
            second_half * cosine + first_half * sine,
            vectors[..., ROT:],
        ],
        axis=-1,
    )


def attend_kernel(
    heads, head_dim, requests, span,
    sreq_ref, skind_ref, slim_ref, sfresh_ref,
    q_ref, kf_ref, vf_ref, kc_ref, vc_ref,
    out_ref, ko_ref, vo_ref, acc_t, stats, tok_ref, ml_ref,
):
    step = pl.program_id(0)
    lanes = ml_ref.shape[1]
    width = heads * head_dim

    @pl.when(step == 0)
    def _init():
        acc_t[...] = jnp.zeros_like(acc_t)
        row = lax.broadcasted_iota(jnp.int32, stats.shape, 1)
        stats[...] = jnp.where(row < heads, mask_score, 0.0).astype(jnp.float32)

    request = sreq_ref[step]
    kind = skind_ref[step]
    limit = slim_ref[step]
    scale = 1.0 / math.sqrt(head_dim)

    def attend(k_ref, v_ref, masked):
        base = pl.multiple_of(request * span, span)
        if masked:
            keys_at = lax.broadcasted_iota(jnp.int32, (PAGE, span), 0)
            queries_at = lax.broadcasted_iota(jnp.int32, (PAGE, span), 1)
            allowed = queries_at - keys_at >= limit
        v_t = v_ref[0].astype(jnp.float32).T.astype(jnp.bfloat16)
        for h in range(heads):
            cut = slice(h * head_dim, (h + 1) * head_dim)
            q_h = q_ref[0, pl.ds(base, span), cut]
            k_h = k_ref[0, :, cut]
            scores = lax.dot_general(
                k_h, q_h, (((1,), (1,)), ((), ())), preferred_element_type=jnp.float32
            ) * scale
            if masked:
                scores = jnp.where(allowed, scores, mask_score)
            m_prev = stats[request, h : h + 1, :]
            l_prev = stats[request, heads + h : heads + h + 1, :]
            m_new = jnp.maximum(m_prev, jnp.max(scores, axis=0, keepdims=True))
            m_new = m_new.astype(jnp.bfloat16).astype(jnp.float32)
            alpha = jnp.exp(m_prev - m_new)
            weights = jnp.exp(scores - m_new)
            if masked:
                weights = jnp.where(allowed, weights, 0.0)
            l_new = alpha * l_prev + jnp.sum(weights, axis=0, keepdims=True)
            contrib = jnp.dot(
                v_t[cut, :], weights.astype(jnp.bfloat16), preferred_element_type=jnp.float32
            )
            slot = request * heads + h
            acc_t[slot] = alpha * acc_t[slot] + contrib
            stats[request, h : h + 1, :] = m_new
            stats[request, heads + h : heads + h + 1, :] = l_new
            stats[request, 2 * heads + h : 2 * heads + h + 1, :] = l_new

    @pl.when(kind == 1)
    def _cached():
        attend(kc_ref, vc_ref, False)

    @pl.when(kind == 2)
    def _fresh():
        attend(kf_ref, vf_ref, True)

    @pl.when(kind == 2)
    def _store_fresh():
        ko_ref[...] = kf_ref[...]
        vo_ref[...] = vf_ref[...]

    @pl.when(kind != 2)
    def _store_cached():
        ko_ref[...] = kc_ref[...]
        vo_ref[...] = vc_ref[...]

    @pl.when(step == pl.num_programs(0) - 1)
    def _emit():
        stat_rows = stats.shape[1]
        for r in range(requests):
            rows = pl.ds(r * span, span)
            for h in range(heads):
                tok_ref[rows, h * head_dim : (h + 1) * head_dim] = acc_t[r * heads + h].T
            block = jnp.concatenate(
                [stats[r], jnp.zeros((lanes - stat_rows, span), jnp.float32)], axis=0
            )
            ml_ref[rows, :] = block.T
        chunks, rows_per, _ = out_ref.shape
        lane = lax.broadcasted_iota(jnp.int32, (rows_per, lanes), 1)
        for d in range(chunks):
            rows = pl.ds(d * rows_per, rows_per)
            out_ref[d, :, :width] = tok_ref[rows, :].astype(jnp.bfloat16)
            ml = ml_ref[rows, :]
            rounded = ml.astype(jnp.bfloat16).astype(jnp.float32)
            packed = jnp.where(
                lane < 2 * heads,
                rounded,
                jnp.where(lane < 3 * heads, ml - rounded, 0.0),
            )
            out_ref[d, :, width:] = packed.astype(jnp.bfloat16)


def local_attention(slot_request, slot_kind, slot_limit, slot_fresh, gathered, kc, vc,
                    heads, head_dim, requests, span, chunks):
    _, tokens, width = gathered.shape
    slot_count = kc.shape[0]
    rows_per = tokens // chunks
    kernel = functools.partial(attend_kernel, heads, head_dim, requests, span)
    flops = 4 * slot_count * span * PAGE * width
    return pl.pallas_call(
        kernel,
        out_shape=(
            jax.ShapeDtypeStruct((chunks, rows_per, width + 128), jnp.bfloat16),
            jax.ShapeDtypeStruct(kc.shape, kc.dtype),
            jax.ShapeDtypeStruct(vc.shape, vc.dtype),
        ),
        grid_spec=pltpu.PrefetchScalarGridSpec(
            num_scalar_prefetch=4,
            grid=(slot_count,),
            in_specs=[
                pl.BlockSpec((1, tokens, width), lambda s, *_: (0, 0, 0),
                             pipeline_mode=pl.Buffered(1)),
                pl.BlockSpec((1, PAGE, width), lambda s, rq, kd, lm, fr: (1, fr[s], 0)),
                pl.BlockSpec((1, PAGE, width), lambda s, rq, kd, lm, fr: (2, fr[s], 0)),
                pl.BlockSpec((1, PAGE, width), lambda s, *_: (s, 0, 0)),
                pl.BlockSpec((1, PAGE, width), lambda s, *_: (s, 0, 0)),
            ],
            out_specs=[
                pl.BlockSpec((chunks, rows_per, width + 128), lambda s, *_: (0, 0, 0)),
                pl.BlockSpec((1, PAGE, width), lambda s, *_: (s, 0, 0)),
                pl.BlockSpec((1, PAGE, width), lambda s, *_: (s, 0, 0)),
            ],
            scratch_shapes=[
                pltpu.VMEM((requests * heads, head_dim, span), jnp.float32),
                pltpu.VMEM((requests, 16, span), jnp.float32),
                pltpu.VMEM((tokens, width), jnp.float32),
                pltpu.VMEM((tokens, 128), jnp.float32),
            ],
        ),
        compiler_params=pltpu.CompilerParams(
            dimension_semantics=("arbitrary",), vmem_limit_bytes=62 * 1024 * 1024
        ),
        cost_estimate=pl.CostEstimate(
            flops=flops,
            transcendentals=slot_count * span * PAGE * heads,
            bytes_accessed=tokens * width * 2 + 4 * kc.size * 2 + tokens * (width + 128) * 2,
        ),
    )(slot_request, slot_kind, slot_limit, slot_fresh, gathered, gathered, gathered, kc, vc)


def combine_kernel(heads, head_dim, recv_ref, w_ref, out_ref, o_acc, l_acc):
    chunks, rows_per, _ = recv_ref.shape
    width = heads * head_dim
    lanes = 128

    def peak_step(d, peak):
        return jnp.maximum(peak, recv_ref[d, :, width:].astype(jnp.float32))

    peak = lax.fori_loop(
        0, chunks, peak_step, jnp.full((rows_per, lanes), mask_score, jnp.float32)
    )
    o_acc[...] = jnp.zeros_like(o_acc)
    l_acc[...] = jnp.zeros_like(l_acc)

    def sum_step(d, carry):
        mld = recv_ref[d, :, width:].astype(jnp.float32)
        factor = jnp.exp(mld - peak)
        for h in range(heads):
            f_h = factor[:, h : h + 1]
            l_h = mld[:, heads + h : heads + h + 1] + mld[:, 2 * heads + h : 2 * heads + h + 1]
            l_acc[:, h : h + 1] += f_h * l_h
            cut = slice(h * head_dim, (h + 1) * head_dim)
            o_acc[:, cut] += f_h * recv_ref[d, :, cut].astype(jnp.float32)
        return carry

    lax.fori_loop(0, chunks, sum_step, 0)
    parts = []
    for h in range(heads):
        cut = slice(h * head_dim, (h + 1) * head_dim)
        parts.append((o_acc[:, cut] / l_acc[:, h : h + 1]).astype(jnp.bfloat16))
    attended = jnp.concatenate(parts, axis=1)
    out_ref[...] = lax.dot_general(
        attended, w_ref[0], (((1,), (1,)), ((), ())), preferred_element_type=jnp.float32
    ).astype(out_ref.dtype)


def combine_project(received, gathered, heads, head_dim):
    chunks, rows_per, _ = received.shape
    _, tokens, width = gathered.shape
    kernel = functools.partial(combine_kernel, heads, head_dim)
    return pl.pallas_call(
        kernel,
        out_shape=jax.ShapeDtypeStruct((rows_per, tokens), jnp.bfloat16),
        grid=(1,),
        in_specs=[
            pl.BlockSpec(received.shape, lambda i: (0, 0, 0)),
            pl.BlockSpec((1, tokens, width), lambda i: (0, 0, 0)),
        ],
        out_specs=pl.BlockSpec((rows_per, tokens), lambda i: (0, 0)),
        scratch_shapes=[
            pltpu.VMEM((rows_per, width), jnp.float32),
            pltpu.VMEM((rows_per, 128), jnp.float32),
        ],
        compiler_params=pltpu.CompilerParams(vmem_limit_bytes=48 * 1024 * 1024),
        cost_estimate=pl.CostEstimate(
            flops=2 * rows_per * tokens * width + 4 * received.size,
            transcendentals=chunks * rows_per * 128,
            bytes_accessed=received.size * 2 + tokens * width * 2 + rows_per * tokens * 2,
        ),
    )(received, gathered)


def pair_merge_kernel(heads, head_dim, packed_hbm, out_ref, mine, theirs, local_sem, send_sem, recv_sem):
    core = lax.axis_index("core")
    partner = 1 - core
    width = heads * head_dim
    lanes = 128
    chunks, rows_per, _ = out_ref.shape

    barrier = pltpu.get_barrier_semaphore()
    pl.semaphore_signal(barrier, inc=1, device_id={"core": partner}, device_id_type=pl.DeviceIdType.MESH)
    pl.semaphore_wait(barrier, 1)

    local = pltpu.make_async_copy(packed_hbm.at[:, core], mine, local_sem)
    local.start()
    remote = pltpu.make_async_remote_copy(
        src_ref=packed_hbm.at[:, partner],
        dst_ref=theirs,
        send_sem=send_sem,
        recv_sem=recv_sem,
        device_id={"core": partner},
        device_id_type=pl.DeviceIdType.MESH,
    )
    remote.start()
    local.wait()
    remote.wait()

    lane = lax.broadcasted_iota(jnp.int32, (rows_per, lanes), 1)

    def merge_step(c, carry):
        ml_a = mine[c, :, width:].astype(jnp.float32)
        ml_b = theirs[c, :, width:].astype(jnp.float32)
        peak = jnp.maximum(ml_a, ml_b)
        f_a = jnp.exp(ml_a - peak)
        f_b = jnp.exp(ml_b - peak)
        merged = jnp.zeros((rows_per, lanes), jnp.float32)
        for h in range(heads):
            cut = slice(h * head_dim, (h + 1) * head_dim)
            fa_h = f_a[:, h : h + 1]
            fb_h = f_b[:, h : h + 1]
            out_ref[c, :, cut] = (
                fa_h * mine[c, :, cut].astype(jnp.float32)
                + fb_h * theirs[c, :, cut].astype(jnp.float32)
            ).astype(out_ref.dtype)
            l_a = ml_a[:, heads + h : heads + h + 1] + ml_a[:, 2 * heads + h : 2 * heads + h + 1]
            l_b = ml_b[:, heads + h : heads + h + 1] + ml_b[:, 2 * heads + h : 2 * heads + h + 1]
            l_h = fa_h * l_a + fb_h * l_b
            l_hi = l_h.astype(jnp.bfloat16).astype(jnp.float32)
            merged = jnp.where(
                lane == h,
                peak[:, h : h + 1],
                jnp.where(
                    lane == heads + h,
                    l_hi,
                    jnp.where(lane == 2 * heads + h, l_h - l_hi, merged),
                ),
            )
        out_ref[c, :, width:] = merged.astype(out_ref.dtype)
        return carry

    lax.fori_loop(0, chunks, merge_step, 0)


def pair_merge(packed, heads, head_dim):
    devices, rows_per, lanes_all = packed.shape
    chips = devices // 2
    view = packed.reshape(chips, 2, rows_per, lanes_all)
    kernel = functools.partial(pair_merge_kernel, heads, head_dim)
    return pl.pallas_call(
        kernel,
        out_shape=jax.ShapeDtypeStruct((chips, rows_per, lanes_all), packed.dtype),
        in_specs=[pl.BlockSpec(memory_space=pl.ANY)],
        out_specs=pl.BlockSpec(memory_space=pltpu.VMEM),
        scratch_shapes=[
            pltpu.VMEM((chips, rows_per, lanes_all), packed.dtype),
            pltpu.VMEM((chips, rows_per, lanes_all), packed.dtype),
            pltpu.SemaphoreType.DMA(()),
            pltpu.SemaphoreType.DMA(()),
            pltpu.SemaphoreType.DMA(()),
        ],
        compiler_params=pltpu.CompilerParams(
            collective_id=0, has_side_effects=True, vmem_limit_bytes=40 * 1024 * 1024
        ),
        cost_estimate=pl.CostEstimate(
            flops=6 * chips * rows_per * lanes_all,
            transcendentals=2 * chips * rows_per * 128,
            bytes_accessed=3 * chips * rows_per * lanes_all * 2,
        ),
    )(view)


def heads_sum_kernel(groups, block, proj_hbm, out_ref, own, received, own_sem, send_sems, recv_sems):
    group = lax.axis_index("heads")
    barrier = pltpu.get_barrier_semaphore()
    for k in range(1, groups):
        pl.semaphore_signal(
            barrier, inc=1, device_id={"heads": lax.rem(group + k, groups)},
            device_id_type=pl.DeviceIdType.MESH,
        )
    pl.semaphore_wait(barrier, groups - 1)
    local = pltpu.make_async_copy(
        proj_hbm.at[:, pl.ds(pl.multiple_of(group * block, 128), block)], own, own_sem
    )
    local.start()
    copies = []
    for k in range(1, groups):
        dest = lax.rem(group + k, groups)
        copy = pltpu.make_async_remote_copy(
            src_ref=proj_hbm.at[:, pl.ds(pl.multiple_of(dest * block, 128), block)],
            dst_ref=received.at[k - 1],
            send_sem=send_sems.at[k - 1],
            recv_sem=recv_sems.at[k - 1],
            device_id={"heads": dest},
            device_id_type=pl.DeviceIdType.MESH,
        )
        copy.start()
        copies.append(copy)
    local.wait()
    for copy in copies:
        copy.wait()
    total = own[...].astype(jnp.float32)
    for k in range(groups - 1):
        total = total + received[k].astype(jnp.float32)
    out_ref[...] = total


def heads_sum(projected, groups):
    rows, cols = projected.shape
    block = cols // groups
    kernel = functools.partial(heads_sum_kernel, groups, block)
    return pl.pallas_call(
        kernel,
        out_shape=jax.ShapeDtypeStruct((rows, block), jnp.float32),
        in_specs=[pl.BlockSpec(memory_space=pl.ANY)],
        out_specs=pl.BlockSpec(memory_space=pltpu.VMEM),
        scratch_shapes=[
            pltpu.VMEM((rows, block), projected.dtype),
            pltpu.VMEM((groups - 1, rows, block), projected.dtype),
            pltpu.SemaphoreType.DMA(()),
            pltpu.SemaphoreType.DMA((groups - 1,)),
            pltpu.SemaphoreType.DMA((groups - 1,)),
        ],
        compiler_params=pltpu.CompilerParams(collective_id=1, has_side_effects=True),
        cost_estimate=pl.CostEstimate(
            flops=groups * rows * block,
            transcendentals=0,
            bytes_accessed=groups * rows * block * 2 + rows * block * 4,
        ),
    )(projected)


def merge_chunk(heads, head_dim, parts, get_part, out_ref, c):
    rows_per = out_ref.shape[1]
    width = heads * head_dim
    lanes = 128
    lane = lax.broadcasted_iota(jnp.int32, (rows_per, lanes), 1)
    stats = [get_part(j, c, slice(width, width + lanes)).astype(jnp.float32) for j in range(parts)]
    peak = stats[0]
    for j in range(1, parts):
        peak = jnp.maximum(peak, stats[j])
    factors = [jnp.exp(st - peak) for st in stats]
    merged = jnp.zeros((rows_per, lanes), jnp.float32)
    for h in range(heads):
        cut = slice(h * head_dim, (h + 1) * head_dim)
        o_h = jnp.zeros((rows_per, head_dim), jnp.float32)
        l_h = jnp.zeros((rows_per, 1), jnp.float32)
        for j in range(parts):
            f_h = factors[j][:, h : h + 1]
            o_h = o_h + f_h * get_part(j, c, cut).astype(jnp.float32)
            l_j = (
                stats[j][:, heads + h : heads + h + 1]
                + stats[j][:, 2 * heads + h : 2 * heads + h + 1]
            )
            l_h = l_h + f_h * l_j
        out_ref[c, :, cut] = o_h.astype(out_ref.dtype)
        l_hi = l_h.astype(jnp.bfloat16).astype(jnp.float32)
        merged = jnp.where(
            lane == h,
            peak[:, h : h + 1],
            jnp.where(
                lane == heads + h,
                l_hi,
                jnp.where(lane == 2 * heads + h, l_h - l_hi, merged),
            ),
        )
    out_ref[c, :, width:] = merged.astype(out_ref.dtype)


def y_exchange_kernel(heads, head_dim, groups, src_hbm, out_ref, parts, own_sem, send_sems, recv_sems):
    me = lax.axis_index("y")
    chunks = out_ref.shape[0]
    barrier = pltpu.get_barrier_semaphore()
    for k in range(1, groups):
        pl.semaphore_signal(
            barrier, inc=1, device_id={"y": lax.rem(me + k, groups)},
            device_id_type=pl.DeviceIdType.MESH,
        )
    pl.semaphore_wait(barrier, groups - 1)
    local = pltpu.make_async_copy(src_hbm.at[:, me], parts.at[0], own_sem)
    local.start()
    copies = []
    for k in range(1, groups):
        dest = lax.rem(me + k, groups)
        copy = pltpu.make_async_remote_copy(
            src_ref=src_hbm.at[:, dest],
            dst_ref=parts.at[k],
            send_sem=send_sems.at[k - 1],
            recv_sem=recv_sems.at[k - 1],
            device_id={"y": dest},
            device_id_type=pl.DeviceIdType.MESH,
        )
        copy.start()
        copies.append(copy)
    local.wait()
    for copy in copies:
        copy.wait()

    def get_part(j, c, cut):
        return parts[j, c, :, cut]

    def step(c, carry):
        merge_chunk(heads, head_dim, groups, get_part, out_ref, c)
        return carry

    lax.fori_loop(0, chunks, step, 0)


def y_exchange(by_y, heads, head_dim):
    chunks, groups, rows_per, lanes_all = by_y.shape
    kernel = functools.partial(y_exchange_kernel, heads, head_dim, groups)
    return pl.pallas_call(
        kernel,
        out_shape=jax.ShapeDtypeStruct((chunks, rows_per, lanes_all), by_y.dtype),
        in_specs=[pl.BlockSpec(memory_space=pl.ANY)],
        out_specs=pl.BlockSpec(memory_space=pltpu.VMEM),
        scratch_shapes=[
            pltpu.VMEM((groups, chunks, rows_per, lanes_all), by_y.dtype),
            pltpu.SemaphoreType.DMA(()),
            pltpu.SemaphoreType.DMA((groups - 1,)),
            pltpu.SemaphoreType.DMA((groups - 1,)),
        ],
        compiler_params=pltpu.CompilerParams(
            collective_id=2, has_side_effects=True, vmem_limit_bytes=32 * 1024 * 1024
        ),
        cost_estimate=pl.CostEstimate(
            flops=4 * by_y.size,
            transcendentals=chunks * groups * rows_per * 128,
            bytes_accessed=2 * by_y.size * 2,
        ),
    )(by_y)


def z_exchange_kernel(groups, src_hbm, out_ref, parts, own_sem, send_sems, recv_sems):
    me = lax.axis_index("z")
    barrier = pltpu.get_barrier_semaphore()
    for k in range(1, groups):
        pl.semaphore_signal(
            barrier, inc=1, device_id={"z": lax.rem(me + k, groups)},
            device_id_type=pl.DeviceIdType.MESH,
        )
    pl.semaphore_wait(barrier, groups - 1)
    local = pltpu.make_async_copy(src_hbm.at[me], parts.at[0], own_sem)
    local.start()
    copies = []
    for k in range(1, groups):
        dest = lax.rem(me + k, groups)
        copy = pltpu.make_async_remote_copy(
            src_ref=src_hbm.at[dest],
            dst_ref=parts.at[k],
            send_sem=send_sems.at[k - 1],
            recv_sem=recv_sems.at[k - 1],
            device_id={"z": dest},
            device_id_type=pl.DeviceIdType.MESH,
        )
        copy.start()
        copies.append(copy)
    local.wait()
    for copy in copies:
        copy.wait()
    out_ref[...] = parts[...]


def z_exchange(merged):
    groups, rows_per, lanes_all = merged.shape
    kernel = functools.partial(z_exchange_kernel, groups)
    return pl.pallas_call(
        kernel,
        out_shape=jax.ShapeDtypeStruct(merged.shape, merged.dtype),
        in_specs=[pl.BlockSpec(memory_space=pl.ANY)],
        out_specs=pl.BlockSpec(memory_space=pltpu.VMEM),
        scratch_shapes=[
            pltpu.VMEM(merged.shape, merged.dtype),
            pltpu.SemaphoreType.DMA(()),
            pltpu.SemaphoreType.DMA((groups - 1,)),
            pltpu.SemaphoreType.DMA((groups - 1,)),
        ],
        compiler_params=pltpu.CompilerParams(collective_id=3, has_side_effects=True),
        cost_estimate=pl.CostEstimate(
            flops=0, transcendentals=0, bytes_accessed=3 * merged.size * 2
        ),
    )(merged)

def per_device(
    queries,
    keys,
    values,
    key_cache,
    value_cache,
    cache_len,
    page_table,
    append_slots,
    out_weight,
    out_bias,
):
    tok_dev, head_count, head_dim = queries.shape
    width = head_count * head_dim
    requests = cache_len.shape[0]
    max_pages = page_table.shape[1]
    new_pages = append_slots.shape[1]
    span_len = new_pages * PAGE
    slot_count = key_cache.shape[0]
    page_devices = lax.axis_size(PAGES)
    device_at = lax.axis_index(PAGES)
    token_ids = device_at * tok_dev + jnp.arange(tok_dev, dtype=jnp.int32)
    request_ids = token_ids // span_len
    request_grid = jnp.arange(requests, dtype=jnp.int32)
    starts = jnp.sum(
        jnp.where(request_ids[:, None] == request_grid[None, :], cache_len[None, :], 0), axis=1
    )
    positions = (starts + token_ids % span_len).astype(jnp.float32)
    rotated_q = rotate(queries.astype(jnp.float32), positions).astype(jnp.bfloat16)
    rotated_k = rotate(keys.astype(jnp.float32), positions).astype(jnp.bfloat16)
    w_cols = out_weight.shape[1]
    w_plane = jnp.pad(out_weight.T, ((0, tok_dev - w_cols), (0, 0)))
    stacked = jnp.stack(
        [
            rotated_q.reshape(tok_dev, width),
            rotated_k.reshape(tok_dev, width),
            values.reshape(tok_dev, width),
        ]
    )
    w_all = lax.all_gather(w_plane[None], PAGES, axis=1, tiled=True)
    gathered = lax.all_gather(stacked, PAGES, axis=1, tiled=True)
    my_slots = device_at * slot_count + jnp.arange(slot_count, dtype=jnp.int32)
    cached_hit = page_table.reshape(-1)[None, :] == my_slots[:, None]
    fresh_hit = append_slots.reshape(-1)[None, :] == my_slots[:, None]
    is_cached = jnp.any(cached_hit, axis=1)
    is_fresh = jnp.any(fresh_hit, axis=1)
    cached_index = jnp.sum(
        jnp.where(cached_hit, jnp.arange(requests * max_pages, dtype=jnp.int32)[None, :], 0), axis=1
    )
    fresh_index = jnp.sum(
        jnp.where(fresh_hit, jnp.arange(requests * new_pages, dtype=jnp.int32)[None, :], 0), axis=1
    )
    slot_request = jnp.where(is_fresh, fresh_index // new_pages, cached_index // max_pages)
    slot_page = jnp.where(is_fresh, fresh_index % new_pages, cached_index % max_pages)
    slot_length = jnp.sum(
        jnp.where(slot_request[:, None] == request_grid[None, :], cache_len[None, :], 0), axis=1
    )
    visible = is_cached & (slot_page * PAGE < slot_length)
    slot_kind = jnp.where(is_fresh, 2, jnp.where(visible, 1, 0)).astype(jnp.int32)
    slot_limit = jnp.where(is_fresh, slot_page * PAGE, -4 * span_len)
    packed, key_slots, value_slots = local_attention(
        slot_request,
        slot_kind,
        slot_limit,
        fresh_index,
        gathered,
        key_cache.reshape(slot_count, PAGE, width),
        value_cache.reshape(slot_count, PAGE, width),
        head_count,
        head_dim,
        requests,
        span_len,
        page_devices,
    )
    paired = pair_merge(packed, head_count, head_dim)
    z_n = lax.axis_size("z")
    y_n = lax.axis_size("y")
    by_y = paired.reshape(z_n, y_n, tok_dev, paired.shape[-1])
    merged = y_exchange(by_y, head_count, head_dim)
    received = z_exchange(merged)
    projected = combine_project(received, w_all, head_count, head_dim)
    head_groups = lax.axis_size("heads")
    summed = heads_sum(projected, head_groups)
    summed = summed.reshape(tok_dev, page_devices // head_groups, tok_dev)[:, :, :w_cols].reshape(
        tok_dev, (page_devices // head_groups) * w_cols
    )
    key_out = key_slots.reshape(key_cache.shape)
    value_out = value_slots.reshape(value_cache.shape)
    hidden = (summed + out_bias[None, :]).astype(jnp.bfloat16)
    return (hidden, key_out, value_out)


def solution(mesh):
    heads_n, pages_n = mesh.devices.shape
    z_n = pages_n // 8
    split = jax.sharding.Mesh(
        mesh.devices.reshape(heads_n, z_n, 4, 2), ("heads", "z", "y", "core")
    )
    placed = (
        P(PAGES, "heads", None),
        P(PAGES, "heads", None),
        P(PAGES, "heads", None),
        P(PAGES, None, "heads", None),
        P(PAGES, None, "heads", None),
        P(),
        P(),
        P(),
        P("heads", PAGES),
        P("heads"),
    )
    return jax.shard_map(
        per_device,
        mesh=split,
        in_specs=placed,
        out_specs=(
            P(PAGES, "heads"),
            P(PAGES, None, "heads", None),
            P(PAGES, None, "heads", None),
        ),
        check_vma=False,
    )
```

```python
import functools
import math

import jax
import jax.numpy as jnp
from jax import lax
from jax.experimental import pallas as pl
from jax.experimental.pallas import tpu as pltpu
from jax.sharding import PartitionSpec as P

ROT = 32
PAGE = 128
PAGES = ("z", "y", "core")


low_score = -1e30
mask_score = -(2.0 ** 100)


def rotate(vectors, positions):
    half_rot = ROT // 2
    inv_freq = 10000.0 ** (-2.0 * jnp.arange(half_rot, dtype=jnp.float32) / ROT)
    angles = positions[:, None] * inv_freq[None, :]
    cosine = jnp.cos(angles)[:, None, :]
    sine = jnp.sin(angles)[:, None, :]
    first_half = vectors[..., :half_rot]
    second_half = vectors[..., half_rot:ROT]
    return jnp.concatenate(
        [
            first_half * cosine - second_half * sine,
            second_half * cosine + first_half * sine,
            vectors[..., ROT:],
        ],
        axis=-1,
    )


def attend_kernel(
    heads, head_dim, requests, span,
    sreq_ref, skind_ref, slim_ref, sfresh_ref,
    q_ref, kf_ref, vf_ref, kc_ref, vc_ref,
    out_ref, ko_ref, vo_ref, acc_t, stats, tok_ref, ml_ref,
):
    step = pl.program_id(0)
    lanes = ml_ref.shape[1]
    width = heads * head_dim

    @pl.when(step == 0)
    def _init():
        acc_t[...] = jnp.zeros_like(acc_t)
        row = lax.broadcasted_iota(jnp.int32, stats.shape, 1)
        stats[...] = jnp.where(row < heads, mask_score, 0.0).astype(jnp.float32)

    request = sreq_ref[step]
    kind = skind_ref[step]
    limit = slim_ref[step]
    scale = 1.0 / math.sqrt(head_dim)

    def attend(k_ref, v_ref, masked):
        base = pl.multiple_of(request * span, span)
        if masked:
            keys_at = lax.broadcasted_iota(jnp.int32, (PAGE, span), 0)
            queries_at = lax.broadcasted_iota(jnp.int32, (PAGE, span), 1)
            allowed = queries_at - keys_at >= limit
        v_t = v_ref[0].astype(jnp.float32).T.astype(jnp.bfloat16)
        for h in range(heads):
            cut = slice(h * head_dim, (h + 1) * head_dim)
            q_h = q_ref[0, pl.ds(base, span), cut]
            k_h = k_ref[0, :, cut]
            scores = lax.dot_general(
                k_h, q_h, (((1,), (1,)), ((), ())), preferred_element_type=jnp.float32
            ) * scale
            if masked:
                scores = jnp.where(allowed, scores, mask_score)
            m_prev = stats[request, h : h + 1, :]
            l_prev = stats[request, heads + h : heads + h + 1, :]
            m_new = jnp.maximum(m_prev, jnp.max(scores, axis=0, keepdims=True))
            m_new = m_new.astype(jnp.bfloat16).astype(jnp.float32)
            alpha = jnp.exp(m_prev - m_new)
            weights = jnp.exp(scores - m_new)
            if masked:
                weights = jnp.where(allowed, weights, 0.0)
            l_new = alpha * l_prev + jnp.sum(weights, axis=0, keepdims=True)
            contrib = jnp.dot(
                v_t[cut, :], weights.astype(jnp.bfloat16), preferred_element_type=jnp.float32
            )
            slot = request * heads + h
            acc_t[slot] = alpha * acc_t[slot] + contrib
            stats[request, h : h + 1, :] = m_new
            stats[request, heads + h : heads + h + 1, :] = l_new
            stats[request, 2 * heads + h : 2 * heads + h + 1, :] = l_new

    @pl.when(kind == 1)
    def _cached():
        attend(kc_ref, vc_ref, False)

    @pl.when(kind == 2)
    def _fresh():
        attend(kf_ref, vf_ref, True)

    @pl.when(kind == 2)
    def _store_fresh():
        ko_ref[...] = kf_ref[...]
        vo_ref[...] = vf_ref[...]

    @pl.when(kind != 2)
    def _store_cached():
        ko_ref[...] = kc_ref[...]
        vo_ref[...] = vc_ref[...]

    @pl.when(step == pl.num_programs(0) - 1)
    def _emit():
        stat_rows = stats.shape[1]
        for r in range(requests):
            rows = pl.ds(r * span, span)
            for h in range(heads):
                tok_ref[rows, h * head_dim : (h + 1) * head_dim] = acc_t[r * heads + h].T
            block = jnp.concatenate(
                [stats[r], jnp.zeros((lanes - stat_rows, span), jnp.float32)], axis=0
            )
            ml_ref[rows, :] = block.T
        chunks, rows_per, _ = out_ref.shape
        lane = lax.broadcasted_iota(jnp.int32, (rows_per, lanes), 1)
        for d in range(chunks):
            rows = pl.ds(d * rows_per, rows_per)
            out_ref[d, :, :width] = tok_ref[rows, :].astype(jnp.bfloat16)
            ml = ml_ref[rows, :]
            rounded = ml.astype(jnp.bfloat16).astype(jnp.float32)
            packed = jnp.where(
                lane < 2 * heads,
                rounded,
                jnp.where(lane < 3 * heads, ml - rounded, 0.0),
            )
            out_ref[d, :, width:] = packed.astype(jnp.bfloat16)


def local_attention(slot_request, slot_kind, slot_limit, slot_fresh, gathered, kc, vc,
                    heads, head_dim, requests, span, chunks):
    _, tokens, width = gathered.shape
    slot_count = kc.shape[0]
    rows_per = tokens // chunks
    kernel = functools.partial(attend_kernel, heads, head_dim, requests, span)
    flops = 4 * slot_count * span * PAGE * width
    return pl.pallas_call(
        kernel,
        out_shape=(
            jax.ShapeDtypeStruct((chunks, rows_per, width + 128), jnp.bfloat16),
            jax.ShapeDtypeStruct(kc.shape, kc.dtype),
            jax.ShapeDtypeStruct(vc.shape, vc.dtype),
        ),
        grid_spec=pltpu.PrefetchScalarGridSpec(
            num_scalar_prefetch=4,
            grid=(slot_count,),
            in_specs=[
                pl.BlockSpec((1, tokens, width), lambda s, *_: (0, 0, 0),
                             pipeline_mode=pl.Buffered(1)),
                pl.BlockSpec((1, PAGE, width), lambda s, rq, kd, lm, fr: (1, fr[s], 0)),
                pl.BlockSpec((1, PAGE, width), lambda s, rq, kd, lm, fr: (2, fr[s], 0)),
                pl.BlockSpec((1, PAGE, width), lambda s, *_: (s, 0, 0)),
                pl.BlockSpec((1, PAGE, width), lambda s, *_: (s, 0, 0)),
            ],
            out_specs=[
                pl.BlockSpec((chunks, rows_per, width + 128), lambda s, *_: (0, 0, 0)),
                pl.BlockSpec((1, PAGE, width), lambda s, *_: (s, 0, 0)),
                pl.BlockSpec((1, PAGE, width), lambda s, *_: (s, 0, 0)),
            ],
            scratch_shapes=[
                pltpu.VMEM((requests * heads, head_dim, span), jnp.float32),
                pltpu.VMEM((requests, 16, span), jnp.float32),
                pltpu.VMEM((tokens, width), jnp.float32),
                pltpu.VMEM((tokens, 128), jnp.float32),
            ],
        ),
        compiler_params=pltpu.CompilerParams(
            dimension_semantics=("arbitrary",), vmem_limit_bytes=62 * 1024 * 1024
        ),
        cost_estimate=pl.CostEstimate(
            flops=flops,
            transcendentals=slot_count * span * PAGE * heads,
            bytes_accessed=tokens * width * 2 + 4 * kc.size * 2 + tokens * (width + 128) * 2,
        ),
    )(slot_request, slot_kind, slot_limit, slot_fresh, gathered, gathered, gathered, kc, vc)


def combine_kernel(heads, head_dim, recv_ref, w_ref, out_ref, o_acc, l_acc):
    chunks, rows_per, _ = recv_ref.shape
    width = heads * head_dim
    lanes = 128

    def peak_step(d, peak):
        return jnp.maximum(peak, recv_ref[d, :, width:].astype(jnp.float32))

    peak = lax.fori_loop(
        0, chunks, peak_step, jnp.full((rows_per, lanes), mask_score, jnp.float32)
    )
    o_acc[...] = jnp.zeros_like(o_acc)
    l_acc[...] = jnp.zeros_like(l_acc)

    def sum_step(d, carry):
        mld = recv_ref[d, :, width:].astype(jnp.float32)
        factor = jnp.exp(mld - peak)
        for h in range(heads):
            f_h = factor[:, h : h + 1]
            l_h = mld[:, heads + h : heads + h + 1] + mld[:, 2 * heads + h : 2 * heads + h + 1]
            l_acc[:, h : h + 1] += f_h * l_h
            cut = slice(h * head_dim, (h + 1) * head_dim)
            o_acc[:, cut] += f_h * recv_ref[d, :, cut].astype(jnp.float32)
        return carry

    lax.fori_loop(0, chunks, sum_step, 0)
    parts = []
    for h in range(heads):
        cut = slice(h * head_dim, (h + 1) * head_dim)
        parts.append((o_acc[:, cut] / l_acc[:, h : h + 1]).astype(jnp.bfloat16))
    attended = jnp.concatenate(parts, axis=1)
    out_ref[...] = lax.dot_general(
        attended, w_ref[0], (((1,), (1,)), ((), ())), preferred_element_type=jnp.float32
    ).astype(out_ref.dtype)


def combine_project(received, gathered, heads, head_dim):
    chunks, rows_per, _ = received.shape
    _, tokens, width = gathered.shape
    kernel = functools.partial(combine_kernel, heads, head_dim)
    return pl.pallas_call(
        kernel,
        out_shape=jax.ShapeDtypeStruct((rows_per, tokens), jnp.bfloat16),
        grid=(1,),
        in_specs=[
            pl.BlockSpec(received.shape, lambda i: (0, 0, 0)),
            pl.BlockSpec((1, tokens, width), lambda i: (0, 0, 0)),
        ],
        out_specs=pl.BlockSpec((rows_per, tokens), lambda i: (0, 0)),
        scratch_shapes=[
            pltpu.VMEM((rows_per, width), jnp.float32),
            pltpu.VMEM((rows_per, 128), jnp.float32),
        ],
        compiler_params=pltpu.CompilerParams(vmem_limit_bytes=48 * 1024 * 1024),
        cost_estimate=pl.CostEstimate(
            flops=2 * rows_per * tokens * width + 4 * received.size,
            transcendentals=chunks * rows_per * 128,
            bytes_accessed=received.size * 2 + tokens * width * 2 + rows_per * tokens * 2,
        ),
    )(received, gathered)


def pair_merge_kernel(heads, head_dim, packed_hbm, out_ref, mine, theirs, local_sem, send_sem, recv_sem):
    core = lax.axis_index("core")
    partner = 1 - core
    width = heads * head_dim
    lanes = 128
    chunks, rows_per, _ = out_ref.shape

    barrier = pltpu.get_barrier_semaphore()
    pl.semaphore_signal(barrier, inc=1, device_id={"core": partner}, device_id_type=pl.DeviceIdType.MESH)
    pl.semaphore_wait(barrier, 1)

    pieces = 2
    size = chunks // pieces
    pending = []
    for p in range(pieces):
        rows = pl.ds(p * size, size)
        local = pltpu.make_async_copy(
            packed_hbm.at[rows, core], mine.at[rows], local_sem.at[p]
        )
        local.start()
        remote = pltpu.make_async_remote_copy(
            src_ref=packed_hbm.at[rows, partner],
            dst_ref=theirs.at[rows],
            send_sem=send_sem.at[p],
            recv_sem=recv_sem.at[p],
            device_id={"core": partner},
            device_id_type=pl.DeviceIdType.MESH,
        )
        remote.start()
        pending.append((local, remote))

    lane = lax.broadcasted_iota(jnp.int32, (rows_per, lanes), 1)

    def merge_step(c, carry):
        ml_a = mine[c, :, width:].astype(jnp.float32)
        ml_b = theirs[c, :, width:].astype(jnp.float32)
        peak = jnp.maximum(ml_a, ml_b)
        f_a = jnp.exp(ml_a - peak)
        f_b = jnp.exp(ml_b - peak)
        merged = jnp.zeros((rows_per, lanes), jnp.float32)
        for h in range(heads):
            cut = slice(h * head_dim, (h + 1) * head_dim)
            fa_h = f_a[:, h : h + 1]
            fb_h = f_b[:, h : h + 1]
            out_ref[c, :, cut] = (
                fa_h * mine[c, :, cut].astype(jnp.float32)
                + fb_h * theirs[c, :, cut].astype(jnp.float32)
            ).astype(out_ref.dtype)
            l_a = ml_a[:, heads + h : heads + h + 1] + ml_a[:, 2 * heads + h : 2 * heads + h + 1]
            l_b = ml_b[:, heads + h : heads + h + 1] + ml_b[:, 2 * heads + h : 2 * heads + h + 1]
            l_h = fa_h * l_a + fb_h * l_b
            l_hi = l_h.astype(jnp.bfloat16).astype(jnp.float32)
            merged = jnp.where(
                lane == h,
                peak[:, h : h + 1],
                jnp.where(
                    lane == heads + h,
                    l_hi,
                    jnp.where(lane == 2 * heads + h, l_h - l_hi, merged),
                ),
            )
        out_ref[c, :, width:] = merged.astype(out_ref.dtype)
        return carry

    for p in range(pieces):
        local, remote = pending[p]
        local.wait()
        remote.wait()
        lax.fori_loop(p * size, (p + 1) * size, merge_step, 0)


def pair_merge(packed, heads, head_dim):
    devices, rows_per, lanes_all = packed.shape
    chips = devices // 2
    view = packed.reshape(chips, 2, rows_per, lanes_all)
    kernel = functools.partial(pair_merge_kernel, heads, head_dim)
    return pl.pallas_call(
        kernel,
        out_shape=jax.ShapeDtypeStruct((chips, rows_per, lanes_all), packed.dtype),
        in_specs=[pl.BlockSpec(memory_space=pl.ANY)],
        out_specs=pl.BlockSpec(memory_space=pltpu.VMEM),
        scratch_shapes=[
            pltpu.VMEM((chips, rows_per, lanes_all), packed.dtype),
            pltpu.VMEM((chips, rows_per, lanes_all), packed.dtype),
            pltpu.SemaphoreType.DMA((2,)),
            pltpu.SemaphoreType.DMA((2,)),
            pltpu.SemaphoreType.DMA((2,)),
        ],
        compiler_params=pltpu.CompilerParams(
            collective_id=0, has_side_effects=True, vmem_limit_bytes=40 * 1024 * 1024
        ),
        cost_estimate=pl.CostEstimate(
            flops=6 * chips * rows_per * lanes_all,
            transcendentals=2 * chips * rows_per * 128,
            bytes_accessed=3 * chips * rows_per * lanes_all * 2,
        ),
    )(view)


def heads_sum_kernel(groups, block, proj_hbm, out_ref, own, received, own_sem, send_sems, recv_sems):
    group = lax.axis_index("heads")
    barrier = pltpu.get_barrier_semaphore()
    for k in range(1, groups):
        pl.semaphore_signal(
            barrier, inc=1, device_id={"heads": lax.rem(group + k, groups)},
            device_id_type=pl.DeviceIdType.MESH,
        )
    pl.semaphore_wait(barrier, groups - 1)
    local = pltpu.make_async_copy(
        proj_hbm.at[:, pl.ds(pl.multiple_of(group * block, 128), block)], own, own_sem
    )
    local.start()
    copies = []
    for k in range(1, groups):
        dest = lax.rem(group + k, groups)
        copy = pltpu.make_async_remote_copy(
            src_ref=proj_hbm.at[:, pl.ds(pl.multiple_of(dest * block, 128), block)],
            dst_ref=received.at[k - 1],
            send_sem=send_sems.at[k - 1],
            recv_sem=recv_sems.at[k - 1],
            device_id={"heads": dest},
            device_id_type=pl.DeviceIdType.MESH,
        )
        copy.start()
        copies.append(copy)
    local.wait()
    for copy in copies:
        copy.wait()
    total = own[...].astype(jnp.float32)
    for k in range(groups - 1):
        total = total + received[k].astype(jnp.float32)
    out_ref[...] = total


def heads_sum(projected, groups):
    rows, cols = projected.shape
    block = cols // groups
    kernel = functools.partial(heads_sum_kernel, groups, block)
    return pl.pallas_call(
        kernel,
        out_shape=jax.ShapeDtypeStruct((rows, block), jnp.float32),
        in_specs=[pl.BlockSpec(memory_space=pl.ANY)],
        out_specs=pl.BlockSpec(memory_space=pltpu.VMEM),
        scratch_shapes=[
            pltpu.VMEM((rows, block), projected.dtype),
            pltpu.VMEM((groups - 1, rows, block), projected.dtype),
            pltpu.SemaphoreType.DMA(()),
            pltpu.SemaphoreType.DMA((groups - 1,)),
            pltpu.SemaphoreType.DMA((groups - 1,)),
        ],
        compiler_params=pltpu.CompilerParams(collective_id=1, has_side_effects=True),
        cost_estimate=pl.CostEstimate(
            flops=groups * rows * block,
            transcendentals=0,
            bytes_accessed=groups * rows * block * 2 + rows * block * 4,
        ),
    )(projected)


def merge_chunk(heads, head_dim, parts, get_part, out_ref, c):
    rows_per = out_ref.shape[1]
    width = heads * head_dim
    lanes = 128
    lane = lax.broadcasted_iota(jnp.int32, (rows_per, lanes), 1)
    stats = [get_part(j, c, slice(width, width + lanes)).astype(jnp.float32) for j in range(parts)]
    peak = stats[0]
    for j in range(1, parts):
        peak = jnp.maximum(peak, stats[j])
    factors = [jnp.exp(st - peak) for st in stats]
    merged = jnp.zeros((rows_per, lanes), jnp.float32)
    for h in range(heads):
        cut = slice(h * head_dim, (h + 1) * head_dim)
        o_h = jnp.zeros((rows_per, head_dim), jnp.float32)
        l_h = jnp.zeros((rows_per, 1), jnp.float32)
        for j in range(parts):
            f_h = factors[j][:, h : h + 1]
            o_h = o_h + f_h * get_part(j, c, cut).astype(jnp.float32)
            l_j = (
                stats[j][:, heads + h : heads + h + 1]
                + stats[j][:, 2 * heads + h : 2 * heads + h + 1]
            )
            l_h = l_h + f_h * l_j
        out_ref[c, :, cut] = o_h.astype(out_ref.dtype)
        l_hi = l_h.astype(jnp.bfloat16).astype(jnp.float32)
        merged = jnp.where(
            lane == h,
            peak[:, h : h + 1],
            jnp.where(
                lane == heads + h,
                l_hi,
                jnp.where(lane == 2 * heads + h, l_h - l_hi, merged),
            ),
        )
    out_ref[c, :, width:] = merged.astype(out_ref.dtype)


def y_exchange_kernel(heads, head_dim, groups, src_hbm, out_ref, parts, own_sem, send_sems, recv_sems):
    me = lax.axis_index("y")
    chunks = out_ref.shape[0]
    barrier = pltpu.get_barrier_semaphore()
    for k in range(1, groups):
        pl.semaphore_signal(
            barrier, inc=1, device_id={"y": lax.rem(me + k, groups)},
            device_id_type=pl.DeviceIdType.MESH,
        )
    pl.semaphore_wait(barrier, groups - 1)
    local = pltpu.make_async_copy(src_hbm.at[:, me], parts.at[0], own_sem)
    local.start()
    copies = []
    for k in range(1, groups):
        dest = lax.rem(me + k, groups)
        copy = pltpu.make_async_remote_copy(
            src_ref=src_hbm.at[:, dest],
            dst_ref=parts.at[k],
            send_sem=send_sems.at[k - 1],
            recv_sem=recv_sems.at[k - 1],
            device_id={"y": dest},
            device_id_type=pl.DeviceIdType.MESH,
        )
        copy.start()
        copies.append(copy)
    local.wait()
    for copy in copies:
        copy.wait()

    def get_part(j, c, cut):
        return parts[j, c, :, cut]

    def step(c, carry):
        merge_chunk(heads, head_dim, groups, get_part, out_ref, c)
        return carry

    lax.fori_loop(0, chunks, step, 0)


def y_exchange(by_y, heads, head_dim):
    chunks, groups, rows_per, lanes_all = by_y.shape
    kernel = functools.partial(y_exchange_kernel, heads, head_dim, groups)
    return pl.pallas_call(
        kernel,
        out_shape=jax.ShapeDtypeStruct((chunks, rows_per, lanes_all), by_y.dtype),
        in_specs=[pl.BlockSpec(memory_space=pl.ANY)],
        out_specs=pl.BlockSpec(memory_space=pltpu.VMEM),
        scratch_shapes=[
            pltpu.VMEM((groups, chunks, rows_per, lanes_all), by_y.dtype),
            pltpu.SemaphoreType.DMA(()),
            pltpu.SemaphoreType.DMA((groups - 1,)),
            pltpu.SemaphoreType.DMA((groups - 1,)),
        ],
        compiler_params=pltpu.CompilerParams(
            collective_id=2, has_side_effects=True, vmem_limit_bytes=32 * 1024 * 1024
        ),
        cost_estimate=pl.CostEstimate(
            flops=4 * by_y.size,
            transcendentals=chunks * groups * rows_per * 128,
            bytes_accessed=2 * by_y.size * 2,
        ),
    )(by_y)


def z_exchange_kernel(groups, src_hbm, out_ref, parts, own_sem, send_sems, recv_sems):
    me = lax.axis_index("z")
    barrier = pltpu.get_barrier_semaphore()
    for k in range(1, groups):
        pl.semaphore_signal(
            barrier, inc=1, device_id={"z": lax.rem(me + k, groups)},
            device_id_type=pl.DeviceIdType.MESH,
        )
    pl.semaphore_wait(barrier, groups - 1)
    local = pltpu.make_async_copy(src_hbm.at[me], parts.at[0], own_sem)
    local.start()
    copies = []
    for k in range(1, groups):
        dest = lax.rem(me + k, groups)
        copy = pltpu.make_async_remote_copy(
            src_ref=src_hbm.at[dest],
            dst_ref=parts.at[k],
            send_sem=send_sems.at[k - 1],
            recv_sem=recv_sems.at[k - 1],
            device_id={"z": dest},
            device_id_type=pl.DeviceIdType.MESH,
        )
        copy.start()
        copies.append(copy)
    local.wait()
    for copy in copies:
        copy.wait()
    out_ref[...] = parts[...]


def z_exchange(merged):
    groups, rows_per, lanes_all = merged.shape
    kernel = functools.partial(z_exchange_kernel, groups)
    return pl.pallas_call(
        kernel,
        out_shape=jax.ShapeDtypeStruct(merged.shape, merged.dtype),
        in_specs=[pl.BlockSpec(memory_space=pl.ANY)],
        out_specs=pl.BlockSpec(memory_space=pltpu.VMEM),
        scratch_shapes=[
            pltpu.VMEM(merged.shape, merged.dtype),
            pltpu.SemaphoreType.DMA(()),
            pltpu.SemaphoreType.DMA((groups - 1,)),
            pltpu.SemaphoreType.DMA((groups - 1,)),
        ],
        compiler_params=pltpu.CompilerParams(collective_id=3, has_side_effects=True),
        cost_estimate=pl.CostEstimate(
            flops=0, transcendentals=0, bytes_accessed=3 * merged.size * 2
        ),
    )(merged)

def per_device(
    queries,
    keys,
    values,
    key_cache,
    value_cache,
    cache_len,
    page_table,
    append_slots,
    out_weight,
    out_bias,
):
    tok_dev, head_count, head_dim = queries.shape
    width = head_count * head_dim
    requests = cache_len.shape[0]
    max_pages = page_table.shape[1]
    new_pages = append_slots.shape[1]
    span_len = new_pages * PAGE
    slot_count = key_cache.shape[0]
    page_devices = lax.axis_size(PAGES)
    device_at = lax.axis_index(PAGES)
    token_ids = device_at * tok_dev + jnp.arange(tok_dev, dtype=jnp.int32)
    request_ids = token_ids // span_len
    request_grid = jnp.arange(requests, dtype=jnp.int32)
    starts = jnp.sum(
        jnp.where(request_ids[:, None] == request_grid[None, :], cache_len[None, :], 0), axis=1
    )
    positions = (starts + token_ids % span_len).astype(jnp.float32)
    rotated_q = rotate(queries.astype(jnp.float32), positions).astype(jnp.bfloat16)
    rotated_k = rotate(keys.astype(jnp.float32), positions).astype(jnp.bfloat16)
    w_cols = out_weight.shape[1]
    w_plane = jnp.pad(out_weight.T, ((0, tok_dev - w_cols), (0, 0)))
    stacked = jnp.stack(
        [
            rotated_q.reshape(tok_dev, width),
            rotated_k.reshape(tok_dev, width),
            values.reshape(tok_dev, width),
        ]
    )
    w_all = lax.all_gather(w_plane[None], PAGES, axis=1, tiled=True)
    gathered = lax.all_gather(stacked, PAGES, axis=1, tiled=True)
    my_slots = device_at * slot_count + jnp.arange(slot_count, dtype=jnp.int32)
    cached_hit = page_table.reshape(-1)[None, :] == my_slots[:, None]
    fresh_hit = append_slots.reshape(-1)[None, :] == my_slots[:, None]
    is_cached = jnp.any(cached_hit, axis=1)
    is_fresh = jnp.any(fresh_hit, axis=1)
    cached_index = jnp.sum(
        jnp.where(cached_hit, jnp.arange(requests * max_pages, dtype=jnp.int32)[None, :], 0), axis=1
    )
    fresh_index = jnp.sum(
        jnp.where(fresh_hit, jnp.arange(requests * new_pages, dtype=jnp.int32)[None, :], 0), axis=1
    )
    slot_request = jnp.where(is_fresh, fresh_index // new_pages, cached_index // max_pages)
    slot_page = jnp.where(is_fresh, fresh_index % new_pages, cached_index % max_pages)
    slot_length = jnp.sum(
        jnp.where(slot_request[:, None] == request_grid[None, :], cache_len[None, :], 0), axis=1
    )
    visible = is_cached & (slot_page * PAGE < slot_length)
    slot_kind = jnp.where(is_fresh, 2, jnp.where(visible, 1, 0)).astype(jnp.int32)
    slot_limit = jnp.where(is_fresh, slot_page * PAGE, -4 * span_len)
    packed, key_slots, value_slots = local_attention(
        slot_request,
        slot_kind,
        slot_limit,
        fresh_index,
        gathered,
        key_cache.reshape(slot_count, PAGE, width),
        value_cache.reshape(slot_count, PAGE, width),
        head_count,
        head_dim,
        requests,
        span_len,
        page_devices,
    )
    paired = pair_merge(packed, head_count, head_dim)
    z_n = lax.axis_size("z")
    y_n = lax.axis_size("y")
    by_y = paired.reshape(z_n, y_n, tok_dev, paired.shape[-1])
    merged = y_exchange(by_y, head_count, head_dim)
    received = z_exchange(merged)
    projected = combine_project(received, w_all, head_count, head_dim)
    head_groups = lax.axis_size("heads")
    summed = heads_sum(projected, head_groups)
    summed = summed.reshape(tok_dev, page_devices // head_groups, tok_dev)[:, :, :w_cols].reshape(
        tok_dev, (page_devices // head_groups) * w_cols
    )
    key_out = key_slots.reshape(key_cache.shape)
    value_out = value_slots.reshape(value_cache.shape)
    hidden = (summed + out_bias[None, :]).astype(jnp.bfloat16)
    return (hidden, key_out, value_out)


def solution(mesh):
    heads_n, pages_n = mesh.devices.shape
    z_n = pages_n // 8
    split = jax.sharding.Mesh(
        mesh.devices.reshape(heads_n, z_n, 4, 2), ("heads", "z", "y", "core")
    )
    placed = (
        P(PAGES, "heads", None),
        P(PAGES, "heads", None),
        P(PAGES, "heads", None),
        P(PAGES, None, "heads", None),
        P(PAGES, None, "heads", None),
        P(),
        P(),
        P(),
        P("heads", PAGES),
        P("heads"),
    )
    return jax.shard_map(
        per_device,
        mesh=split,
        in_specs=placed,
        out_specs=(
            P(PAGES, "heads"),
            P(PAGES, None, "heads", None),
            P(PAGES, None, "heads", None),
        ),
        check_vma=False,
    )
```

```python
import functools
import math

import jax
import jax.numpy as jnp
from jax import lax
from jax.experimental import pallas as pl
from jax.experimental.pallas import tpu as pltpu
from jax.sharding import PartitionSpec as P

ROT = 32
PAGE = 128
PAGES = ("z", "y", "core")


low_score = -1e30
mask_score = -(2.0 ** 100)


def rotate(vectors, positions):
    half_rot = ROT // 2
    inv_freq = 10000.0 ** (-2.0 * jnp.arange(half_rot, dtype=jnp.float32) / ROT)
    angles = positions[:, None] * inv_freq[None, :]
    cosine = jnp.cos(angles)[:, None, :]
    sine = jnp.sin(angles)[:, None, :]
    first_half = vectors[..., :half_rot]
    second_half = vectors[..., half_rot:ROT]
    return jnp.concatenate(
        [
            first_half * cosine - second_half * sine,
            second_half * cosine + first_half * sine,
            vectors[..., ROT:],
        ],
        axis=-1,
    )


def attend_kernel(
    heads, head_dim, requests, span,
    sreq_ref, skind_ref, slim_ref, sfresh_ref,
    q_ref, kf_ref, vf_ref, kc_ref, vc_ref,
    out_ref, ko_ref, vo_ref, acc_t, stats, tok_ref, ml_ref,
):
    step = pl.program_id(0)
    lanes = ml_ref.shape[1]
    width = heads * head_dim

    @pl.when(step == 0)
    def _init():
        acc_t[...] = jnp.zeros_like(acc_t)
        row = lax.broadcasted_iota(jnp.int32, stats.shape, 1)
        stats[...] = jnp.where(row < heads, mask_score, 0.0).astype(jnp.float32)

    request = sreq_ref[step]
    kind = skind_ref[step]
    limit = slim_ref[step]
    scale = 1.0 / math.sqrt(head_dim)

    def attend(k_ref, v_ref, masked):
        base = pl.multiple_of(request * span, span)
        if masked:
            keys_at = lax.broadcasted_iota(jnp.int32, (PAGE, span), 0)
            queries_at = lax.broadcasted_iota(jnp.int32, (PAGE, span), 1)
            allowed = queries_at - keys_at >= limit
        v_t = v_ref[0].astype(jnp.float32).T.astype(jnp.bfloat16)
        for h in range(heads):
            cut = slice(h * head_dim, (h + 1) * head_dim)
            q_h = q_ref[0, pl.ds(base, span), cut]
            k_h = k_ref[0, :, cut]
            scores = lax.dot_general(
                k_h, q_h, (((1,), (1,)), ((), ())), preferred_element_type=jnp.float32
            ) * scale
            if masked:
                scores = jnp.where(allowed, scores, mask_score)
            m_prev = stats[request, h : h + 1, :]
            l_prev = stats[request, heads + h : heads + h + 1, :]
            m_new = jnp.maximum(m_prev, jnp.max(scores, axis=0, keepdims=True))
            m_new = m_new.astype(jnp.bfloat16).astype(jnp.float32)
            alpha = jnp.exp(m_prev - m_new)
            weights = jnp.exp(scores - m_new)
            if masked:
                weights = jnp.where(allowed, weights, 0.0)
            l_new = alpha * l_prev + jnp.sum(weights, axis=0, keepdims=True)
            contrib = jnp.dot(
                v_t[cut, :], weights.astype(jnp.bfloat16), preferred_element_type=jnp.float32
            )
            slot = request * heads + h
            acc_t[slot] = alpha * acc_t[slot] + contrib
            stats[request, h : h + 1, :] = m_new
            stats[request, heads + h : heads + h + 1, :] = l_new
            stats[request, 2 * heads + h : 2 * heads + h + 1, :] = l_new

    @pl.when(kind == 1)
    def _cached():
        attend(kc_ref, vc_ref, False)

    @pl.when(kind == 2)
    def _fresh():
        attend(kf_ref, vf_ref, True)

    @pl.when(kind == 2)
    def _store_fresh():
        ko_ref[...] = kf_ref[...]
        vo_ref[...] = vf_ref[...]

    @pl.when(kind != 2)
    def _store_cached():
        ko_ref[...] = kc_ref[...]
        vo_ref[...] = vc_ref[...]

    @pl.when(step == pl.num_programs(0) - 1)
    def _emit():
        stat_rows = stats.shape[1]
        for r in range(requests):
            rows = pl.ds(r * span, span)
            for h in range(heads):
                tok_ref[rows, h * head_dim : (h + 1) * head_dim] = acc_t[r * heads + h].T
            block = jnp.concatenate(
                [stats[r], jnp.zeros((lanes - stat_rows, span), jnp.float32)], axis=0
            )
            ml_ref[rows, :] = block.T
        chunks, rows_per, _ = out_ref.shape
        lane = lax.broadcasted_iota(jnp.int32, (rows_per, lanes), 1)
        for d in range(chunks):
            rows = pl.ds(d * rows_per, rows_per)
            out_ref[d, :, :width] = tok_ref[rows, :].astype(jnp.bfloat16)
            ml = ml_ref[rows, :]
            rounded = ml.astype(jnp.bfloat16).astype(jnp.float32)
            packed = jnp.where(
                lane < 2 * heads,
                rounded,
                jnp.where(lane < 3 * heads, ml - rounded, 0.0),
            )
            out_ref[d, :, width:] = packed.astype(jnp.bfloat16)


def local_attention(slot_request, slot_kind, slot_limit, slot_fresh, gathered, kc, vc,
                    heads, head_dim, requests, span, chunks):
    _, tokens, width = gathered.shape
    slot_count = kc.shape[0]
    rows_per = tokens // chunks
    kernel = functools.partial(attend_kernel, heads, head_dim, requests, span)
    flops = 4 * slot_count * span * PAGE * width
    return pl.pallas_call(
        kernel,
        out_shape=(
            jax.ShapeDtypeStruct((chunks, rows_per, width + 128), jnp.bfloat16),
            jax.ShapeDtypeStruct(kc.shape, kc.dtype),
            jax.ShapeDtypeStruct(vc.shape, vc.dtype),
        ),
        grid_spec=pltpu.PrefetchScalarGridSpec(
            num_scalar_prefetch=4,
            grid=(slot_count,),
            in_specs=[
                pl.BlockSpec((1, tokens, width), lambda s, *_: (0, 0, 0),
                             pipeline_mode=pl.Buffered(1)),
                pl.BlockSpec((1, PAGE, width), lambda s, rq, kd, lm, fr: (1, fr[s], 0)),
                pl.BlockSpec((1, PAGE, width), lambda s, rq, kd, lm, fr: (2, fr[s], 0)),
                pl.BlockSpec((1, PAGE, width), lambda s, *_: (s, 0, 0)),
                pl.BlockSpec((1, PAGE, width), lambda s, *_: (s, 0, 0)),
            ],
            out_specs=[
                pl.BlockSpec((chunks, rows_per, width + 128), lambda s, *_: (0, 0, 0)),
                pl.BlockSpec((1, PAGE, width), lambda s, *_: (s, 0, 0)),
                pl.BlockSpec((1, PAGE, width), lambda s, *_: (s, 0, 0)),
            ],
            scratch_shapes=[
                pltpu.VMEM((requests * heads, head_dim, span), jnp.float32),
                pltpu.VMEM((requests, 16, span), jnp.float32),
                pltpu.VMEM((tokens, width), jnp.float32),
                pltpu.VMEM((tokens, 128), jnp.float32),
            ],
        ),
        compiler_params=pltpu.CompilerParams(
            dimension_semantics=("arbitrary",), vmem_limit_bytes=62 * 1024 * 1024
        ),
        cost_estimate=pl.CostEstimate(
            flops=flops,
            transcendentals=slot_count * span * PAGE * heads,
            bytes_accessed=tokens * width * 2 + 4 * kc.size * 2 + tokens * (width + 128) * 2,
        ),
    )(slot_request, slot_kind, slot_limit, slot_fresh, gathered, gathered, gathered, kc, vc)


def combine_kernel(heads, head_dim, recv_ref, w_ref, out_ref, o_acc, l_acc):
    chunks, rows_per, _ = recv_ref.shape
    width = heads * head_dim
    lanes = 128

    def peak_step(d, peak):
        return jnp.maximum(peak, recv_ref[d, :, width:].astype(jnp.float32))

    peak = lax.fori_loop(
        0, chunks, peak_step, jnp.full((rows_per, lanes), mask_score, jnp.float32)
    )
    o_acc[...] = jnp.zeros_like(o_acc)
    l_acc[...] = jnp.zeros_like(l_acc)

    def sum_step(d, carry):
        mld = recv_ref[d, :, width:].astype(jnp.float32)
        factor = jnp.exp(mld - peak)
        for h in range(heads):
            f_h = factor[:, h : h + 1]
            l_h = mld[:, heads + h : heads + h + 1] + mld[:, 2 * heads + h : 2 * heads + h + 1]
            l_acc[:, h : h + 1] += f_h * l_h
            cut = slice(h * head_dim, (h + 1) * head_dim)
            o_acc[:, cut] += f_h * recv_ref[d, :, cut].astype(jnp.float32)
        return carry

    lax.fori_loop(0, chunks, sum_step, 0)
    parts = []
    for h in range(heads):
        cut = slice(h * head_dim, (h + 1) * head_dim)
        parts.append((o_acc[:, cut] / l_acc[:, h : h + 1]).astype(jnp.bfloat16))
    attended = jnp.concatenate(parts, axis=1)
    out_ref[...] = lax.dot_general(
        attended, w_ref[0], (((1,), (1,)), ((), ())), preferred_element_type=jnp.float32
    ).astype(out_ref.dtype)


def combine_project(received, gathered, heads, head_dim):
    chunks, rows_per, _ = received.shape
    _, tokens, width = gathered.shape
    kernel = functools.partial(combine_kernel, heads, head_dim)
    return pl.pallas_call(
        kernel,
        out_shape=jax.ShapeDtypeStruct((rows_per, tokens), jnp.bfloat16),
        grid=(1,),
        in_specs=[
            pl.BlockSpec(received.shape, lambda i: (0, 0, 0)),
            pl.BlockSpec((1, tokens, width), lambda i: (0, 0, 0)),
        ],
        out_specs=pl.BlockSpec((rows_per, tokens), lambda i: (0, 0)),
        scratch_shapes=[
            pltpu.VMEM((rows_per, width), jnp.float32),
            pltpu.VMEM((rows_per, 128), jnp.float32),
        ],
        compiler_params=pltpu.CompilerParams(vmem_limit_bytes=48 * 1024 * 1024),
        cost_estimate=pl.CostEstimate(
            flops=2 * rows_per * tokens * width + 4 * received.size,
            transcendentals=chunks * rows_per * 128,
            bytes_accessed=received.size * 2 + tokens * width * 2 + rows_per * tokens * 2,
        ),
    )(received, gathered)


def pair_merge_kernel(heads, head_dim, packed_hbm, out_ref, mine, theirs, local_sem, send_sem, recv_sem):
    core = lax.axis_index("core")
    partner = 1 - core
    width = heads * head_dim
    lanes = 128
    chunks, rows_per, _ = out_ref.shape

    barrier = pltpu.get_barrier_semaphore()
    pl.semaphore_signal(barrier, inc=1, device_id={"core": partner}, device_id_type=pl.DeviceIdType.MESH)
    pl.semaphore_wait(barrier, 1)

    pieces = 2
    size = chunks // pieces
    pending = []
    for p in range(pieces):
        rows = pl.ds(p * size, size)
        local = pltpu.make_async_copy(
            packed_hbm.at[rows, core], mine.at[rows], local_sem.at[p]
        )
        local.start()
        remote = pltpu.make_async_remote_copy(
            src_ref=packed_hbm.at[rows, partner],
            dst_ref=theirs.at[rows],
            send_sem=send_sem.at[p],
            recv_sem=recv_sem.at[p],
            device_id={"core": partner},
            device_id_type=pl.DeviceIdType.MESH,
        )
        remote.start()
        pending.append((local, remote))

    lane = lax.broadcasted_iota(jnp.int32, (rows_per, lanes), 1)

    def merge_step(c, carry):
        ml_a = mine[c, :, width:].astype(jnp.float32)
        ml_b = theirs[c, :, width:].astype(jnp.float32)
        peak = jnp.maximum(ml_a, ml_b)
        f_a = jnp.exp(ml_a - peak)
        f_b = jnp.exp(ml_b - peak)
        merged = jnp.zeros((rows_per, lanes), jnp.float32)
        for h in range(heads):
            cut = slice(h * head_dim, (h + 1) * head_dim)
            fa_h = f_a[:, h : h + 1]
            fb_h = f_b[:, h : h + 1]
            out_ref[c, :, cut] = (
                fa_h * mine[c, :, cut].astype(jnp.float32)
                + fb_h * theirs[c, :, cut].astype(jnp.float32)
            ).astype(out_ref.dtype)
            l_a = ml_a[:, heads + h : heads + h + 1] + ml_a[:, 2 * heads + h : 2 * heads + h + 1]
            l_b = ml_b[:, heads + h : heads + h + 1] + ml_b[:, 2 * heads + h : 2 * heads + h + 1]
            l_h = fa_h * l_a + fb_h * l_b
            l_hi = l_h.astype(jnp.bfloat16).astype(jnp.float32)
            merged = jnp.where(
                lane == h,
                peak[:, h : h + 1],
                jnp.where(
                    lane == heads + h,
                    l_hi,
                    jnp.where(lane == 2 * heads + h, l_h - l_hi, merged),
                ),
            )
        out_ref[c, :, width:] = merged.astype(out_ref.dtype)
        return carry

    for p in range(pieces):
        local, remote = pending[p]
        local.wait()
        remote.wait()
        lax.fori_loop(p * size, (p + 1) * size, merge_step, 0)


def pair_merge(packed, heads, head_dim):
    devices, rows_per, lanes_all = packed.shape
    chips = devices // 2
    view = packed.reshape(chips, 2, rows_per, lanes_all)
    kernel = functools.partial(pair_merge_kernel, heads, head_dim)
    return pl.pallas_call(
        kernel,
        out_shape=jax.ShapeDtypeStruct((chips, rows_per, lanes_all), packed.dtype),
        in_specs=[pl.BlockSpec(memory_space=pl.ANY)],
        out_specs=pl.BlockSpec(memory_space=pltpu.VMEM),
        scratch_shapes=[
            pltpu.VMEM((chips, rows_per, lanes_all), packed.dtype),
            pltpu.VMEM((chips, rows_per, lanes_all), packed.dtype),
            pltpu.SemaphoreType.DMA((2,)),
            pltpu.SemaphoreType.DMA((2,)),
            pltpu.SemaphoreType.DMA((2,)),
        ],
        compiler_params=pltpu.CompilerParams(
            collective_id=0, has_side_effects=True, vmem_limit_bytes=40 * 1024 * 1024
        ),
        cost_estimate=pl.CostEstimate(
            flops=6 * chips * rows_per * lanes_all,
            transcendentals=2 * chips * rows_per * 128,
            bytes_accessed=3 * chips * rows_per * lanes_all * 2,
        ),
    )(view)


def heads_sum_kernel(groups, block, proj_hbm, out_ref, own, received, own_sem, send_sems, recv_sems):
    group = lax.axis_index("heads")
    barrier = pltpu.get_barrier_semaphore()
    for k in range(1, groups):
        pl.semaphore_signal(
            barrier, inc=1, device_id={"heads": lax.rem(group + k, groups)},
            device_id_type=pl.DeviceIdType.MESH,
        )
    pl.semaphore_wait(barrier, groups - 1)
    local = pltpu.make_async_copy(
        proj_hbm.at[:, pl.ds(pl.multiple_of(group * block, 128), block)], own, own_sem
    )
    local.start()
    copies = []
    for k in range(1, groups):
        dest = lax.rem(group + k, groups)
        copy = pltpu.make_async_remote_copy(
            src_ref=proj_hbm.at[:, pl.ds(pl.multiple_of(dest * block, 128), block)],
            dst_ref=received.at[k - 1],
            send_sem=send_sems.at[k - 1],
            recv_sem=recv_sems.at[k - 1],
            device_id={"heads": dest},
            device_id_type=pl.DeviceIdType.MESH,
        )
        copy.start()
        copies.append(copy)
    local.wait()
    for copy in copies:
        copy.wait()
    total = own[...].astype(jnp.float32)
    for k in range(groups - 1):
        total = total + received[k].astype(jnp.float32)
    out_ref[...] = total


def heads_sum(projected, groups):
    rows, cols = projected.shape
    block = cols // groups
    kernel = functools.partial(heads_sum_kernel, groups, block)
    return pl.pallas_call(
        kernel,
        out_shape=jax.ShapeDtypeStruct((rows, block), jnp.float32),
        in_specs=[pl.BlockSpec(memory_space=pl.ANY)],
        out_specs=pl.BlockSpec(memory_space=pltpu.VMEM),
        scratch_shapes=[
            pltpu.VMEM((rows, block), projected.dtype),
            pltpu.VMEM((groups - 1, rows, block), projected.dtype),
            pltpu.SemaphoreType.DMA(()),
            pltpu.SemaphoreType.DMA((groups - 1,)),
            pltpu.SemaphoreType.DMA((groups - 1,)),
        ],
        compiler_params=pltpu.CompilerParams(collective_id=1, has_side_effects=True),
        cost_estimate=pl.CostEstimate(
            flops=groups * rows * block,
            transcendentals=0,
            bytes_accessed=groups * rows * block * 2 + rows * block * 4,
        ),
    )(projected)


def merge_chunk(heads, head_dim, parts, get_part, out_ref, c):
    rows_per = out_ref.shape[1]
    width = heads * head_dim
    lanes = 128
    lane = lax.broadcasted_iota(jnp.int32, (rows_per, lanes), 1)
    stats = [get_part(j, c, slice(width, width + lanes)).astype(jnp.float32) for j in range(parts)]
    peak = stats[0]
    for j in range(1, parts):
        peak = jnp.maximum(peak, stats[j])
    factors = [jnp.exp(st - peak) for st in stats]
    merged = jnp.zeros((rows_per, lanes), jnp.float32)
    for h in range(heads):
        cut = slice(h * head_dim, (h + 1) * head_dim)
        o_h = jnp.zeros((rows_per, head_dim), jnp.float32)
        l_h = jnp.zeros((rows_per, 1), jnp.float32)
        for j in range(parts):
            f_h = factors[j][:, h : h + 1]
            o_h = o_h + f_h * get_part(j, c, cut).astype(jnp.float32)
            l_j = (
                stats[j][:, heads + h : heads + h + 1]
                + stats[j][:, 2 * heads + h : 2 * heads + h + 1]
            )
            l_h = l_h + f_h * l_j
        out_ref[c, :, cut] = o_h.astype(out_ref.dtype)
        l_hi = l_h.astype(jnp.bfloat16).astype(jnp.float32)
        merged = jnp.where(
            lane == h,
            peak[:, h : h + 1],
            jnp.where(
                lane == heads + h,
                l_hi,
                jnp.where(lane == 2 * heads + h, l_h - l_hi, merged),
            ),
        )
    out_ref[c, :, width:] = merged.astype(out_ref.dtype)


def y_exchange_kernel(heads, head_dim, groups, src_hbm, out_ref, parts, own_sem, send_sems, recv_sems):
    me = lax.axis_index("y")
    chunks = out_ref.shape[0]
    barrier = pltpu.get_barrier_semaphore()
    for k in range(1, groups):
        pl.semaphore_signal(
            barrier, inc=1, device_id={"y": lax.rem(me + k, groups)},
            device_id_type=pl.DeviceIdType.MESH,
        )
    pl.semaphore_wait(barrier, groups - 1)
    pieces = 2
    size = chunks // pieces
    pending = []
    for p in range(pieces):
        rows = pl.ds(p * size, size)
        local = pltpu.make_async_copy(src_hbm.at[rows, me], parts.at[0, rows], own_sem.at[p])
        local.start()
        copies = [local]
        for k in range(1, groups):
            dest = lax.rem(me + k, groups)
            copy = pltpu.make_async_remote_copy(
                src_ref=src_hbm.at[rows, dest],
                dst_ref=parts.at[k, rows],
                send_sem=send_sems.at[p, k - 1],
                recv_sem=recv_sems.at[p, k - 1],
                device_id={"y": dest},
                device_id_type=pl.DeviceIdType.MESH,
            )
            copy.start()
            copies.append(copy)
        pending.append(copies)

    def get_part(j, c, cut):
        return parts[j, c, :, cut]

    def step(c, carry):
        merge_chunk(heads, head_dim, groups, get_part, out_ref, c)
        return carry

    for p in range(pieces):
        for copy in pending[p]:
            copy.wait()
        lax.fori_loop(p * size, (p + 1) * size, step, 0)


def y_exchange(by_y, heads, head_dim):
    chunks, groups, rows_per, lanes_all = by_y.shape
    kernel = functools.partial(y_exchange_kernel, heads, head_dim, groups)
    return pl.pallas_call(
        kernel,
        out_shape=jax.ShapeDtypeStruct((chunks, rows_per, lanes_all), by_y.dtype),
        in_specs=[pl.BlockSpec(memory_space=pl.ANY)],
        out_specs=pl.BlockSpec(memory_space=pltpu.VMEM),
        scratch_shapes=[
            pltpu.VMEM((groups, chunks, rows_per, lanes_all), by_y.dtype),
            pltpu.SemaphoreType.DMA((2,)),
            pltpu.SemaphoreType.DMA((2, groups - 1)),
            pltpu.SemaphoreType.DMA((2, groups - 1)),
        ],
        compiler_params=pltpu.CompilerParams(
            collective_id=2, has_side_effects=True, vmem_limit_bytes=32 * 1024 * 1024
        ),
        cost_estimate=pl.CostEstimate(
            flops=4 * by_y.size,
            transcendentals=chunks * groups * rows_per * 128,
            bytes_accessed=2 * by_y.size * 2,
        ),
    )(by_y)


def z_exchange_kernel(groups, src_hbm, out_ref, parts, own_sem, send_sems, recv_sems):
    me = lax.axis_index("z")
    barrier = pltpu.get_barrier_semaphore()
    for k in range(1, groups):
        pl.semaphore_signal(
            barrier, inc=1, device_id={"z": lax.rem(me + k, groups)},
            device_id_type=pl.DeviceIdType.MESH,
        )
    pl.semaphore_wait(barrier, groups - 1)
    local = pltpu.make_async_copy(src_hbm.at[me], parts.at[0], own_sem)
    local.start()
    copies = []
    for k in range(1, groups):
        dest = lax.rem(me + k, groups)
        copy = pltpu.make_async_remote_copy(
            src_ref=src_hbm.at[dest],
            dst_ref=parts.at[k],
            send_sem=send_sems.at[k - 1],
            recv_sem=recv_sems.at[k - 1],
            device_id={"z": dest},
            device_id_type=pl.DeviceIdType.MESH,
        )
        copy.start()
        copies.append(copy)
    local.wait()
    for copy in copies:
        copy.wait()
    out_ref[...] = parts[...]


def z_exchange(merged):
    groups, rows_per, lanes_all = merged.shape
    kernel = functools.partial(z_exchange_kernel, groups)
    return pl.pallas_call(
        kernel,
        out_shape=jax.ShapeDtypeStruct(merged.shape, merged.dtype),
        in_specs=[pl.BlockSpec(memory_space=pl.ANY)],
        out_specs=pl.BlockSpec(memory_space=pltpu.VMEM),
        scratch_shapes=[
            pltpu.VMEM(merged.shape, merged.dtype),
            pltpu.SemaphoreType.DMA(()),
            pltpu.SemaphoreType.DMA((groups - 1,)),
            pltpu.SemaphoreType.DMA((groups - 1,)),
        ],
        compiler_params=pltpu.CompilerParams(collective_id=3, has_side_effects=True),
        cost_estimate=pl.CostEstimate(
            flops=0, transcendentals=0, bytes_accessed=3 * merged.size * 2
        ),
    )(merged)

def per_device(
    queries,
    keys,
    values,
    key_cache,
    value_cache,
    cache_len,
    page_table,
    append_slots,
    out_weight,
    out_bias,
):
    tok_dev, head_count, head_dim = queries.shape
    width = head_count * head_dim
    requests = cache_len.shape[0]
    max_pages = page_table.shape[1]
    new_pages = append_slots.shape[1]
    span_len = new_pages * PAGE
    slot_count = key_cache.shape[0]
    page_devices = lax.axis_size(PAGES)
    device_at = lax.axis_index(PAGES)
    token_ids = device_at * tok_dev + jnp.arange(tok_dev, dtype=jnp.int32)
    request_ids = token_ids // span_len
    request_grid = jnp.arange(requests, dtype=jnp.int32)
    starts = jnp.sum(
        jnp.where(request_ids[:, None] == request_grid[None, :], cache_len[None, :], 0), axis=1
    )
    positions = (starts + token_ids % span_len).astype(jnp.float32)
    rotated_q = rotate(queries.astype(jnp.float32), positions).astype(jnp.bfloat16)
    rotated_k = rotate(keys.astype(jnp.float32), positions).astype(jnp.bfloat16)
    w_cols = out_weight.shape[1]
    w_plane = jnp.pad(out_weight.T, ((0, tok_dev - w_cols), (0, 0)))
    stacked = jnp.stack(
        [
            rotated_q.reshape(tok_dev, width),
            rotated_k.reshape(tok_dev, width),
            values.reshape(tok_dev, width),
        ]
    )
    w_all = lax.all_gather(w_plane[None], PAGES, axis=1, tiled=True)
    gathered = lax.all_gather(stacked, PAGES, axis=1, tiled=True)
    my_slots = device_at * slot_count + jnp.arange(slot_count, dtype=jnp.int32)
    cached_hit = page_table.reshape(-1)[None, :] == my_slots[:, None]
    fresh_hit = append_slots.reshape(-1)[None, :] == my_slots[:, None]
    is_cached = jnp.any(cached_hit, axis=1)
    is_fresh = jnp.any(fresh_hit, axis=1)
    cached_index = jnp.sum(
        jnp.where(cached_hit, jnp.arange(requests * max_pages, dtype=jnp.int32)[None, :], 0), axis=1
    )
    fresh_index = jnp.sum(
        jnp.where(fresh_hit, jnp.arange(requests * new_pages, dtype=jnp.int32)[None, :], 0), axis=1
    )
    slot_request = jnp.where(is_fresh, fresh_index // new_pages, cached_index // max_pages)
    slot_page = jnp.where(is_fresh, fresh_index % new_pages, cached_index % max_pages)
    slot_length = jnp.sum(
        jnp.where(slot_request[:, None] == request_grid[None, :], cache_len[None, :], 0), axis=1
    )
    visible = is_cached & (slot_page * PAGE < slot_length)
    slot_kind = jnp.where(is_fresh, 2, jnp.where(visible, 1, 0)).astype(jnp.int32)
    slot_limit = jnp.where(is_fresh, slot_page * PAGE, -4 * span_len)
    packed, key_slots, value_slots = local_attention(
        slot_request,
        slot_kind,
        slot_limit,
        fresh_index,
        gathered,
        key_cache.reshape(slot_count, PAGE, width),
        value_cache.reshape(slot_count, PAGE, width),
        head_count,
        head_dim,
        requests,
        span_len,
        page_devices,
    )
    paired = pair_merge(packed, head_count, head_dim)
    z_n = lax.axis_size("z")
    y_n = lax.axis_size("y")
    by_y = paired.reshape(z_n, y_n, tok_dev, paired.shape[-1])
    merged = y_exchange(by_y, head_count, head_dim)
    received = z_exchange(merged)
    projected = combine_project(received, w_all, head_count, head_dim)
    head_groups = lax.axis_size("heads")
    summed = heads_sum(projected, head_groups)
    summed = summed.reshape(tok_dev, page_devices // head_groups, tok_dev)[:, :, :w_cols].reshape(
        tok_dev, (page_devices // head_groups) * w_cols
    )
    key_out = key_slots.reshape(key_cache.shape)
    value_out = value_slots.reshape(value_cache.shape)
    hidden = (summed + out_bias[None, :]).astype(jnp.bfloat16)
    return (hidden, key_out, value_out)


def solution(mesh):
    heads_n, pages_n = mesh.devices.shape
    z_n = pages_n // 8
    split = jax.sharding.Mesh(
        mesh.devices.reshape(heads_n, z_n, 4, 2), ("heads", "z", "y", "core")
    )
    placed = (
        P(PAGES, "heads", None),
        P(PAGES, "heads", None),
        P(PAGES, "heads", None),
        P(PAGES, None, "heads", None),
        P(PAGES, None, "heads", None),
        P(),
        P(),
        P(),
        P("heads", PAGES),
        P("heads"),
    )
    return jax.shard_map(
        per_device,
        mesh=split,
        in_specs=placed,
        out_specs=(
            P(PAGES, "heads"),
            P(PAGES, None, "heads", None),
            P(PAGES, None, "heads", None),
        ),
        check_vma=False,
    )
```

```python
import functools
import math

import jax
import jax.numpy as jnp
from jax import lax
from jax.experimental import pallas as pl
from jax.experimental.pallas import tpu as pltpu
from jax.sharding import PartitionSpec as P

ROT = 32
PAGE = 128
PAGES = ("z", "y", "core")


low_score = -1e30
mask_score = -(2.0 ** 100)


def rotate(vectors, positions):
    half_rot = ROT // 2
    inv_freq = 10000.0 ** (-2.0 * jnp.arange(half_rot, dtype=jnp.float32) / ROT)
    angles = positions[:, None] * inv_freq[None, :]
    cosine = jnp.cos(angles)[:, None, :]
    sine = jnp.sin(angles)[:, None, :]
    first_half = vectors[..., :half_rot]
    second_half = vectors[..., half_rot:ROT]
    return jnp.concatenate(
        [
            first_half * cosine - second_half * sine,
            second_half * cosine + first_half * sine,
            vectors[..., ROT:],
        ],
        axis=-1,
    )


def attend_kernel(
    heads, head_dim, requests, span,
    sreq_ref, skind_ref, slim_ref, sfresh_ref,
    q_ref, kf_ref, vf_ref, kc_ref, vc_ref,
    out_ref, ko_ref, vo_ref, acc_t, stats, tok_ref, ml_ref,
):
    step = pl.program_id(0)
    lanes = ml_ref.shape[1]
    width = heads * head_dim

    @pl.when(step == 0)
    def _init():
        acc_t[...] = jnp.zeros_like(acc_t)
        row = lax.broadcasted_iota(jnp.int32, stats.shape, 1)
        stats[...] = jnp.where(row < heads, mask_score, 0.0).astype(jnp.float32)

    request = sreq_ref[step]
    kind = skind_ref[step]
    limit = slim_ref[step]
    scale = 1.0 / math.sqrt(head_dim)

    def attend(k_ref, v_ref, masked):
        base = pl.multiple_of(request * span, span)
        if masked:
            keys_at = lax.broadcasted_iota(jnp.int32, (PAGE, span), 0)
            queries_at = lax.broadcasted_iota(jnp.int32, (PAGE, span), 1)
            allowed = queries_at - keys_at >= limit
        v_t = v_ref[0].astype(jnp.float32).T.astype(jnp.bfloat16)
        for h in range(heads):
            cut = slice(h * head_dim, (h + 1) * head_dim)
            q_h = q_ref[0, pl.ds(base, span), cut]
            k_h = k_ref[0, :, cut]
            scores = lax.dot_general(
                k_h, q_h, (((1,), (1,)), ((), ())), preferred_element_type=jnp.float32
            ) * scale
            if masked:
                scores = jnp.where(allowed, scores, mask_score)
            m_prev = stats[request, h : h + 1, :]
            l_prev = stats[request, heads + h : heads + h + 1, :]
            m_new = jnp.maximum(m_prev, jnp.max(scores, axis=0, keepdims=True))
            m_new = m_new.astype(jnp.bfloat16).astype(jnp.float32)
            alpha = jnp.exp(m_prev - m_new)
            weights = jnp.exp(scores - m_new)
            if masked:
                weights = jnp.where(allowed, weights, 0.0)
            l_new = alpha * l_prev + jnp.sum(weights, axis=0, keepdims=True)
            contrib = jnp.dot(
                v_t[cut, :], weights.astype(jnp.bfloat16), preferred_element_type=jnp.float32
            )
            slot = request * heads + h
            acc_t[slot] = alpha * acc_t[slot] + contrib
            stats[request, h : h + 1, :] = m_new
            stats[request, heads + h : heads + h + 1, :] = l_new
            stats[request, 2 * heads + h : 2 * heads + h + 1, :] = l_new

    @pl.when(kind == 1)
    def _cached():
        attend(kc_ref, vc_ref, False)

    @pl.when(kind == 2)
    def _fresh():
        attend(kf_ref, vf_ref, True)

    @pl.when(kind == 2)
    def _store_fresh():
        ko_ref[...] = kf_ref[...]
        vo_ref[...] = vf_ref[...]

    @pl.when(kind != 2)
    def _store_cached():
        ko_ref[...] = kc_ref[...]
        vo_ref[...] = vc_ref[...]

    @pl.when(step == pl.num_programs(0) - 1)
    def _emit():
        stat_rows = stats.shape[1]
        for r in range(requests):
            rows = pl.ds(r * span, span)
            for h in range(heads):
                tok_ref[rows, h * head_dim : (h + 1) * head_dim] = acc_t[r * heads + h].T
            block = jnp.concatenate(
                [stats[r], jnp.zeros((lanes - stat_rows, span), jnp.float32)], axis=0
            )
            ml_ref[rows, :] = block.T
        chunks, rows_per, _ = out_ref.shape
        lane = lax.broadcasted_iota(jnp.int32, (rows_per, lanes), 1)
        for d in range(chunks):
            rows = pl.ds(d * rows_per, rows_per)
            out_ref[d, :, :width] = tok_ref[rows, :].astype(jnp.bfloat16)
            ml = ml_ref[rows, :]
            rounded = ml.astype(jnp.bfloat16).astype(jnp.float32)
            packed = jnp.where(
                lane < 2 * heads,
                rounded,
                jnp.where(lane < 3 * heads, ml - rounded, 0.0),
            )
            out_ref[d, :, width:] = packed.astype(jnp.bfloat16)


def local_attention(slot_request, slot_kind, slot_limit, slot_fresh, gathered, kc, vc,
                    heads, head_dim, requests, span, chunks):
    _, tokens, width = gathered.shape
    slot_count = kc.shape[0]
    rows_per = tokens // chunks
    kernel = functools.partial(attend_kernel, heads, head_dim, requests, span)
    flops = 4 * slot_count * span * PAGE * width
    return pl.pallas_call(
        kernel,
        out_shape=(
            jax.ShapeDtypeStruct((chunks, rows_per, width + 128), jnp.bfloat16),
            jax.ShapeDtypeStruct(kc.shape, kc.dtype),
            jax.ShapeDtypeStruct(vc.shape, vc.dtype),
        ),
        grid_spec=pltpu.PrefetchScalarGridSpec(
            num_scalar_prefetch=4,
            grid=(slot_count,),
            in_specs=[
                pl.BlockSpec((1, tokens, width), lambda s, *_: (0, 0, 0),
                             pipeline_mode=pl.Buffered(1)),
                pl.BlockSpec((1, PAGE, width), lambda s, rq, kd, lm, fr: (1, fr[s], 0)),
                pl.BlockSpec((1, PAGE, width), lambda s, rq, kd, lm, fr: (2, fr[s], 0)),
                pl.BlockSpec((1, PAGE, width), lambda s, *_: (s, 0, 0)),
                pl.BlockSpec((1, PAGE, width), lambda s, *_: (s, 0, 0)),
            ],
            out_specs=[
                pl.BlockSpec((chunks, rows_per, width + 128), lambda s, *_: (0, 0, 0)),
                pl.BlockSpec((1, PAGE, width), lambda s, *_: (s, 0, 0)),
                pl.BlockSpec((1, PAGE, width), lambda s, *_: (s, 0, 0)),
            ],
            scratch_shapes=[
                pltpu.VMEM((requests * heads, head_dim, span), jnp.float32),
                pltpu.VMEM((requests, 16, span), jnp.float32),
                pltpu.VMEM((tokens, width), jnp.float32),
                pltpu.VMEM((tokens, 128), jnp.float32),
            ],
        ),
        compiler_params=pltpu.CompilerParams(
            dimension_semantics=("arbitrary",), vmem_limit_bytes=62 * 1024 * 1024
        ),
        cost_estimate=pl.CostEstimate(
            flops=flops,
            transcendentals=slot_count * span * PAGE * heads,
            bytes_accessed=tokens * width * 2 + 4 * kc.size * 2 + tokens * (width + 128) * 2,
        ),
    )(slot_request, slot_kind, slot_limit, slot_fresh, gathered, gathered, gathered, kc, vc)


def combine_kernel(heads, head_dim, recv_ref, w_ref, out_ref, o_acc, l_acc):
    chunks, rows_per, _ = recv_ref.shape
    width = heads * head_dim
    lanes = 128

    def peak_step(d, peak):
        return jnp.maximum(peak, recv_ref[d, :, width:].astype(jnp.float32))

    peak = lax.fori_loop(
        0, chunks, peak_step, jnp.full((rows_per, lanes), mask_score, jnp.float32)
    )
    o_acc[...] = jnp.zeros_like(o_acc)
    l_acc[...] = jnp.zeros_like(l_acc)

    def sum_step(d, carry):
        mld = recv_ref[d, :, width:].astype(jnp.float32)
        factor = jnp.exp(mld - peak)
        for h in range(heads):
            f_h = factor[:, h : h + 1]
            l_h = mld[:, heads + h : heads + h + 1] + mld[:, 2 * heads + h : 2 * heads + h + 1]
            l_acc[:, h : h + 1] += f_h * l_h
            cut = slice(h * head_dim, (h + 1) * head_dim)
            o_acc[:, cut] += f_h * recv_ref[d, :, cut].astype(jnp.float32)
        return carry

    lax.fori_loop(0, chunks, sum_step, 0)
    parts = []
    for h in range(heads):
        cut = slice(h * head_dim, (h + 1) * head_dim)
        parts.append((o_acc[:, cut] / l_acc[:, h : h + 1]).astype(jnp.bfloat16))
    attended = jnp.concatenate(parts, axis=1)
    out_ref[...] = lax.dot_general(
        attended, w_ref[0], (((1,), (1,)), ((), ())), preferred_element_type=jnp.float32
    ).astype(out_ref.dtype)


def combine_project(received, gathered, heads, head_dim):
    chunks, rows_per, _ = received.shape
    _, tokens, width = gathered.shape
    kernel = functools.partial(combine_kernel, heads, head_dim)
    return pl.pallas_call(
        kernel,
        out_shape=jax.ShapeDtypeStruct((rows_per, tokens), jnp.bfloat16),
        grid=(1,),
        in_specs=[
            pl.BlockSpec(received.shape, lambda i: (0, 0, 0)),
            pl.BlockSpec((1, tokens, width), lambda i: (0, 0, 0)),
        ],
        out_specs=pl.BlockSpec((rows_per, tokens), lambda i: (0, 0)),
        scratch_shapes=[
            pltpu.VMEM((rows_per, width), jnp.float32),
            pltpu.VMEM((rows_per, 128), jnp.float32),
        ],
        compiler_params=pltpu.CompilerParams(vmem_limit_bytes=48 * 1024 * 1024),
        cost_estimate=pl.CostEstimate(
            flops=2 * rows_per * tokens * width + 4 * received.size,
            transcendentals=chunks * rows_per * 128,
            bytes_accessed=received.size * 2 + tokens * width * 2 + rows_per * tokens * 2,
        ),
    )(received, gathered)


def pair_merge_kernel(heads, head_dim, packed_hbm, out_ref, mine, theirs, local_sem, send_sem, recv_sem):
    core = lax.axis_index("core")
    partner = 1 - core
    width = heads * head_dim
    lanes = 128
    chunks, rows_per, _ = out_ref.shape

    barrier = pltpu.get_barrier_semaphore()
    pl.semaphore_signal(barrier, inc=1, device_id={"core": partner}, device_id_type=pl.DeviceIdType.MESH)
    pl.semaphore_wait(barrier, 1)

    pieces = 4
    size = chunks // pieces
    pending = []
    for p in range(pieces):
        rows = pl.ds(p * size, size)
        local = pltpu.make_async_copy(
            packed_hbm.at[rows, core], mine.at[rows], local_sem.at[p]
        )
        local.start()
        remote = pltpu.make_async_remote_copy(
            src_ref=packed_hbm.at[rows, partner],
            dst_ref=theirs.at[rows],
            send_sem=send_sem.at[p],
            recv_sem=recv_sem.at[p],
            device_id={"core": partner},
            device_id_type=pl.DeviceIdType.MESH,
        )
        remote.start()
        pending.append((local, remote))

    lane = lax.broadcasted_iota(jnp.int32, (rows_per, lanes), 1)

    def merge_step(c, carry):
        ml_a = mine[c, :, width:].astype(jnp.float32)
        ml_b = theirs[c, :, width:].astype(jnp.float32)
        peak = jnp.maximum(ml_a, ml_b)
        f_a = jnp.exp(ml_a - peak)
        f_b = jnp.exp(ml_b - peak)
        merged = jnp.zeros((rows_per, lanes), jnp.float32)
        for h in range(heads):
            cut = slice(h * head_dim, (h + 1) * head_dim)
            fa_h = f_a[:, h : h + 1]
            fb_h = f_b[:, h : h + 1]
            out_ref[c, :, cut] = (
                fa_h * mine[c, :, cut].astype(jnp.float32)
                + fb_h * theirs[c, :, cut].astype(jnp.float32)
            ).astype(out_ref.dtype)
            l_a = ml_a[:, heads + h : heads + h + 1] + ml_a[:, 2 * heads + h : 2 * heads + h + 1]
            l_b = ml_b[:, heads + h : heads + h + 1] + ml_b[:, 2 * heads + h : 2 * heads + h + 1]
            l_h = fa_h * l_a + fb_h * l_b
            l_hi = l_h.astype(jnp.bfloat16).astype(jnp.float32)
            merged = jnp.where(
                lane == h,
                peak[:, h : h + 1],
                jnp.where(
                    lane == heads + h,
                    l_hi,
                    jnp.where(lane == 2 * heads + h, l_h - l_hi, merged),
                ),
            )
        out_ref[c, :, width:] = merged.astype(out_ref.dtype)
        return carry

    for p in range(pieces):
        local, remote = pending[p]
        local.wait()
        remote.wait()
        lax.fori_loop(p * size, (p + 1) * size, merge_step, 0)


def pair_merge(packed, heads, head_dim):
    devices, rows_per, lanes_all = packed.shape
    chips = devices // 2
    view = packed.reshape(chips, 2, rows_per, lanes_all)
    kernel = functools.partial(pair_merge_kernel, heads, head_dim)
    return pl.pallas_call(
        kernel,
        out_shape=jax.ShapeDtypeStruct((chips, rows_per, lanes_all), packed.dtype),
        in_specs=[pl.BlockSpec(memory_space=pl.ANY)],
        out_specs=pl.BlockSpec(memory_space=pltpu.VMEM),
        scratch_shapes=[
            pltpu.VMEM((chips, rows_per, lanes_all), packed.dtype),
            pltpu.VMEM((chips, rows_per, lanes_all), packed.dtype),
            pltpu.SemaphoreType.DMA((4,)),
            pltpu.SemaphoreType.DMA((4,)),
            pltpu.SemaphoreType.DMA((4,)),
        ],
        compiler_params=pltpu.CompilerParams(
            collective_id=0, has_side_effects=True, vmem_limit_bytes=40 * 1024 * 1024
        ),
        cost_estimate=pl.CostEstimate(
            flops=6 * chips * rows_per * lanes_all,
            transcendentals=2 * chips * rows_per * 128,
            bytes_accessed=3 * chips * rows_per * lanes_all * 2,
        ),
    )(view)


def heads_sum_kernel(groups, block, proj_hbm, out_ref, own, received, own_sem, send_sems, recv_sems):
    group = lax.axis_index("heads")
    barrier = pltpu.get_barrier_semaphore()
    for k in range(1, groups):
        pl.semaphore_signal(
            barrier, inc=1, device_id={"heads": lax.rem(group + k, groups)},
            device_id_type=pl.DeviceIdType.MESH,
        )
    pl.semaphore_wait(barrier, groups - 1)
    local = pltpu.make_async_copy(
        proj_hbm.at[:, pl.ds(pl.multiple_of(group * block, 128), block)], own, own_sem
    )
    local.start()
    copies = []
    for k in range(1, groups):
        dest = lax.rem(group + k, groups)
        copy = pltpu.make_async_remote_copy(
            src_ref=proj_hbm.at[:, pl.ds(pl.multiple_of(dest * block, 128), block)],
            dst_ref=received.at[k - 1],
            send_sem=send_sems.at[k - 1],
            recv_sem=recv_sems.at[k - 1],
            device_id={"heads": dest},
            device_id_type=pl.DeviceIdType.MESH,
        )
        copy.start()
        copies.append(copy)
    local.wait()
    for copy in copies:
        copy.wait()
    total = own[...].astype(jnp.float32)
    for k in range(groups - 1):
        total = total + received[k].astype(jnp.float32)
    out_ref[...] = total


def heads_sum(projected, groups):
    rows, cols = projected.shape
    block = cols // groups
    kernel = functools.partial(heads_sum_kernel, groups, block)
    return pl.pallas_call(
        kernel,
        out_shape=jax.ShapeDtypeStruct((rows, block), jnp.float32),
        in_specs=[pl.BlockSpec(memory_space=pl.ANY)],
        out_specs=pl.BlockSpec(memory_space=pltpu.VMEM),
        scratch_shapes=[
            pltpu.VMEM((rows, block), projected.dtype),
            pltpu.VMEM((groups - 1, rows, block), projected.dtype),
            pltpu.SemaphoreType.DMA(()),
            pltpu.SemaphoreType.DMA((groups - 1,)),
            pltpu.SemaphoreType.DMA((groups - 1,)),
        ],
        compiler_params=pltpu.CompilerParams(collective_id=1, has_side_effects=True),
        cost_estimate=pl.CostEstimate(
            flops=groups * rows * block,
            transcendentals=0,
            bytes_accessed=groups * rows * block * 2 + rows * block * 4,
        ),
    )(projected)


def merge_chunk(heads, head_dim, parts, get_part, out_ref, c):
    rows_per = out_ref.shape[1]
    width = heads * head_dim
    lanes = 128
    lane = lax.broadcasted_iota(jnp.int32, (rows_per, lanes), 1)
    stats = [get_part(j, c, slice(width, width + lanes)).astype(jnp.float32) for j in range(parts)]
    peak = stats[0]
    for j in range(1, parts):
        peak = jnp.maximum(peak, stats[j])
    factors = [jnp.exp(st - peak) for st in stats]
    merged = jnp.zeros((rows_per, lanes), jnp.float32)
    for h in range(heads):
        cut = slice(h * head_dim, (h + 1) * head_dim)
        o_h = jnp.zeros((rows_per, head_dim), jnp.float32)
        l_h = jnp.zeros((rows_per, 1), jnp.float32)
        for j in range(parts):
            f_h = factors[j][:, h : h + 1]
            o_h = o_h + f_h * get_part(j, c, cut).astype(jnp.float32)
            l_j = (
                stats[j][:, heads + h : heads + h + 1]
                + stats[j][:, 2 * heads + h : 2 * heads + h + 1]
            )
            l_h = l_h + f_h * l_j
        out_ref[c, :, cut] = o_h.astype(out_ref.dtype)
        l_hi = l_h.astype(jnp.bfloat16).astype(jnp.float32)
        merged = jnp.where(
            lane == h,
            peak[:, h : h + 1],
            jnp.where(
                lane == heads + h,
                l_hi,
                jnp.where(lane == 2 * heads + h, l_h - l_hi, merged),
            ),
        )
    out_ref[c, :, width:] = merged.astype(out_ref.dtype)


def y_exchange_kernel(heads, head_dim, groups, src_hbm, out_ref, parts, own_sem, send_sems, recv_sems):
    me = lax.axis_index("y")
    chunks = out_ref.shape[0]
    barrier = pltpu.get_barrier_semaphore()
    for k in range(1, groups):
        pl.semaphore_signal(
            barrier, inc=1, device_id={"y": lax.rem(me + k, groups)},
            device_id_type=pl.DeviceIdType.MESH,
        )
    pl.semaphore_wait(barrier, groups - 1)
    pieces = 4
    size = chunks // pieces
    pending = []
    for p in range(pieces):
        rows = pl.ds(p * size, size)
        local = pltpu.make_async_copy(src_hbm.at[rows, me], parts.at[0, rows], own_sem.at[p])
        local.start()
        copies = [local]
        for k in range(1, groups):
            dest = lax.rem(me + k, groups)
            copy = pltpu.make_async_remote_copy(
                src_ref=src_hbm.at[rows, dest],
                dst_ref=parts.at[k, rows],
                send_sem=send_sems.at[p, k - 1],
                recv_sem=recv_sems.at[p, k - 1],
                device_id={"y": dest},
                device_id_type=pl.DeviceIdType.MESH,
            )
            copy.start()
            copies.append(copy)
        pending.append(copies)

    def get_part(j, c, cut):
        return parts[j, c, :, cut]

    def step(c, carry):
        merge_chunk(heads, head_dim, groups, get_part, out_ref, c)
        return carry

    for p in range(pieces):
        for copy in pending[p]:
            copy.wait()
        lax.fori_loop(p * size, (p + 1) * size, step, 0)


def y_exchange(by_y, heads, head_dim):
    chunks, groups, rows_per, lanes_all = by_y.shape
    kernel = functools.partial(y_exchange_kernel, heads, head_dim, groups)
    return pl.pallas_call(
        kernel,
        out_shape=jax.ShapeDtypeStruct((chunks, rows_per, lanes_all), by_y.dtype),
        in_specs=[pl.BlockSpec(memory_space=pl.ANY)],
        out_specs=pl.BlockSpec(memory_space=pltpu.VMEM),
        scratch_shapes=[
            pltpu.VMEM((groups, chunks, rows_per, lanes_all), by_y.dtype),
            pltpu.SemaphoreType.DMA((4,)),
            pltpu.SemaphoreType.DMA((4, groups - 1)),
            pltpu.SemaphoreType.DMA((4, groups - 1)),
        ],
        compiler_params=pltpu.CompilerParams(
            collective_id=2, has_side_effects=True, vmem_limit_bytes=32 * 1024 * 1024
        ),
        cost_estimate=pl.CostEstimate(
            flops=4 * by_y.size,
            transcendentals=chunks * groups * rows_per * 128,
            bytes_accessed=2 * by_y.size * 2,
        ),
    )(by_y)


def z_exchange_kernel(groups, src_hbm, out_ref, parts, own_sem, send_sems, recv_sems):
    me = lax.axis_index("z")
    barrier = pltpu.get_barrier_semaphore()
    for k in range(1, groups):
        pl.semaphore_signal(
            barrier, inc=1, device_id={"z": lax.rem(me + k, groups)},
            device_id_type=pl.DeviceIdType.MESH,
        )
    pl.semaphore_wait(barrier, groups - 1)
    local = pltpu.make_async_copy(src_hbm.at[me], parts.at[0], own_sem)
    local.start()
    copies = []
    for k in range(1, groups):
        dest = lax.rem(me + k, groups)
        copy = pltpu.make_async_remote_copy(
            src_ref=src_hbm.at[dest],
            dst_ref=parts.at[k],
            send_sem=send_sems.at[k - 1],
            recv_sem=recv_sems.at[k - 1],
            device_id={"z": dest},
            device_id_type=pl.DeviceIdType.MESH,
        )
        copy.start()
        copies.append(copy)
    local.wait()
    for copy in copies:
        copy.wait()
    out_ref[...] = parts[...]


def z_exchange(merged):
    groups, rows_per, lanes_all = merged.shape
    kernel = functools.partial(z_exchange_kernel, groups)
    return pl.pallas_call(
        kernel,
        out_shape=jax.ShapeDtypeStruct(merged.shape, merged.dtype),
        in_specs=[pl.BlockSpec(memory_space=pl.ANY)],
        out_specs=pl.BlockSpec(memory_space=pltpu.VMEM),
        scratch_shapes=[
            pltpu.VMEM(merged.shape, merged.dtype),
            pltpu.SemaphoreType.DMA(()),
            pltpu.SemaphoreType.DMA((groups - 1,)),
            pltpu.SemaphoreType.DMA((groups - 1,)),
        ],
        compiler_params=pltpu.CompilerParams(collective_id=3, has_side_effects=True),
        cost_estimate=pl.CostEstimate(
            flops=0, transcendentals=0, bytes_accessed=3 * merged.size * 2
        ),
    )(merged)

def per_device(
    queries,
    keys,
    values,
    key_cache,
    value_cache,
    cache_len,
    page_table,
    append_slots,
    out_weight,
    out_bias,
):
    tok_dev, head_count, head_dim = queries.shape
    width = head_count * head_dim
    requests = cache_len.shape[0]
    max_pages = page_table.shape[1]
    new_pages = append_slots.shape[1]
    span_len = new_pages * PAGE
    slot_count = key_cache.shape[0]
    page_devices = lax.axis_size(PAGES)
    device_at = lax.axis_index(PAGES)
    token_ids = device_at * tok_dev + jnp.arange(tok_dev, dtype=jnp.int32)
    request_ids = token_ids // span_len
    request_grid = jnp.arange(requests, dtype=jnp.int32)
    starts = jnp.sum(
        jnp.where(request_ids[:, None] == request_grid[None, :], cache_len[None, :], 0), axis=1
    )
    positions = (starts + token_ids % span_len).astype(jnp.float32)
    rotated_q = rotate(queries.astype(jnp.float32), positions).astype(jnp.bfloat16)
    rotated_k = rotate(keys.astype(jnp.float32), positions).astype(jnp.bfloat16)
    w_cols = out_weight.shape[1]
    w_plane = jnp.pad(out_weight.T, ((0, tok_dev - w_cols), (0, 0)))
    stacked = jnp.stack(
        [
            rotated_q.reshape(tok_dev, width),
            rotated_k.reshape(tok_dev, width),
            values.reshape(tok_dev, width),
        ]
    )
    w_all = lax.all_gather(w_plane[None], PAGES, axis=1, tiled=True)
    gathered = lax.all_gather(stacked, PAGES, axis=1, tiled=True)
    my_slots = device_at * slot_count + jnp.arange(slot_count, dtype=jnp.int32)
    cached_hit = page_table.reshape(-1)[None, :] == my_slots[:, None]
    fresh_hit = append_slots.reshape(-1)[None, :] == my_slots[:, None]
    is_cached = jnp.any(cached_hit, axis=1)
    is_fresh = jnp.any(fresh_hit, axis=1)
    cached_index = jnp.sum(
        jnp.where(cached_hit, jnp.arange(requests * max_pages, dtype=jnp.int32)[None, :], 0), axis=1
    )
    fresh_index = jnp.sum(
        jnp.where(fresh_hit, jnp.arange(requests * new_pages, dtype=jnp.int32)[None, :], 0), axis=1
    )
    slot_request = jnp.where(is_fresh, fresh_index // new_pages, cached_index // max_pages)
    slot_page = jnp.where(is_fresh, fresh_index % new_pages, cached_index % max_pages)
    slot_length = jnp.sum(
        jnp.where(slot_request[:, None] == request_grid[None, :], cache_len[None, :], 0), axis=1
    )
    visible = is_cached & (slot_page * PAGE < slot_length)
    slot_kind = jnp.where(is_fresh, 2, jnp.where(visible, 1, 0)).astype(jnp.int32)
    slot_limit = jnp.where(is_fresh, slot_page * PAGE, -4 * span_len)
    packed, key_slots, value_slots = local_attention(
        slot_request,
        slot_kind,
        slot_limit,
        fresh_index,
        gathered,
        key_cache.reshape(slot_count, PAGE, width),
        value_cache.reshape(slot_count, PAGE, width),
        head_count,
        head_dim,
        requests,
        span_len,
        page_devices,
    )
    paired = pair_merge(packed, head_count, head_dim)
    z_n = lax.axis_size("z")
    y_n = lax.axis_size("y")
    by_y = paired.reshape(z_n, y_n, tok_dev, paired.shape[-1])
    merged = y_exchange(by_y, head_count, head_dim)
    received = z_exchange(merged)
    projected = combine_project(received, w_all, head_count, head_dim)
    head_groups = lax.axis_size("heads")
    summed = heads_sum(projected, head_groups)
    summed = summed.reshape(tok_dev, page_devices // head_groups, tok_dev)[:, :, :w_cols].reshape(
        tok_dev, (page_devices // head_groups) * w_cols
    )
    key_out = key_slots.reshape(key_cache.shape)
    value_out = value_slots.reshape(value_cache.shape)
    hidden = (summed + out_bias[None, :]).astype(jnp.bfloat16)
    return (hidden, key_out, value_out)


def solution(mesh):
    heads_n, pages_n = mesh.devices.shape
    z_n = pages_n // 8
    split = jax.sharding.Mesh(
        mesh.devices.reshape(heads_n, z_n, 4, 2), ("heads", "z", "y", "core")
    )
    placed = (
        P(PAGES, "heads", None),
        P(PAGES, "heads", None),
        P(PAGES, "heads", None),
        P(PAGES, None, "heads", None),
        P(PAGES, None, "heads", None),
        P(),
        P(),
        P(),
        P("heads", PAGES),
        P("heads"),
    )
    return jax.shard_map(
        per_device,
        mesh=split,
        in_specs=placed,
        out_specs=(
            P(PAGES, "heads"),
            P(PAGES, None, "heads", None),
            P(PAGES, None, "heads", None),
        ),
        check_vma=False,
    )
```

```python
import functools
import math

import jax
import jax.numpy as jnp
from jax import lax
from jax.experimental import pallas as pl
from jax.experimental.pallas import tpu as pltpu
from jax.sharding import PartitionSpec as P

ROT = 32
PAGE = 128
PAGES = ("z", "y", "core")


low_score = -1e30
mask_score = -(2.0 ** 100)


def rotate(vectors, positions):
    half_rot = ROT // 2
    inv_freq = 10000.0 ** (-2.0 * jnp.arange(half_rot, dtype=jnp.float32) / ROT)
    angles = positions[:, None] * inv_freq[None, :]
    cosine = jnp.cos(angles)[:, None, :]
    sine = jnp.sin(angles)[:, None, :]
    first_half = vectors[..., :half_rot]
    second_half = vectors[..., half_rot:ROT]
    return jnp.concatenate(
        [
            first_half * cosine - second_half * sine,
            second_half * cosine + first_half * sine,
            vectors[..., ROT:],
        ],
        axis=-1,
    )


def attend_kernel(
    heads, head_dim, requests, span,
    sreq_ref, skind_ref, slim_ref, sfresh_ref,
    q_ref, kf_ref, vf_ref, kc_ref, vc_ref,
    out_ref, ko_ref, vo_ref, acc_t, stats, tok_ref, ml_ref,
):
    step = pl.program_id(0)
    lanes = ml_ref.shape[1]
    width = heads * head_dim

    @pl.when(step == 0)
    def _init():
        acc_t[...] = jnp.zeros_like(acc_t)
        row = lax.broadcasted_iota(jnp.int32, stats.shape, 1)
        stats[...] = jnp.where(row < heads, mask_score, 0.0).astype(jnp.float32)

    request = sreq_ref[step]
    kind = skind_ref[step]
    limit = slim_ref[step]
    scale = 1.0 / math.sqrt(head_dim)

    def attend(k_ref, v_ref, masked):
        base = pl.multiple_of(request * span, span)
        if masked:
            keys_at = lax.broadcasted_iota(jnp.int32, (PAGE, span), 0)
            queries_at = lax.broadcasted_iota(jnp.int32, (PAGE, span), 1)
            allowed = queries_at - keys_at >= limit
        v_t = v_ref[0].astype(jnp.float32).T.astype(jnp.bfloat16)
        for h in range(heads):
            cut = slice(h * head_dim, (h + 1) * head_dim)
            q_h = q_ref[0, pl.ds(base, span), cut]
            k_h = k_ref[0, :, cut]
            scores = lax.dot_general(
                k_h, q_h, (((1,), (1,)), ((), ())), preferred_element_type=jnp.float32
            ) * scale
            if masked:
                scores = jnp.where(allowed, scores, mask_score)
            m_prev = stats[request, h : h + 1, :]
            l_prev = stats[request, heads + h : heads + h + 1, :]
            m_new = jnp.maximum(m_prev, jnp.max(scores, axis=0, keepdims=True))
            m_new = m_new.astype(jnp.bfloat16).astype(jnp.float32)
            alpha = jnp.exp(m_prev - m_new)
            weights = jnp.exp(scores - m_new)
            if masked:
                weights = jnp.where(allowed, weights, 0.0)
            l_new = alpha * l_prev + jnp.sum(weights, axis=0, keepdims=True)
            contrib = jnp.dot(
                v_t[cut, :], weights.astype(jnp.bfloat16), preferred_element_type=jnp.float32
            )
            slot = request * heads + h
            acc_t[slot] = alpha * acc_t[slot] + contrib
            stats[request, h : h + 1, :] = m_new
            stats[request, heads + h : heads + h + 1, :] = l_new
            stats[request, 2 * heads + h : 2 * heads + h + 1, :] = l_new

    @pl.when(kind == 1)
    def _cached():
        attend(kc_ref, vc_ref, False)

    @pl.when(kind == 2)
    def _fresh():
        attend(kf_ref, vf_ref, True)

    @pl.when(kind == 2)
    def _store_fresh():
        ko_ref[...] = kf_ref[...]
        vo_ref[...] = vf_ref[...]

    @pl.when(kind != 2)
    def _store_cached():
        ko_ref[...] = kc_ref[...]
        vo_ref[...] = vc_ref[...]

    @pl.when(step == pl.num_programs(0) - 1)
    def _emit():
        stat_rows = stats.shape[1]
        for r in range(requests):
            rows = pl.ds(r * span, span)
            for h in range(heads):
                tok_ref[rows, h * head_dim : (h + 1) * head_dim] = acc_t[r * heads + h].T
            block = jnp.concatenate(
                [stats[r], jnp.zeros((lanes - stat_rows, span), jnp.float32)], axis=0
            )
            ml_ref[rows, :] = block.T
        chunks, rows_per, _ = out_ref.shape
        lane = lax.broadcasted_iota(jnp.int32, (rows_per, lanes), 1)
        for d in range(chunks):
            rows = pl.ds(d * rows_per, rows_per)
            out_ref[d, :, :width] = tok_ref[rows, :].astype(jnp.bfloat16)
            ml = ml_ref[rows, :]
            rounded = ml.astype(jnp.bfloat16).astype(jnp.float32)
            packed = jnp.where(
                lane < 2 * heads,
                rounded,
                jnp.where(lane < 3 * heads, ml - rounded, 0.0),
            )
            out_ref[d, :, width:] = packed.astype(jnp.bfloat16)


def local_attention(slot_request, slot_kind, slot_limit, slot_fresh, gathered, kc, vc,
                    heads, head_dim, requests, span, chunks):
    _, tokens, width = gathered.shape
    slot_count = kc.shape[0]
    rows_per = tokens // chunks
    kernel = functools.partial(attend_kernel, heads, head_dim, requests, span)
    flops = 4 * slot_count * span * PAGE * width
    return pl.pallas_call(
        kernel,
        out_shape=(
            jax.ShapeDtypeStruct((chunks, rows_per, width + 128), jnp.bfloat16),
            jax.ShapeDtypeStruct(kc.shape, kc.dtype),
            jax.ShapeDtypeStruct(vc.shape, vc.dtype),
        ),
        grid_spec=pltpu.PrefetchScalarGridSpec(
            num_scalar_prefetch=4,
            grid=(slot_count,),
            in_specs=[
                pl.BlockSpec((1, tokens, width), lambda s, *_: (0, 0, 0),
                             pipeline_mode=pl.Buffered(1)),
                pl.BlockSpec((1, PAGE, width), lambda s, rq, kd, lm, fr: (1, fr[s], 0)),
                pl.BlockSpec((1, PAGE, width), lambda s, rq, kd, lm, fr: (2, fr[s], 0)),
                pl.BlockSpec((1, PAGE, width), lambda s, *_: (s, 0, 0)),
                pl.BlockSpec((1, PAGE, width), lambda s, *_: (s, 0, 0)),
            ],
            out_specs=[
                pl.BlockSpec((chunks, rows_per, width + 128), lambda s, *_: (0, 0, 0)),
                pl.BlockSpec((1, PAGE, width), lambda s, *_: (s, 0, 0)),
                pl.BlockSpec((1, PAGE, width), lambda s, *_: (s, 0, 0)),
            ],
            scratch_shapes=[
                pltpu.VMEM((requests * heads, head_dim, span), jnp.float32),
                pltpu.VMEM((requests, 16, span), jnp.float32),
                pltpu.VMEM((tokens, width), jnp.float32),
                pltpu.VMEM((tokens, 128), jnp.float32),
            ],
        ),
        compiler_params=pltpu.CompilerParams(
            dimension_semantics=("arbitrary",), vmem_limit_bytes=62 * 1024 * 1024
        ),
        cost_estimate=pl.CostEstimate(
            flops=flops,
            transcendentals=slot_count * span * PAGE * heads,
            bytes_accessed=tokens * width * 2 + 4 * kc.size * 2 + tokens * (width + 128) * 2,
        ),
    )(slot_request, slot_kind, slot_limit, slot_fresh, gathered, gathered, gathered, kc, vc)


def combine_kernel(heads, head_dim, recv_ref, w_ref, out_ref, o_acc, l_acc):
    chunks, rows_per, _ = recv_ref.shape
    width = heads * head_dim
    lanes = 128

    def peak_step(d, peak):
        return jnp.maximum(peak, recv_ref[d, :, width:].astype(jnp.float32))

    peak = lax.fori_loop(
        0, chunks, peak_step, jnp.full((rows_per, lanes), mask_score, jnp.float32)
    )
    o_acc[...] = jnp.zeros_like(o_acc)
    l_acc[...] = jnp.zeros_like(l_acc)

    def sum_step(d, carry):
        mld = recv_ref[d, :, width:].astype(jnp.float32)
        factor = jnp.exp(mld - peak)
        for h in range(heads):
            f_h = factor[:, h : h + 1]
            l_h = mld[:, heads + h : heads + h + 1] + mld[:, 2 * heads + h : 2 * heads + h + 1]
            l_acc[:, h : h + 1] += f_h * l_h
            cut = slice(h * head_dim, (h + 1) * head_dim)
            o_acc[:, cut] += f_h * recv_ref[d, :, cut].astype(jnp.float32)
        return carry

    lax.fori_loop(0, chunks, sum_step, 0)
    parts = []
    for h in range(heads):
        cut = slice(h * head_dim, (h + 1) * head_dim)
        parts.append((o_acc[:, cut] / l_acc[:, h : h + 1]).astype(jnp.bfloat16))
    attended = jnp.concatenate(parts, axis=1)
    out_ref[...] = lax.dot_general(
        attended, w_ref[0], (((1,), (1,)), ((), ())), preferred_element_type=jnp.float32
    ).astype(out_ref.dtype)


def combine_project(received, gathered, heads, head_dim):
    chunks, rows_per, _ = received.shape
    _, tokens, width = gathered.shape
    kernel = functools.partial(combine_kernel, heads, head_dim)
    return pl.pallas_call(
        kernel,
        out_shape=jax.ShapeDtypeStruct((rows_per, tokens), jnp.bfloat16),
        grid=(1,),
        in_specs=[
            pl.BlockSpec(received.shape, lambda i: (0, 0, 0)),
            pl.BlockSpec((1, tokens, width), lambda i: (0, 0, 0)),
        ],
        out_specs=pl.BlockSpec((rows_per, tokens), lambda i: (0, 0)),
        scratch_shapes=[
            pltpu.VMEM((rows_per, width), jnp.float32),
            pltpu.VMEM((rows_per, 128), jnp.float32),
        ],
        compiler_params=pltpu.CompilerParams(vmem_limit_bytes=48 * 1024 * 1024),
        cost_estimate=pl.CostEstimate(
            flops=2 * rows_per * tokens * width + 4 * received.size,
            transcendentals=chunks * rows_per * 128,
            bytes_accessed=received.size * 2 + tokens * width * 2 + rows_per * tokens * 2,
        ),
    )(received, gathered)


def pair_merge_kernel(heads, head_dim, packed_hbm, out_ref, mine, theirs, local_sem, send_sem, recv_sem):
    core = lax.axis_index("core")
    partner = 1 - core
    width = heads * head_dim
    lanes = 128
    chunks, rows_per, _ = out_ref.shape

    barrier = pltpu.get_barrier_semaphore()
    pl.semaphore_signal(barrier, inc=1, device_id={"core": partner}, device_id_type=pl.DeviceIdType.MESH)
    pl.semaphore_wait(barrier, 1)

    pieces = 8
    size = chunks // pieces
    pending = []
    for p in range(pieces):
        rows = pl.ds(p * size, size)
        local = pltpu.make_async_copy(
            packed_hbm.at[rows, core], mine.at[rows], local_sem.at[p]
        )
        local.start()
        remote = pltpu.make_async_remote_copy(
            src_ref=packed_hbm.at[rows, partner],
            dst_ref=theirs.at[rows],
            send_sem=send_sem.at[p],
            recv_sem=recv_sem.at[p],
            device_id={"core": partner},
            device_id_type=pl.DeviceIdType.MESH,
        )
        remote.start()
        pending.append((local, remote))

    lane = lax.broadcasted_iota(jnp.int32, (rows_per, lanes), 1)

    def merge_step(c, carry):
        ml_a = mine[c, :, width:].astype(jnp.float32)
        ml_b = theirs[c, :, width:].astype(jnp.float32)
        peak = jnp.maximum(ml_a, ml_b)
        f_a = jnp.exp(ml_a - peak)
        f_b = jnp.exp(ml_b - peak)
        merged = jnp.zeros((rows_per, lanes), jnp.float32)
        for h in range(heads):
            cut = slice(h * head_dim, (h + 1) * head_dim)
            fa_h = f_a[:, h : h + 1]
            fb_h = f_b[:, h : h + 1]
            out_ref[c, :, cut] = (
                fa_h * mine[c, :, cut].astype(jnp.float32)
                + fb_h * theirs[c, :, cut].astype(jnp.float32)
            ).astype(out_ref.dtype)
            l_a = ml_a[:, heads + h : heads + h + 1] + ml_a[:, 2 * heads + h : 2 * heads + h + 1]
            l_b = ml_b[:, heads + h : heads + h + 1] + ml_b[:, 2 * heads + h : 2 * heads + h + 1]
            l_h = fa_h * l_a + fb_h * l_b
            l_hi = l_h.astype(jnp.bfloat16).astype(jnp.float32)
            merged = jnp.where(
                lane == h,
                peak[:, h : h + 1],
                jnp.where(
                    lane == heads + h,
                    l_hi,
                    jnp.where(lane == 2 * heads + h, l_h - l_hi, merged),
                ),
            )
        out_ref[c, :, width:] = merged.astype(out_ref.dtype)
        return carry

    for p in range(pieces):
        local, remote = pending[p]
        local.wait()
        remote.wait()
        lax.fori_loop(p * size, (p + 1) * size, merge_step, 0)


def pair_merge(packed, heads, head_dim):
    devices, rows_per, lanes_all = packed.shape
    chips = devices // 2
    view = packed.reshape(chips, 2, rows_per, lanes_all)
    kernel = functools.partial(pair_merge_kernel, heads, head_dim)
    return pl.pallas_call(
        kernel,
        out_shape=jax.ShapeDtypeStruct((chips, rows_per, lanes_all), packed.dtype),
        in_specs=[pl.BlockSpec(memory_space=pl.ANY)],
        out_specs=pl.BlockSpec(memory_space=pltpu.VMEM),
        scratch_shapes=[
            pltpu.VMEM((chips, rows_per, lanes_all), packed.dtype),
            pltpu.VMEM((chips, rows_per, lanes_all), packed.dtype),
            pltpu.SemaphoreType.DMA((8,)),
            pltpu.SemaphoreType.DMA((8,)),
            pltpu.SemaphoreType.DMA((8,)),
        ],
        compiler_params=pltpu.CompilerParams(
            collective_id=0, has_side_effects=True, vmem_limit_bytes=40 * 1024 * 1024
        ),
        cost_estimate=pl.CostEstimate(
            flops=6 * chips * rows_per * lanes_all,
            transcendentals=2 * chips * rows_per * 128,
            bytes_accessed=3 * chips * rows_per * lanes_all * 2,
        ),
    )(view)


def heads_sum_kernel(groups, block, proj_hbm, out_ref, own, received, own_sem, send_sems, recv_sems):
    group = lax.axis_index("heads")
    barrier = pltpu.get_barrier_semaphore()
    for k in range(1, groups):
        pl.semaphore_signal(
            barrier, inc=1, device_id={"heads": lax.rem(group + k, groups)},
            device_id_type=pl.DeviceIdType.MESH,
        )
    pl.semaphore_wait(barrier, groups - 1)
    local = pltpu.make_async_copy(
        proj_hbm.at[:, pl.ds(pl.multiple_of(group * block, 128), block)], own, own_sem
    )
    local.start()
    copies = []
    for k in range(1, groups):
        dest = lax.rem(group + k, groups)
        copy = pltpu.make_async_remote_copy(
            src_ref=proj_hbm.at[:, pl.ds(pl.multiple_of(dest * block, 128), block)],
            dst_ref=received.at[k - 1],
            send_sem=send_sems.at[k - 1],
            recv_sem=recv_sems.at[k - 1],
            device_id={"heads": dest},
            device_id_type=pl.DeviceIdType.MESH,
        )
        copy.start()
        copies.append(copy)
    local.wait()
    for copy in copies:
        copy.wait()
    total = own[...].astype(jnp.float32)
    for k in range(groups - 1):
        total = total + received[k].astype(jnp.float32)
    out_ref[...] = total


def heads_sum(projected, groups):
    rows, cols = projected.shape
    block = cols // groups
    kernel = functools.partial(heads_sum_kernel, groups, block)
    return pl.pallas_call(
        kernel,
        out_shape=jax.ShapeDtypeStruct((rows, block), jnp.float32),
        in_specs=[pl.BlockSpec(memory_space=pl.ANY)],
        out_specs=pl.BlockSpec(memory_space=pltpu.VMEM),
        scratch_shapes=[
            pltpu.VMEM((rows, block), projected.dtype),
            pltpu.VMEM((groups - 1, rows, block), projected.dtype),
            pltpu.SemaphoreType.DMA(()),
            pltpu.SemaphoreType.DMA((groups - 1,)),
            pltpu.SemaphoreType.DMA((groups - 1,)),
        ],
        compiler_params=pltpu.CompilerParams(collective_id=1, has_side_effects=True),
        cost_estimate=pl.CostEstimate(
            flops=groups * rows * block,
            transcendentals=0,
            bytes_accessed=groups * rows * block * 2 + rows * block * 4,
        ),
    )(projected)


def merge_chunk(heads, head_dim, parts, get_part, out_ref, c):
    rows_per = out_ref.shape[1]
    width = heads * head_dim
    lanes = 128
    lane = lax.broadcasted_iota(jnp.int32, (rows_per, lanes), 1)
    stats = [get_part(j, c, slice(width, width + lanes)).astype(jnp.float32) for j in range(parts)]
    peak = stats[0]
    for j in range(1, parts):
        peak = jnp.maximum(peak, stats[j])
    factors = [jnp.exp(st - peak) for st in stats]
    merged = jnp.zeros((rows_per, lanes), jnp.float32)
    for h in range(heads):
        cut = slice(h * head_dim, (h + 1) * head_dim)
        o_h = jnp.zeros((rows_per, head_dim), jnp.float32)
        l_h = jnp.zeros((rows_per, 1), jnp.float32)
        for j in range(parts):
            f_h = factors[j][:, h : h + 1]
            o_h = o_h + f_h * get_part(j, c, cut).astype(jnp.float32)
            l_j = (
                stats[j][:, heads + h : heads + h + 1]
                + stats[j][:, 2 * heads + h : 2 * heads + h + 1]
            )
            l_h = l_h + f_h * l_j
        out_ref[c, :, cut] = o_h.astype(out_ref.dtype)
        l_hi = l_h.astype(jnp.bfloat16).astype(jnp.float32)
        merged = jnp.where(
            lane == h,
            peak[:, h : h + 1],
            jnp.where(
                lane == heads + h,
                l_hi,
                jnp.where(lane == 2 * heads + h, l_h - l_hi, merged),
            ),
        )
    out_ref[c, :, width:] = merged.astype(out_ref.dtype)


def y_exchange_kernel(heads, head_dim, groups, src_hbm, out_ref, parts, own_sem, send_sems, recv_sems):
    me = lax.axis_index("y")
    chunks = out_ref.shape[0]
    barrier = pltpu.get_barrier_semaphore()
    for k in range(1, groups):
        pl.semaphore_signal(
            barrier, inc=1, device_id={"y": lax.rem(me + k, groups)},
            device_id_type=pl.DeviceIdType.MESH,
        )
    pl.semaphore_wait(barrier, groups - 1)
    pieces = 8
    size = chunks // pieces
    pending = []
    for p in range(pieces):
        rows = pl.ds(p * size, size)
        local = pltpu.make_async_copy(src_hbm.at[rows, me], parts.at[0, rows], own_sem.at[p])
        local.start()
        copies = [local]
        for k in range(1, groups):
            dest = lax.rem(me + k, groups)
            copy = pltpu.make_async_remote_copy(
                src_ref=src_hbm.at[rows, dest],
                dst_ref=parts.at[k, rows],
                send_sem=send_sems.at[p, k - 1],
                recv_sem=recv_sems.at[p, k - 1],
                device_id={"y": dest},
                device_id_type=pl.DeviceIdType.MESH,
            )
            copy.start()
            copies.append(copy)
        pending.append(copies)

    def get_part(j, c, cut):
        return parts[j, c, :, cut]

    def step(c, carry):
        merge_chunk(heads, head_dim, groups, get_part, out_ref, c)
        return carry

    for p in range(pieces):
        for copy in pending[p]:
            copy.wait()
        lax.fori_loop(p * size, (p + 1) * size, step, 0)


def y_exchange(by_y, heads, head_dim):
    chunks, groups, rows_per, lanes_all = by_y.shape
    kernel = functools.partial(y_exchange_kernel, heads, head_dim, groups)
    return pl.pallas_call(
        kernel,
        out_shape=jax.ShapeDtypeStruct((chunks, rows_per, lanes_all), by_y.dtype),
        in_specs=[pl.BlockSpec(memory_space=pl.ANY)],
        out_specs=pl.BlockSpec(memory_space=pltpu.VMEM),
        scratch_shapes=[
            pltpu.VMEM((groups, chunks, rows_per, lanes_all), by_y.dtype),
            pltpu.SemaphoreType.DMA((8,)),
            pltpu.SemaphoreType.DMA((8, groups - 1)),
            pltpu.SemaphoreType.DMA((8, groups - 1)),
        ],
        compiler_params=pltpu.CompilerParams(
            collective_id=2, has_side_effects=True, vmem_limit_bytes=32 * 1024 * 1024
        ),
        cost_estimate=pl.CostEstimate(
            flops=4 * by_y.size,
            transcendentals=chunks * groups * rows_per * 128,
            bytes_accessed=2 * by_y.size * 2,
        ),
    )(by_y)


def z_exchange_kernel(groups, src_hbm, out_ref, parts, own_sem, send_sems, recv_sems):
    me = lax.axis_index("z")
    barrier = pltpu.get_barrier_semaphore()
    for k in range(1, groups):
        pl.semaphore_signal(
            barrier, inc=1, device_id={"z": lax.rem(me + k, groups)},
            device_id_type=pl.DeviceIdType.MESH,
        )
    pl.semaphore_wait(barrier, groups - 1)
    local = pltpu.make_async_copy(src_hbm.at[me], parts.at[0], own_sem)
    local.start()
    copies = []
    for k in range(1, groups):
        dest = lax.rem(me + k, groups)
        copy = pltpu.make_async_remote_copy(
            src_ref=src_hbm.at[dest],
            dst_ref=parts.at[k],
            send_sem=send_sems.at[k - 1],
            recv_sem=recv_sems.at[k - 1],
            device_id={"z": dest},
            device_id_type=pl.DeviceIdType.MESH,
        )
        copy.start()
        copies.append(copy)
    local.wait()
    for copy in copies:
        copy.wait()
    out_ref[...] = parts[...]


def z_exchange(merged):
    groups, rows_per, lanes_all = merged.shape
    kernel = functools.partial(z_exchange_kernel, groups)
    return pl.pallas_call(
        kernel,
        out_shape=jax.ShapeDtypeStruct(merged.shape, merged.dtype),
        in_specs=[pl.BlockSpec(memory_space=pl.ANY)],
        out_specs=pl.BlockSpec(memory_space=pltpu.VMEM),
        scratch_shapes=[
            pltpu.VMEM(merged.shape, merged.dtype),
            pltpu.SemaphoreType.DMA(()),
            pltpu.SemaphoreType.DMA((groups - 1,)),
            pltpu.SemaphoreType.DMA((groups - 1,)),
        ],
        compiler_params=pltpu.CompilerParams(collective_id=3, has_side_effects=True),
        cost_estimate=pl.CostEstimate(
            flops=0, transcendentals=0, bytes_accessed=3 * merged.size * 2
        ),
    )(merged)

def per_device(
    queries,
    keys,
    values,
    key_cache,
    value_cache,
    cache_len,
    page_table,
    append_slots,
    out_weight,
    out_bias,
):
    tok_dev, head_count, head_dim = queries.shape
    width = head_count * head_dim
    requests = cache_len.shape[0]
    max_pages = page_table.shape[1]
    new_pages = append_slots.shape[1]
    span_len = new_pages * PAGE
    slot_count = key_cache.shape[0]
    page_devices = lax.axis_size(PAGES)
    device_at = lax.axis_index(PAGES)
    token_ids = device_at * tok_dev + jnp.arange(tok_dev, dtype=jnp.int32)
    request_ids = token_ids // span_len
    request_grid = jnp.arange(requests, dtype=jnp.int32)
    starts = jnp.sum(
        jnp.where(request_ids[:, None] == request_grid[None, :], cache_len[None, :], 0), axis=1
    )
    positions = (starts + token_ids % span_len).astype(jnp.float32)
    rotated_q = rotate(queries.astype(jnp.float32), positions).astype(jnp.bfloat16)
    rotated_k = rotate(keys.astype(jnp.float32), positions).astype(jnp.bfloat16)
    w_cols = out_weight.shape[1]
    w_plane = jnp.pad(out_weight.T, ((0, tok_dev - w_cols), (0, 0)))
    stacked = jnp.stack(
        [
            rotated_q.reshape(tok_dev, width),
            rotated_k.reshape(tok_dev, width),
            values.reshape(tok_dev, width),
        ]
    )
    w_all = lax.all_gather(w_plane[None], PAGES, axis=1, tiled=True)
    gathered = lax.all_gather(stacked, PAGES, axis=1, tiled=True)
    my_slots = device_at * slot_count + jnp.arange(slot_count, dtype=jnp.int32)
    cached_hit = page_table.reshape(-1)[None, :] == my_slots[:, None]
    fresh_hit = append_slots.reshape(-1)[None, :] == my_slots[:, None]
    is_cached = jnp.any(cached_hit, axis=1)
    is_fresh = jnp.any(fresh_hit, axis=1)
    cached_index = jnp.sum(
        jnp.where(cached_hit, jnp.arange(requests * max_pages, dtype=jnp.int32)[None, :], 0), axis=1
    )
    fresh_index = jnp.sum(
        jnp.where(fresh_hit, jnp.arange(requests * new_pages, dtype=jnp.int32)[None, :], 0), axis=1
    )
    slot_request = jnp.where(is_fresh, fresh_index // new_pages, cached_index // max_pages)
    slot_page = jnp.where(is_fresh, fresh_index % new_pages, cached_index % max_pages)
    slot_length = jnp.sum(
        jnp.where(slot_request[:, None] == request_grid[None, :], cache_len[None, :], 0), axis=1
    )
    visible = is_cached & (slot_page * PAGE < slot_length)
    slot_kind = jnp.where(is_fresh, 2, jnp.where(visible, 1, 0)).astype(jnp.int32)
    slot_limit = jnp.where(is_fresh, slot_page * PAGE, -4 * span_len)
    packed, key_slots, value_slots = local_attention(
        slot_request,
        slot_kind,
        slot_limit,
        fresh_index,
        gathered,
        key_cache.reshape(slot_count, PAGE, width),
        value_cache.reshape(slot_count, PAGE, width),
        head_count,
        head_dim,
        requests,
        span_len,
        page_devices,
    )
    paired = pair_merge(packed, head_count, head_dim)
    z_n = lax.axis_size("z")
    y_n = lax.axis_size("y")
    by_y = paired.reshape(z_n, y_n, tok_dev, paired.shape[-1])
    merged = y_exchange(by_y, head_count, head_dim)
    received = z_exchange(merged)
    projected = combine_project(received, w_all, head_count, head_dim)
    head_groups = lax.axis_size("heads")
    summed = heads_sum(projected, head_groups)
    summed = summed.reshape(tok_dev, page_devices // head_groups, tok_dev)[:, :, :w_cols].reshape(
        tok_dev, (page_devices // head_groups) * w_cols
    )
    key_out = key_slots.reshape(key_cache.shape)
    value_out = value_slots.reshape(value_cache.shape)
    hidden = (summed + out_bias[None, :]).astype(jnp.bfloat16)
    return (hidden, key_out, value_out)


def solution(mesh):
    heads_n, pages_n = mesh.devices.shape
    z_n = pages_n // 8
    split = jax.sharding.Mesh(
        mesh.devices.reshape(heads_n, z_n, 4, 2), ("heads", "z", "y", "core")
    )
    placed = (
        P(PAGES, "heads", None),
        P(PAGES, "heads", None),
        P(PAGES, "heads", None),
        P(PAGES, None, "heads", None),
        P(PAGES, None, "heads", None),
        P(),
        P(),
        P(),
        P("heads", PAGES),
        P("heads"),
    )
    return jax.shard_map(
        per_device,
        mesh=split,
        in_specs=placed,
        out_specs=(
            P(PAGES, "heads"),
            P(PAGES, None, "heads", None),
            P(PAGES, None, "heads", None),
        ),
        check_vma=False,
    )
```
